32 devices in a mesh: groups: 2 (over y), row: 8 (over z, x), col: 2 (over core).
Axes of the slice: x: 2, y: 2, z: 4, core: 2. Of those that a mesh axis runs over, the one named last changes fastest.
Arguments:
- teacher: bfloat16 [16384, 4096], P(('groups', 'row'), 'col'), parts along dimension 0, may hold values from -6 to 6
- proj_weight: bfloat16 [4096, 512], P('col'), may hold values from -0.09375 to 0.09375
- student: bfloat16 [512, 32, 512], P(('groups', 'col'), 'row'), parts along dimension 0, may hold values from -6 to 6
- dw_kernel: float32 [7, 7, 512], replicated, may hold values from -2 to 2
- dw_bias: float32 [512], replicated, may hold values from -4 to 4
- norm_gain: float32 [512], replicated, may hold values from 0.1 to 1.9
- norm_bias: float32 [512], replicated, may hold values from -4 to 4
- w_in: bfloat16 [512, 2048], replicated, may hold values from -0.25 to 0.25
- b_in: float32 [2048], replicated, may hold values from -4 to 4
- w_out: bfloat16 [2048, 512], replicated, may hold values from -0.125 to 0.125
- b_out: float32 [512], replicated, may hold values from -4 to 4
- layer_scale: float32 [512], replicated, may hold values from 0.25 to 1
Outputs:
- student_grad: float32 [512, 32, 512], P(('groups', 'col'), 'row'), parts along dimension 0
The draws below stay inside these ranges and needn't reach their ends.
There are 2 independent parts, one for each index of `groups`. The reference program is written for one: setup_inputs(seed, part) draws one part's arguments, and reference() takes and returns one part's arrays. A program takes and returns all parts, laid end to end along the dimension named above; an argument that names none is the same for every part. Nothing has to cross between parts.
All inputs are finite; a program needn't handle non-finite values.
Results may differ from the reference program's by a relative error of at most 0.0044.
Values may be sent and summed in bfloat16 or wider, within the bound.
No kernel may reach another device: no remote copies, remote signals or barrier semaphores. Data moves between devices by JAX's collectives and lax.ppermute only.
A program may use at most 64 MiB of HBM per device.

```python
import math
import jax
import jax.numpy as jnp
from jax import lax

TEACHER_DIM = 4096
CHANNELS = 512
HIDDEN_SIZE = 2048
GRID_U = 32
GRID_V = 256
TOKENS = 8192


def block_levels(rng, shape, cuts, least, high):
    factor_of, own = 1.0, jax.random.fold_in(rng, 6)
    for dim, blocks in cuts:
        heights = jnp.exp(jax.random.uniform(jax.random.fold_in(own, dim), (blocks,), jnp.float32, least / len(cuts), high / len(cuts)))
        factor_of = factor_of * jnp.repeat(heights, shape[dim] // blocks).reshape([-1 if axis == dim else 1 for axis in range(len(shape))])
    return factor_of


def normal_values(stream_key, shape, deviation, bound, cuts=(), dtype=jnp.bfloat16):
    loudness = block_levels(stream_key, shape, cuts, -0.22, 0.18) if cuts else 1.0
    values = jax.random.normal(stream_key, shape, jnp.float32) * deviation * loudness
    return jnp.minimum(jnp.maximum(values, -bound), bound).astype(dtype)


def setup_inputs(seed: int = 0, part: int = 0) -> dict:
    keys = jax.random.split(jax.random.key(seed), 13)
    own_keys = jax.random.split(jax.random.fold_in(keys[12], part), 13)
    return {
        "teacher": normal_values(own_keys[0], (TOKENS, TEACHER_DIM), 1.0, 6.0, ((0, 8), (1, 2))),
        "proj_weight": normal_values(keys[1], (TEACHER_DIM, CHANNELS), TEACHER_DIM ** -0.5, 0.09375, ((0, 2),)),
        "student": normal_values(own_keys[2], (GRID_V, GRID_U, CHANNELS), 1.0, 6.0, ((0, 2), (1, 8))),
        "dw_kernel": normal_values(keys[3], (7, 7, CHANNELS), 0.15, 2.0, (), jnp.float32),
        "dw_bias": normal_values(keys[4], (CHANNELS,), 0.5, 4.0, (), jnp.float32),
        "norm_gain": jnp.clip(1.0 + 0.18 * jax.random.normal(keys[5], (CHANNELS,), jnp.float32), 0.1, 1.9),
        "norm_bias": normal_values(keys[6], (CHANNELS,), 0.5, 4.0, (), jnp.float32),
        "w_in": normal_values(keys[7], (CHANNELS, HIDDEN_SIZE), CHANNELS ** -0.5, 0.25),
        "b_in": normal_values(keys[8], (HIDDEN_SIZE,), 0.5, 4.0, (), jnp.float32),
        "w_out": normal_values(keys[9], (HIDDEN_SIZE, CHANNELS), HIDDEN_SIZE ** -0.5, 0.125),
        "b_out": normal_values(keys[10], (CHANNELS,), 0.5, 4.0, (), jnp.float32),
        "layer_scale": jnp.clip(jnp.exp(jax.random.uniform(keys[11], (CHANNELS,), jnp.float32, math.log(0.25), math.log(1.0))), 0.25, 1.0),
    }


NORM_EPSILON = 1e-06

def depthwise(padded, kernel, out_rows, out_cols):
    summed = jnp.zeros((out_rows, out_cols, padded.shape[2]), jnp.float32)
    for row_tap in range(7):
        for col_tap in range(7):
            window = padded[row_tap:row_tap + out_rows, col_tap:col_tap + out_cols].astype(jnp.float32)
            summed = summed + kernel[row_tap, col_tap] * window
    return summed

def gelu_slope(values):
    return 0.5 * (1.0 + lax.erf(values * 0.7071067811865476)) + values * jnp.exp(-0.5 * values * values) * 0.3989422804014327

def reference(teacher, proj_weight, student, dw_kernel, dw_bias, norm_gain, norm_bias, w_in, b_in, w_out, b_out, layer_scale):
    target = jnp.dot(teacher, proj_weight, preferred_element_type=jnp.float32).astype(jnp.bfloat16)
    target = target.reshape(GRID_V, GRID_U, CHANNELS)
    padded = jnp.pad(student.astype(jnp.float32), ((3, 3), (3, 3), (0, 0)))
    conv_out = depthwise(padded, dw_kernel, GRID_V, GRID_U) + dw_bias
    mean_val = lax.optimization_barrier(jnp.mean(conv_out, axis=-1, keepdims=True))
    centred = conv_out - mean_val
    variance = lax.optimization_barrier(jnp.mean(centred * centred, axis=-1, keepdims=True))
    inv_scale = lax.rsqrt(variance + NORM_EPSILON)
    normal_form = centred * inv_scale
    normed = (normal_form * norm_gain + norm_bias).astype(jnp.bfloat16).reshape(-1, CHANNELS)
    hidden_pre = jnp.dot(normed, w_in, preferred_element_type=jnp.float32) + b_in
    activated = jax.nn.gelu(hidden_pre, approximate=False).astype(jnp.bfloat16)
    branch = jnp.dot(activated, w_out, preferred_element_type=jnp.float32) + b_out
    branch = branch.reshape(GRID_V, GRID_U, CHANNELS)
    mismatch = student.astype(jnp.float32) + layer_scale * branch - target.astype(jnp.float32)
    d_branch = (layer_scale * mismatch).astype(jnp.bfloat16).reshape(-1, CHANNELS)
    d_activated = jnp.dot(d_branch, w_out.T, preferred_element_type=jnp.float32)
    d_hidden = (d_activated * gelu_slope(hidden_pre)).astype(jnp.bfloat16)
    d_normed = jnp.dot(d_hidden, w_in.T, preferred_element_type=jnp.float32).reshape(GRID_V, GRID_U, CHANNELS)
    scaled = d_normed * norm_gain
    d_conv_out = inv_scale * (scaled - lax.optimization_barrier(jnp.mean(scaled, axis=-1, keepdims=True)) - normal_form * lax.optimization_barrier(jnp.mean(scaled * normal_form, axis=-1, keepdims=True)))
    d_padded = jnp.pad(d_conv_out, ((3, 3), (3, 3), (0, 0)))
    return mismatch + depthwise(d_padded, dw_kernel[::-1, ::-1], GRID_V, GRID_U)
```

```python
import functools

import jax
import jax.numpy as jnp
from jax import lax
from jax.experimental import pallas as pl
from jax.experimental.pallas import tpu as pltpu
from jax.sharding import PartitionSpec as P

NORM_EPSILON = 1e-06
REACH = 3
TAPS = 2 * REACH + 1
LANES = 128
SUBLANES = 8
MLP_TILE = 256


def fill_padded(padded, parts):
    place = 0
    for part in parts:
        for u in range(part.shape[0]):
            for tile in range(padded.shape[0]):
                padded[tile, place] = part[u, :, tile * LANES : (tile + 1) * LANES].astype(
                    jnp.float32
                )
            place += 1


def depthwise(padded, taps, store, tile_u, tile_v, flip):
    tiles = padded.shape[0]
    blocks = tile_v // (2 * SUBLANES)

    def step(index, carry):
        tile = index // blocks
        base = (index % blocks) * (2 * SUBLANES)
        sums = [[None] * tile_u for _ in range(2)]
        for row_tap in range(TAPS):
            weights = []
            for col_tap in range(TAPS):
                tap = row_tap * TAPS + col_tap
                weights.append(taps[TAPS * TAPS - 1 - tap if flip else tap, tile])
            for source in range(tile_u + TAPS - 1):
                for half in range(2):
                    values = padded[
                        tile, source, pl.ds(base + half * SUBLANES + row_tap, SUBLANES), :
                    ]
                    for u in range(max(0, source - TAPS + 1), min(tile_u, source + 1)):
                        term = weights[source - u] * values
                        sums[half][u] = term if sums[half][u] is None else sums[half][u] + term
        for half in range(2):
            for u in range(tile_u):
                store(tile, u, base + half * SUBLANES, sums[half][u])
        return carry

    lax.fori_loop(0, tiles * blocks, step, 0)


def block_kernel(
    left,
    middle,
    right,
    taps,
    dw_bias,
    norm_gain,
    norm_bias,
    w_in,
    b_in,
    w_out,
    b_out,
    layer_scale,
    target,
    mismatch_out,
    d_conv_out,
    padded,
    normal_form,
    inv_scale,
    normed,
    activated,
    slope,
    d_branch,
    d_hidden,
    d_normed,
):
    tile_u, tile_v, channels = target.shape
    rows = tile_u * tile_v
    hidden = w_in.shape[1]
    fill_padded(padded, (left, middle, right))

    def store_conv(tile, u, base, value):
        row = pl.multiple_of(u * tile_v + base, SUBLANES)
        lane = pl.multiple_of(tile * LANES, LANES)
        normal_form[pl.ds(row, SUBLANES), pl.ds(lane, LANES)] = value

    depthwise(padded, taps, store_conv, tile_u, tile_v, False)

    chunk = 32

    def norm_step(index, carry):
        here = pl.ds(pl.multiple_of(index * chunk, chunk), chunk)
        conv = normal_form[here, :] + dw_bias[...]
        centred = conv - jnp.mean(conv, axis=-1, keepdims=True)
        variance = jnp.mean(centred * centred, axis=-1, keepdims=True)
        inverse = lax.rsqrt(variance + NORM_EPSILON)
        form = centred * inverse
        normal_form[here, :] = form
        inv_scale[here, :] = jnp.broadcast_to(inverse, (chunk, LANES))
        normed[here, :] = (form * norm_gain[...] + norm_bias[...]).astype(jnp.bfloat16)
        return carry

    lax.fori_loop(0, rows // chunk, norm_step, 0)

    half_rows = rows // 2

    def up_step(index, carry):
        here = pl.ds(pl.multiple_of((index % 2) * half_rows, half_rows), half_rows)
        tile = pl.ds(pl.multiple_of((index // 2) * MLP_TILE, MLP_TILE), MLP_TILE)
        pre = (
            jnp.dot(normed[here, :], w_in[:, tile], preferred_element_type=jnp.float32)
            + b_in[:, tile]
        )
        phi = 0.5 * (1.0 + lax.erf(pre * 0.7071067811865476))
        activated[here, tile] = (pre * phi).astype(jnp.bfloat16)
        slope[here, tile] = phi + pre * jnp.exp(-0.5 * pre * pre) * 0.3989422804014327
        return carry

    lax.fori_loop(0, 2 * (hidden // MLP_TILE), up_step, 0)

    def down_step(u, carry):
        here = pl.ds(pl.multiple_of(u * tile_v, tile_v), tile_v)
        branch = (
            jnp.dot(activated[here, :], w_out[...], preferred_element_type=jnp.float32)
            + b_out[...]
        )
        mismatch = (
            middle[u, REACH : REACH + tile_v, :].astype(jnp.float32)
            + layer_scale[...] * branch
            - target[u].astype(jnp.float32)
        )
        mismatch_out[u] = mismatch
        d_branch[here, :] = (layer_scale[...] * mismatch).astype(jnp.bfloat16)
        return carry

    lax.fori_loop(0, tile_u, down_step, 0)

    contract_last = (((1,), (1,)), ((), ()))

    def back_step(index, carry):
        here = pl.ds(pl.multiple_of((index % 2) * half_rows, half_rows), half_rows)
        tile = pl.ds(pl.multiple_of((index // 2) * MLP_TILE, MLP_TILE), MLP_TILE)
        d_activated = lax.dot_general(
            d_branch[here, :], w_out[tile, :], contract_last, preferred_element_type=jnp.float32
        )
        d_hidden[here, tile] = (d_activated * slope[here, tile]).astype(jnp.bfloat16)
        return carry

    lax.fori_loop(0, 2 * (hidden // MLP_TILE), back_step, 0)

    def in_step(u, carry):
        here = pl.ds(pl.multiple_of(u * tile_v, tile_v), tile_v)
        d_normed[here, :] = lax.dot_general(
            d_hidden[here, :], w_in[...], contract_last, preferred_element_type=jnp.float32
        )
        return carry

    lax.fori_loop(0, tile_u, in_step, 0)

    def d_norm_step(index, carry):
        here = pl.ds(pl.multiple_of(index * chunk, chunk), chunk)
        scaled = d_normed[here, :] * norm_gain[...]
        form = normal_form[here, :]
        d_conv = inv_scale[here, :1] * (
            scaled
            - jnp.mean(scaled, axis=-1, keepdims=True)
            - form * jnp.mean(scaled * form, axis=-1, keepdims=True)
        )
        d_conv_out[index // (tile_v // chunk), pl.ds(pl.multiple_of(
            (index % (tile_v // chunk)) * chunk, chunk), chunk), :] = d_conv.astype(jnp.bfloat16)
        return carry

    lax.fori_loop(0, rows // chunk, d_norm_step, 0)


def final_kernel(left, middle, right, taps, mismatch, out, padded):
    tile_u, tile_v, channels = mismatch.shape
    fill_padded(padded, (left, middle, right))

    def store_out(tile, u, base, value):
        here = pl.ds(pl.multiple_of(base, SUBLANES), SUBLANES)
        lanes = pl.ds(pl.multiple_of(tile * LANES, LANES), LANES)
        out[u, here, lanes] = mismatch[u, here, lanes] + value

    depthwise(padded, taps, store_out, tile_u, tile_v, True)


def in_vmem(count):
    return [pl.BlockSpec(memory_space=pltpu.VMEM)] * count


def with_halo(tile, core):
    row_count = lax.axis_size("row")
    tile_u, tile_v, channels = tile.shape
    own_edge = jnp.where(core == 0, tile[:, tile_v - REACH :], tile[:, :REACH])
    other_edge = lax.ppermute(own_edge, "col", [(0, 1), (1, 0)])
    nothing = jnp.zeros_like(other_edge)
    fill = -(tile_v + 2 * REACH) % SUBLANES
    extended = jnp.concatenate(
        [
            jnp.where(core == 1, other_edge, nothing),
            tile,
            jnp.where(core == 0, other_edge, nothing),
            jnp.zeros((tile_u, fill, channels), tile.dtype),
        ],
        axis=1,
    )
    forward = [(i, i + 1) for i in range(row_count - 1)]
    backward = [(b, a) for a, b in forward]
    left = lax.ppermute(extended[tile_u - REACH :], "row", forward)
    right = lax.ppermute(extended[:REACH], "row", backward)
    return left, extended, right


def find_target(teacher, proj_weight, core, tile_u):
    row_count = lax.axis_size("row")
    channels = proj_weight.shape[1]
    grid_u = tile_u * row_count
    lines = teacher.shape[0] // (2 * grid_u)
    tokens = lines * grid_u
    away = lax.dynamic_slice_in_dim(teacher, (1 - core) * tokens, tokens)
    sent = jnp.dot(away, proj_weight, preferred_element_type=jnp.float32)
    received = lax.ppermute(sent, "col", [(0, 1), (1, 0)])
    home = lax.dynamic_slice_in_dim(teacher, core * tokens, tokens)
    kept = jnp.dot(home, proj_weight, preferred_element_type=jnp.float32)
    summed = (kept + received).astype(jnp.bfloat16)
    by_u = summed.reshape(lines, row_count, tile_u, channels).transpose(1, 2, 0, 3)
    arrived = lax.all_to_all(by_u, "row", split_axis=0, concat_axis=0, tiled=True)
    halves = row_count // 2
    for_other = lax.dynamic_slice_in_dim(arrived, (1 - core) * halves, halves)
    mine = lax.dynamic_slice_in_dim(arrived, core * halves, halves)
    from_other = lax.ppermute(for_other, "col", [(0, 1), (1, 0)])
    first = jnp.where(core == 0, mine, from_other)
    second = jnp.where(core == 0, from_other, mine)
    both = jnp.stack([first, second], axis=1)
    return both.transpose(2, 0, 1, 3, 4).reshape(tile_u, halves * 2 * lines, channels)


def on_device(
    teacher,
    proj_weight,
    student,
    dw_kernel,
    dw_bias,
    norm_gain,
    norm_bias,
    w_in,
    b_in,
    w_out,
    b_out,
    layer_scale,
):
    core = lax.axis_index("col")
    tile_v, tile_u, channels = student.shape
    hidden = w_in.shape[1]
    rows = tile_u * tile_v
    tiles = channels // LANES
    halo = with_halo(student.transpose(1, 0, 2), core)
    target = find_target(teacher, proj_weight, core, tile_u)
    taps = jnp.broadcast_to(
        dw_kernel.reshape(TAPS * TAPS, tiles, 1, LANES), (TAPS * TAPS, tiles, SUBLANES, LANES)
    )
    padded = pltpu.VMEM((tiles, tile_u + 2 * REACH, halo[1].shape[1], LANES), jnp.float32)
    tile_shape = (tile_u, tile_v, channels)
    mismatch, d_conv = pl.pallas_call(
        block_kernel,
        out_shape=(
            jax.ShapeDtypeStruct(tile_shape, jnp.float32),
            jax.ShapeDtypeStruct(tile_shape, jnp.bfloat16),
        ),
        in_specs=in_vmem(13),
        out_specs=tuple(in_vmem(2)),
        scratch_shapes=[
            padded,
            pltpu.VMEM((rows, channels), jnp.float32),
            pltpu.VMEM((rows, LANES), jnp.float32),
            pltpu.VMEM((rows, channels), jnp.bfloat16),
            pltpu.VMEM((rows, hidden), jnp.bfloat16),
            pltpu.VMEM((rows, hidden), jnp.float32),
            pltpu.VMEM((rows, channels), jnp.bfloat16),
            pltpu.VMEM((rows, hidden), jnp.bfloat16),
            pltpu.VMEM((rows, channels), jnp.float32),
        ],
        compiler_params=pltpu.CompilerParams(vmem_limit_bytes=40 << 20),
        name="block",
    )(
        *halo,
        taps,
        dw_bias[None],
        norm_gain[None],
        norm_bias[None],
        w_in,
        b_in[None],
        w_out,
        b_out[None],
        layer_scale[None],
        target,
    )
    d_halo = with_halo(d_conv, core)
    grad = pl.pallas_call(
        final_kernel,
        out_shape=jax.ShapeDtypeStruct(tile_shape, jnp.float32),
        in_specs=in_vmem(5),
        out_specs=in_vmem(1)[0],
        scratch_shapes=[padded],
        compiler_params=pltpu.CompilerParams(vmem_limit_bytes=24 << 20),
        name="final",
    )(*d_halo, taps, mismatch)
    return grad.transpose(1, 0, 2)


def solution(mesh):
    placed = (
        P(("groups", "row"), "col"),
        P("col", None),
        P(("groups", "col"), "row", None),
        P(),
        P(),
        P(),
        P(),
        P(),
        P(),
        P(),
        P(),
        P(),
    )
    return jax.shard_map(
        on_device,
        mesh=mesh,
        in_specs=placed,
        out_specs=P(("groups", "col"), "row", None),
        check_vma=False,
    )
```

```python
import functools

import jax
import jax.numpy as jnp
from jax import lax
from jax.experimental import pallas as pl
from jax.experimental.pallas import tpu as pltpu
from jax.sharding import PartitionSpec as P

NORM_EPSILON = 1e-06
REACH = 3
TAPS = 2 * REACH + 1
LANES = 128
SUBLANES = 8
EDGE = 8
CHUNK = 32
MLP_TILE = 512
CONTRACT_LAST = (((1,), (1,)), ((), ()))
SWAP = [(0, 1), (1, 0)]


def aligned(start, size):
    return pl.ds(pl.multiple_of(start, size), size)


def spread(padded, place, part, source, row, count):
    for tile in range(padded.shape[0]):
        padded[tile, place, pl.ds(row, count), :] = part[
            source, :count, tile * LANES : (tile + 1) * LANES
        ].astype(jnp.float32)


def spread_edge(padded, place, part, source, start, core, tile_v):
    for tile in range(padded.shape[0]):
        lanes = slice(tile * LANES, (tile + 1) * LANES)
        edge = part[source, start : start + EDGE, lanes].astype(jnp.float32)
        nothing = jnp.zeros_like(edge)
        padded[tile, place, 0:EDGE, :] = jnp.where(core == 1, edge, nothing)
        padded[tile, place, EDGE + tile_v : 2 * EDGE + tile_v, :] = jnp.where(
            core == 0, edge, nothing
        )


def depthwise(padded, taps, begin, store, tile_u, tile_v, sources, flip):
    tiles = padded.shape[0]
    blocks = tile_v // (2 * SUBLANES)

    def step(index, carry):
        tile = index // blocks
        base = pl.multiple_of((index % blocks) * (2 * SUBLANES), 2 * SUBLANES)
        sums = [
            [begin(tile, u, base + half * SUBLANES) for u in range(tile_u)] for half in range(2)
        ]
        for row_tap in range(TAPS):
            weights = []
            for col_tap in range(TAPS):
                tap = row_tap * TAPS + col_tap
                weights.append(taps[TAPS * TAPS - 1 - tap if flip else tap, tile])
            for place, source in enumerate(sources):
                for half in range(2):
                    row = base + (half * SUBLANES + EDGE - REACH + row_tap)
                    values = padded[tile, place, pl.ds(row, SUBLANES), :]
                    for u in range(max(0, source - TAPS + 1), min(tile_u, source + 1)):
                        term = weights[source - u] * values
                        sums[half][u] = term if sums[half][u] is None else sums[half][u] + term
        for half in range(2):
            for u in range(tile_u):
                if sums[half][u] is not None:
                    store(tile, u, base + half * SUBLANES, sums[half][u])
        return carry

    lax.fori_loop(0, tiles * blocks, step, 0)


def project_kernel(core_ref, teacher, weight, upper, lower, home):
    core = core_ref[0]
    lines, _, wide, depth = teacher.shape
    for half, outs in ((1 - core, (upper, lower)), (core, (home,))):
        rows = teacher[:, half].reshape(lines * wide, depth)
        size = lines * wide // len(outs)
        for index, out in enumerate(outs):
            here = rows[index * size : (index + 1) * size]
            product = jnp.dot(here, weight[...], preferred_element_type=jnp.float32)
            out[...] = product.astype(out.dtype)


def combine_kernel(wide, turns_ref, home, upper, lower, *rest):
    *blocks, summed = rest
    for tile in range(summed.shape[0]):
        lanes = slice(tile * LANES, (tile + 1) * LANES)
        half = upper.shape[0]
        for start, received in ((0, upper), (half, lower)):
            here = slice(start, start + half)
            summed[tile, here] = home[here, lanes] + received[:, lanes].astype(jnp.float32)
    for index, block in enumerate(blocks):
        tile_u, lines, _ = block.shape
        for u in range(tile_u):
            rows = pl.ds(turns_ref[index] + u, lines, stride=wide)
            for tile in range(summed.shape[0]):
                lanes = slice(tile * LANES, (tile + 1) * LANES)
                block[u, :, lanes] = summed[tile, rows, :].astype(jnp.bfloat16)


def fill(padded, parts, edges, core, tile_v):
    place = 0
    for part, (edge, start) in zip(parts, edges):
        for u in range(part.shape[0]):
            spread(padded, place, part, u, EDGE, tile_v)
            spread_edge(padded, place, edge, u, start, core, tile_v)
            place += 1


def up_kernel(
    core_ref,
    left,
    middle,
    right,
    edge,
    taps,
    dw_bias,
    norm_gain,
    norm_bias,
    w_in,
    b_in,
    normal_form,
    inv_scale,
    activated,
    slope,
    padded,
    normed,
):
    tile_u, tile_v, channels = middle.shape
    rows = tile_u * tile_v
    hidden = w_in.shape[1]
    sides = [(left, tile_v), (edge, 0), (right, tile_v)]
    fill(padded, (left, middle, right), sides, core_ref[0], tile_v)

    def begin(tile, u, base):
        return None

    def store(tile, u, base, value):
        row = aligned(u * tile_v + base, SUBLANES)
        normal_form[row, aligned(tile * LANES, LANES)] = value

    depthwise(padded, taps, begin, store, tile_u, tile_v, range(tile_u + 2 * REACH), False)

    def norm_step(index, carry):
        here = aligned(index * CHUNK, CHUNK)
        conv = normal_form[here, :] + dw_bias[...]
        centred = conv - jnp.mean(conv, axis=-1, keepdims=True)
        variance = jnp.mean(centred * centred, axis=-1, keepdims=True)
        inverse = lax.rsqrt(variance + NORM_EPSILON)
        form = centred * inverse
        normal_form[here, :] = form
        inv_scale[here, :] = jnp.broadcast_to(inverse, (CHUNK, LANES))
        normed[here, :] = (form * norm_gain[...] + norm_bias[...]).astype(jnp.bfloat16)
        return carry

    lax.fori_loop(0, rows // CHUNK, norm_step, 0)

    for start in range(0, hidden, MLP_TILE):
        tile = slice(start, start + MLP_TILE)
        for here in row_halves(rows):
            pre = (
                jnp.dot(normed[here, :], w_in[:, tile], preferred_element_type=jnp.float32)
                + b_in[:, tile]
            )
            phi = 0.5 * (1.0 + lax.erf(pre * 0.7071067811865476))
            activated[here, tile] = (pre * phi).astype(jnp.bfloat16)
            slope[here, tile] = phi + pre * jnp.exp(-0.5 * pre * pre) * 0.3989422804014327


def row_halves(rows):
    return slice(0, rows // 2), slice(rows // 2, rows)


def back_kernel(
    pieces,
    places_ref,
    middle,
    normal_form,
    inv_scale,
    activated,
    slope,
    norm_gain,
    w_in,
    w_out,
    b_out,
    layer_scale,
    *rest,
):
    targets = rest[:pieces]
    mismatch_out, d_out, target, d_branch, d_hidden, d_normed = rest[pieces:]
    tile_u, tile_v, channels = middle.shape
    rows = tile_u * tile_v
    hidden = w_in.shape[1]
    chunks = tile_v // CHUNK
    for index, piece in enumerate(targets):
        target[:, aligned(places_ref[index], piece.shape[1]), :] = piece[...]

    for here in row_halves(rows):
        d_normed[here, :] = jnp.dot(
            activated[here, :], w_out[...], preferred_element_type=jnp.float32
        )

    def mismatch_step(index, carry):
        u = index // chunks
        inside = aligned((index % chunks) * CHUNK, CHUNK)
        here = aligned(index * CHUNK, CHUNK)
        mismatch = (
            middle[u, inside, :].astype(jnp.float32)
            + layer_scale[...] * (d_normed[here, :] + b_out[...])
            - target[u, inside, :].astype(jnp.float32)
        )
        mismatch_out[u, inside, :] = mismatch
        d_branch[here, :] = (layer_scale[...] * mismatch).astype(jnp.bfloat16)
        return carry

    lax.fori_loop(0, tile_u * chunks, mismatch_step, 0)

    for start in range(0, hidden, MLP_TILE):
        tile = slice(start, start + MLP_TILE)
        for here in row_halves(rows):
            d_activated = lax.dot_general(
                d_branch[here, :], w_out[tile, :], CONTRACT_LAST, preferred_element_type=jnp.float32
            )
            d_hidden[here, tile] = (d_activated * slope[here, tile]).astype(jnp.bfloat16)
    for here in row_halves(rows):
        d_normed[here, :] = lax.dot_general(
            d_hidden[here, :], w_in[...], CONTRACT_LAST, preferred_element_type=jnp.float32
        )

    def d_norm_step(index, carry):
        u = index // chunks
        inside = aligned((index % chunks) * CHUNK, CHUNK)
        here = aligned(index * CHUNK, CHUNK)
        scaled = d_normed[here, :] * norm_gain[...]
        form = normal_form[here, :]
        d_conv = inv_scale[here, :1] * (
            scaled
            - jnp.mean(scaled, axis=-1, keepdims=True)
            - form * jnp.mean(scaled * form, axis=-1, keepdims=True)
        )
        d_out[u, inside, :] = d_conv.astype(jnp.bfloat16)
        return carry

    lax.fori_loop(0, tile_u * chunks, d_norm_step, 0)


def inner_kernel(core_ref, middle, edge, taps, mismatch, out, padded):
    tile_u, tile_v, channels = mismatch.shape
    fill(padded, (middle,), [(edge, 0)], core_ref[0], tile_v)

    def place(tile, u, base):
        return u, aligned(base, SUBLANES), aligned(tile * LANES, LANES)

    def begin(tile, u, base):
        return mismatch[place(tile, u, base)]

    def store(tile, u, base, value):
        out[place(tile, u, base)] = value

    own = range(REACH, REACH + tile_u)
    depthwise(padded, taps, begin, store, tile_u, tile_v, own, True)


def rim_kernel(core_ref, left, right, left_edge, right_edge, taps, inner, out, padded):
    tile_u, tile_v, channels = inner.shape
    fill(padded, (left, right), [(left_edge, 0), (right_edge, 0)], core_ref[0], tile_v)

    def place(tile, u, base):
        return u, aligned(base, SUBLANES), aligned(tile * LANES, LANES)

    def begin(tile, u, base):
        return inner[place(tile, u, base)]

    def store(tile, u, base, value):
        out[place(tile, u, base)] = value

    sides = [*range(REACH), *range(REACH + tile_u, 2 * REACH + tile_u)]
    depthwise(padded, taps, begin, store, tile_u, tile_v, sides, True)


def call(kernel, name, outs, scratch, scalars, arrays, flops, limit):
    vmem = pl.BlockSpec(memory_space=pltpu.VMEM)
    smem = pl.BlockSpec(memory_space=pltpu.SMEM)
    moved = 1 if flops == 1 else sum(a.size * a.dtype.itemsize for a in arrays) + sum(
        o.size * o.dtype.itemsize for o in outs
    )
    return pl.pallas_call(
        kernel,
        out_shape=tuple(outs),
        in_specs=[smem] * len(scalars) + [vmem] * len(arrays),
        out_specs=(vmem,) * len(outs),
        scratch_shapes=scratch,
        compiler_params=pltpu.CompilerParams(vmem_limit_bytes=limit << 20),
        cost_estimate=pl.CostEstimate(flops=flops, bytes_accessed=moved, transcendentals=0),
        name=name,
    )(*scalars, *arrays)


def edge_lines(tile, core):
    return jnp.where(core == 0, tile[:, -EDGE:], tile[:, :EDGE])


def to_sides_with_edge(tile, core):
    row_count = lax.axis_size("row")
    forward = [(i, i + 1) for i in range(row_count - 1)]
    backward = [(b, a) for a, b in forward]
    edge = lax.ppermute(edge_lines(tile, core), "col", SWAP)
    last = jnp.concatenate([tile[-REACH:], edge[-REACH:]], axis=1)
    first = jnp.concatenate([tile[:REACH], edge[:REACH]], axis=1)
    left = lax.ppermute(last, "row", forward)
    right = lax.ppermute(first, "row", backward)
    return left, right, edge, last, first


def to_sides(tile, core):
    row_count = lax.axis_size("row")
    forward = [(i, i + 1) for i in range(row_count - 1)]
    backward = [(b, a) for a, b in forward]
    left = lax.ppermute(tile[-REACH:], "row", forward)
    right = lax.ppermute(tile[:REACH], "row", backward)
    own = edge_lines(tile, core)
    edge = lax.ppermute(own, "col", SWAP)

    def across(pairs):
        return [(a * 2 + c, b * 2 + 1 - c) for a, b in pairs for c in range(2)]

    left_edge = lax.ppermute(own[-REACH:], ("row", "col"), across(forward))
    right_edge = lax.ppermute(own[:REACH], ("row", "col"), across(backward))
    return left, right, left_edge, edge, right_edge


def find_target(teacher, proj_weight, core, row, tile_u, tile_v):
    row_count = lax.axis_size("row")
    halves = row_count // 2
    channels = proj_weight.shape[1]
    grid_u = tile_u * row_count
    lines = teacher.shape[0] // grid_u
    scalar = core.astype(jnp.int32)[None]
    half_line = grid_u // 2
    by_half = teacher.reshape(lines, 2, half_line, teacher.shape[1])
    size = (lines * half_line, channels)
    fourth = jax.ShapeDtypeStruct((size[0] // 2, channels), jnp.bfloat16)
    outs = [fourth, fourth, jax.ShapeDtypeStruct(size, jnp.float32)]
    upper, lower, home = call(project_kernel, "project", outs, [], [scalar], [by_half, proj_weight], 1, 12)
    received = [lax.ppermute(away, "col", SWAP) for away in (upper, lower)]
    turns = [lax.rem(turn + row, halves) * tile_u for turn in range(halves)]
    if lines % 16:
        received = jnp.concatenate(received).astype(jnp.float32)
        summed = (home + received).astype(jnp.bfloat16)
        by_u = summed.reshape(lines, half_line, channels).transpose(1, 0, 2)
        blocks = [lax.dynamic_slice_in_dim(by_u, turn, tile_u) for turn in turns]
    else:
        blocks = call(
            functools.partial(combine_kernel, half_line),
            "combine",
            [jax.ShapeDtypeStruct((tile_u, lines, channels), jnp.bfloat16)] * halves,
            [pltpu.VMEM((channels // LANES, *size[:1], LANES), jnp.float32)],
            [jnp.stack(turns).astype(jnp.int32)],
            [home, *received],
            1,
            8,
        )
    pieces, places = [], []
    for turn in range(halves):
        pairs = []
        for r in range(row_count):
            for c in range(2):
                goal = (halves * c + (turn + r) % halves) * 2 + r // halves
                pairs.append((r * 2 + c, goal))
        pieces.append(lax.ppermute(blocks[turn], ("row", "col"), pairs))
        places.append(lax.rem(row + (halves - turn), halves) * lines)
    places = jnp.stack(places).astype(jnp.int32)
    if lines % 16:
        whole = jnp.zeros((tile_u, tile_v, channels), jnp.bfloat16)
        for index, piece in enumerate(pieces):
            whole = lax.dynamic_update_slice_in_dim(whole, piece, places[index], axis=1)
        return [whole], jnp.zeros((1,), jnp.int32)
    return pieces, places


def on_device(
    teacher,
    proj_weight,
    student,
    dw_kernel,
    dw_bias,
    norm_gain,
    norm_bias,
    w_in,
    b_in,
    w_out,
    b_out,
    layer_scale,
):
    core = lax.axis_index("col")
    row = lax.axis_index("row")
    tile_v, tile_u, channels = student.shape
    hidden = w_in.shape[1]
    tiles = channels // LANES
    wide = tile_v + 2 * EDGE
    scalar = core.astype(jnp.int32)[None]
    f32, bf16 = jnp.float32, jnp.bfloat16

    middle = student.transpose(1, 0, 2)
    left, right, edge, last, first = to_sides_with_edge(middle, core)
    held, _, _ = lax.optimization_barrier((proj_weight, last, first))
    targets, places = find_target(teacher, held, core, row, tile_u, tile_v)
    taps = jnp.broadcast_to(
        dw_kernel.reshape(TAPS * TAPS, tiles, 1, LANES), (TAPS * TAPS, tiles, SUBLANES, LANES)
    )
    matmul = 2 * tile_u * tile_v * channels * hidden
    rows = tile_u * tile_v
    whole_tile = (tile_u, tile_v, channels)
    normal_form, inv_scale, activated, slope = call(
        up_kernel,
        "up",
        [
            jax.ShapeDtypeStruct((rows, channels), f32),
            jax.ShapeDtypeStruct((rows, LANES), f32),
            jax.ShapeDtypeStruct((rows, hidden), bf16),
            jax.ShapeDtypeStruct((rows, hidden), f32),
        ],
        [
            pltpu.VMEM((tiles, tile_u + 2 * REACH, wide, LANES), f32),
            pltpu.VMEM((rows, channels), bf16),
        ],
        [scalar],
        [left, middle, right, edge, taps, dw_bias[None]]
        + [norm_gain[None], norm_bias[None], w_in, b_in[None]],
        4 * matmul,
        16,
    )
    mismatch, d_conv = call(
        functools.partial(back_kernel, len(targets)),
        "back",
        [jax.ShapeDtypeStruct(whole_tile, f32), jax.ShapeDtypeStruct(whole_tile, bf16)],
        [
            pltpu.VMEM(whole_tile, bf16),
            pltpu.VMEM((rows, channels), bf16),
            pltpu.VMEM((rows, hidden), bf16),
            pltpu.VMEM((rows, channels), f32),
        ],
        [places],
        [middle, normal_form, inv_scale, activated, slope, norm_gain[None], w_in, w_out]
        + [b_out[None], layer_scale[None]]
        + targets,
        4 * matmul,
        16,
    )
    left, right, left_edge, edge, right_edge = to_sides(d_conv, core)
    (inner,) = call(
        inner_kernel,
        "inner",
        [jax.ShapeDtypeStruct(whole_tile, f32)],
        [pltpu.VMEM((tiles, tile_u, wide, LANES), f32)],
        [scalar],
        [d_conv, edge, taps, mismatch],
        matmul,
        8,
    )
    (grad,) = call(
        rim_kernel,
        "rim",
        [jax.ShapeDtypeStruct(whole_tile, f32)],
        [pltpu.VMEM((tiles, 2 * REACH, wide, LANES), f32)],
        [scalar],
        [left, right, left_edge, right_edge, taps, inner],
        matmul,
        8,
    )
    return grad.transpose(1, 0, 2)


def solution(mesh):
    placed = (
        P(("groups", "row"), "col"),
        P("col", None),
        P(("groups", "col"), "row", None),
        P(),
        P(),
        P(),
        P(),
        P(),
        P(),
        P(),
        P(),
        P(),
    )
    return jax.shard_map(
        on_device,
        mesh=mesh,
        in_specs=placed,
        out_specs=P(("groups", "col"), "row", None),
        check_vma=False,
    )
```

```python
import functools

import jax
import jax.numpy as jnp
from jax import lax
from jax.experimental import pallas as pl
from jax.experimental.pallas import tpu as pltpu
from jax.sharding import PartitionSpec as P

NORM_EPSILON = 1e-06
REACH = 3
TAPS = 2 * REACH + 1
LANES = 128
SUBLANES = 8
EDGE = 8
CHUNK = 16
COPIES = 2
MLP_TILE = 512
CONTRACT_LAST = (((1,), (1,)), ((), ()))
SWAP = [(0, 1), (1, 0)]


def aligned(start, size):
    return pl.ds(pl.multiple_of(start, size), size)


def lane_tile(tile):
    return slice(tile * LANES, (tile + 1) * LANES)


def project_kernel(other, core_ref, teacher_hbm, weight, *rest):
    *outs, rows, sems = rest
    half = 1 - core_ref[0] if other else core_ref[0]
    lines, wide, depth = rows.shape
    copies = []
    for index in range(COPIES):
        here = pl.ds(index * (lines // COPIES), lines // COPIES)
        copy = pltpu.make_async_copy(
            teacher_hbm.at[here, half], rows.at[here], sems.at[index]
        )
        copy.start()
        copies.append(copy)
    size = lines * wide // COPIES
    for index, copy in enumerate(copies):
        copy.wait()
        here = pl.ds(index * (lines // COPIES), lines // COPIES)
        product = jnp.dot(
            rows[here].reshape(size, depth), weight[...], preferred_element_type=jnp.float32
        )
        out = outs[index * len(outs) // COPIES]
        start = index * size % out.shape[0]
        out[start : start + size] = product.astype(out.dtype)


def combine_kernel(wide, turns_ref, home, upper, lower, *rest):
    *blocks, summed = rest
    half = upper.shape[0]
    for tile in range(summed.shape[0]):
        lanes = lane_tile(tile)
        for start, received in ((0, upper), (half, lower)):
            here = slice(start, start + half)
            summed[tile, here] = home[here, lanes] + received[:, lanes].astype(jnp.float32)
    for index, block in enumerate(blocks):
        tile_u, lines, _ = block.shape
        for u in range(tile_u):
            rows = pl.ds(turns_ref[index] + u, lines, stride=wide)
            for tile in range(summed.shape[0]):
                block[u, :, lane_tile(tile)] = summed[tile, rows, :].astype(jnp.bfloat16)


def spread_taps(taps, kernel):
    for row_tap in range(TAPS):
        for col_tap in range(TAPS):
            for tile in range(taps.shape[1]):
                line = kernel[row_tap, col_tap : col_tap + 1, lane_tile(tile)]
                taps[row_tap * TAPS + col_tap, tile] = jnp.broadcast_to(line, (SUBLANES, LANES))


def spread(padded, place, part, source, start, row, count):
    for tile in range(padded.shape[0]):
        padded[tile, place, pl.ds(row, count), :] = part[
            source, pl.ds(start, count), lane_tile(tile)
        ].astype(jnp.float32)


def depthwise(padded, taps, begin, store, tile_u, count, offset, sources, flip):
    tiles = padded.shape[0]
    blocks = count // (2 * SUBLANES)

    def step(index, carry):
        tile = index // blocks
        base = pl.multiple_of((index % blocks) * (2 * SUBLANES), 2 * SUBLANES)
        sums = [
            [begin(tile, u, base + half * SUBLANES) for u in range(tile_u)] for half in range(2)
        ]
        for row_tap in range(TAPS):
            weights = []
            for col_tap in range(TAPS):
                tap = row_tap * TAPS + col_tap
                weights.append(taps[TAPS * TAPS - 1 - tap if flip else tap, tile])
            for place, source in enumerate(sources):
                for half in range(2):
                    row = base + (half * SUBLANES + row_tap) + offset
                    values = padded[tile, place, pl.ds(row, SUBLANES), :]
                    for u in range(max(0, source - TAPS + 1), min(tile_u, source + 1)):
                        term = weights[source - u] * values
                        sums[half][u] = term if sums[half][u] is None else sums[half][u] + term
        for half in range(2):
            for u in range(tile_u):
                store(tile, u, base + half * SUBLANES, sums[half][u])
        return carry

    lax.fori_loop(0, tiles * blocks, step, 0)


def row_parts(rows):
    half = rows // 2 // 16 * 16
    return slice(0, half), slice(half, rows)


def begins(core, near, tile_v, count):
    top = core if near else 1 - core
    return pl.multiple_of((1 - top) * (tile_v - count), 16)


def up(core, near, count, left, middle, edge, right, kernel, bias, gain, shift, w_in, b_in, refs):
    normal_form, inv_scale, activated, slope, padded, taps, normed, wait_weights = refs
    tile_u, tile_v, channels = middle.shape
    tiles = channels // LANES
    rows = tile_u * count
    hidden = activated.shape[1]
    outside_first = core if near else 1 - core
    start = pl.multiple_of((1 - outside_first) * (tile_v - count - EDGE), EDGE)
    inside = pl.multiple_of(outside_first * EDGE, EDGE)
    outside = pl.multiple_of((1 - outside_first) * (count + EDGE), EDGE)
    spread_taps(taps, kernel)
    place = 0
    for part, rim, begin in ((left, left, tile_v), (middle, edge, 0), (right, right, tile_v)):
        for u in range(part.shape[0]):
            spread(padded, place, part, u, start, inside, count + EDGE)
            if near:
                spread(padded, place, rim, u, begin, outside, EDGE)
            else:
                for tile in range(tiles):
                    padded[tile, place, pl.ds(outside, EDGE), :] = jnp.zeros(
                        (EDGE, LANES), jnp.float32
                    )
            place += 1

    def nothing(tile, u, base):
        return None

    def store(tile, u, base, value):
        row = aligned(u * count + base, SUBLANES)
        normal_form[row, aligned(tile * LANES, LANES)] = value

    sources = range(tile_u + 2 * REACH)
    depthwise(padded, taps, nothing, store, tile_u, count, EDGE - REACH, sources, False)

    def norm_step(index, carry):
        here = aligned(index * CHUNK, CHUNK)
        conv = normal_form[here, :] + bias[...]
        centred = conv - jnp.mean(conv, axis=-1, keepdims=True)
        variance = jnp.mean(centred * centred, axis=-1, keepdims=True)
        inverse = lax.rsqrt(variance + NORM_EPSILON)
        form = centred * inverse
        normal_form[here, :] = form
        inv_scale[here, :] = jnp.broadcast_to(inverse, (CHUNK, LANES))
        normed[here, :] = (form * gain[...] + shift[...]).astype(jnp.bfloat16)
        return carry

    lax.fori_loop(0, rows // CHUNK, norm_step, 0)

    wait_weights()
    for start in range(0, hidden, MLP_TILE):
        tile = slice(start, start + MLP_TILE)
        for here in row_parts(rows):
            pre = (
                jnp.dot(normed[here, :], w_in[:, tile], preferred_element_type=jnp.float32)
                + b_in[:, tile]
            )
            phi = 0.5 * (1.0 + lax.erf(pre * 0.7071067811865476))
            activated[here, tile] = (pre * phi).astype(jnp.bfloat16)
            slope[here, tile] = phi + pre * jnp.exp(-0.5 * pre * pre) * 0.3989422804014327


def back(core, near, count, middle, gain, w_in, w_out, b_out, scale, places, targets, refs):
    (
        normal_form, inv_scale, activated, slope,
        mismatch_out, d_out, last, first, target, d_branch, d_hidden, d_normed,
    ) = refs
    tile_u, tile_v, channels = middle.shape
    rows = tile_u * count
    hidden = activated.shape[1]
    chunks = count // CHUNK
    base = begins(core, near, tile_v, count)
    for index, piece in enumerate(targets):
        target[:, aligned(places[index], piece.shape[1]), :] = piece[...]

    for here in row_parts(rows):
        d_normed[here, :] = jnp.dot(
            activated[here, :], w_out[...], preferred_element_type=jnp.float32
        )

    def mismatch_step(index, carry):
        u = index // chunks
        inside = aligned((index % chunks) * CHUNK, CHUNK)
        whole = aligned(base + (index % chunks) * CHUNK, CHUNK)
        here = aligned(index * CHUNK, CHUNK)
        mismatch = (
            middle[u, whole, :].astype(jnp.float32)
            + scale[...] * (d_normed[here, :] + b_out[...])
            - target[u, whole, :].astype(jnp.float32)
        )
        mismatch_out[u, inside, :] = mismatch
        d_branch[here, :] = (scale[...] * mismatch).astype(jnp.bfloat16)
        return carry

    lax.fori_loop(0, tile_u * chunks, mismatch_step, 0)

    for start in range(0, hidden, MLP_TILE):
        tile = slice(start, start + MLP_TILE)
        for here in row_parts(rows):
            d_activated = lax.dot_general(
                d_branch[here, :], w_out[tile, :], CONTRACT_LAST, preferred_element_type=jnp.float32
            )
            d_hidden[here, tile] = (d_activated * slope[here, tile]).astype(jnp.bfloat16)
    for here in row_parts(rows):
        d_normed[here, :] = lax.dot_general(
            d_hidden[here, :], w_in[...], CONTRACT_LAST, preferred_element_type=jnp.float32
        )

    def d_norm_step(index, carry):
        u = index // chunks
        inside = aligned((index % chunks) * CHUNK, CHUNK)
        here = aligned(index * CHUNK, CHUNK)
        scaled = d_normed[here, :] * gain[...]
        form = normal_form[here, :]
        d_conv = inv_scale[here, :1] * (
            scaled
            - jnp.mean(scaled, axis=-1, keepdims=True)
            - form * jnp.mean(scaled * form, axis=-1, keepdims=True)
        )
        d_out[u, inside, :] = d_conv.astype(jnp.bfloat16)
        return carry

    lax.fori_loop(0, tile_u * chunks, d_norm_step, 0)
    last[:, :count, :] = d_out[tile_u - REACH :]
    first[:, :count, :] = d_out[:REACH]


def near_up_kernel(
    count, core_ref, left, middle, edge, right, kernel, bias, gain, shift, w_in_hbm, b_in,
    normal_form, inv_scale, activated, slope, padded, taps, normed, w_in, sem,
):
    copy = pltpu.make_async_copy(w_in_hbm, w_in, sem)
    copy.start()
    refs = normal_form, inv_scale, activated, slope, padded, taps, normed, copy.wait
    up(
        core_ref[0], True, count, left, middle, edge, right, kernel, bias, gain, shift,
        w_in, b_in, refs,
    )


def near_back_kernel(
    pieces, count, core_ref, places_ref, middle, normal_form, inv_scale, activated, slope,
    gain, w_in, w_out, b_out, scale, *rest,
):
    targets = rest[:pieces]
    mismatch_out, d_out, last, first, own_edge, *scratch = rest[pieces:]
    core = core_ref[0]
    refs = normal_form, inv_scale, activated, slope, mismatch_out, d_out, last, first, *scratch
    back(core, True, count, middle, gain, w_in, w_out, b_out, scale, places_ref, targets, refs)
    border = pl.multiple_of((1 - core) * (count - EDGE), EDGE)
    own_edge[...] = d_out[:, pl.ds(border, EDGE), :]


def far_kernel(
    pieces, count, core_ref, places_ref, left, middle, edge, right, kernel, bias, gain, shift,
    w_in, b_in, w_out, b_out, scale, d_edge, *rest,
):
    targets = rest[:pieces]
    mismatch_out, d_out, last, first = rest[pieces : pieces + 4]
    (
        normal_form, inv_scale, activated, slope, padded, taps, normed,
        target, d_branch, d_hidden, d_normed,
    ) = rest[pieces + 4 :]
    core = core_ref[0]
    refs = normal_form, inv_scale, activated, slope, padded, taps, normed, lambda: None
    up(
        core, False, count, left, middle, edge, right, kernel, bias, gain, shift, w_in, b_in, refs
    )
    refs = (
        normal_form, inv_scale, activated, slope,
        mismatch_out, d_out, last, first, target, d_branch, d_hidden, d_normed,
    )
    back(core, False, count, middle, gain, w_in, w_out, b_out, scale, places_ref, targets, refs)
    last[:, count:, :] = d_edge[d_edge.shape[0] - REACH :]
    first[:, count:, :] = d_edge[:REACH]


def whole_rows(padded, place, near, far, edge, u, start, core, tile_v):
    near_count, far_count = near.shape[1], tile_v - near.shape[1]
    near_base = EDGE + begins(core, True, tile_v, near_count)
    far_base = EDGE + begins(core, False, tile_v, far_count)
    spread(padded, place, near, u, 0, pl.multiple_of(near_base, EDGE), near_count)
    spread(padded, place, far, u, 0, pl.multiple_of(far_base, EDGE), far_count)
    for tile in range(padded.shape[0]):
        rim = edge[u, start : start + EDGE, lane_tile(tile)].astype(jnp.float32)
        nothing = jnp.zeros_like(rim)
        padded[tile, place, 0:EDGE, :] = jnp.where(core == 1, rim, nothing)
        padded[tile, place, EDGE + tile_v : 2 * EDGE + tile_v, :] = jnp.where(
            core == 0, rim, nothing
        )


def inner_kernel(core_ref, near, far, edge, kernel, near_mismatch, far_mismatch, out, padded, taps):
    tile_u, tile_v, channels = out.shape
    core = core_ref[0]
    spread_taps(taps, kernel)
    for u in range(tile_u):
        whole_rows(padded, u, near, far, edge, u, 0, core, tile_v)
    for is_near, mismatch in ((True, near_mismatch), (False, far_mismatch)):
        count = mismatch.shape[1]
        first = begins(core, is_near, tile_v, count)

        def begin(tile, u, base):
            return mismatch[u, aligned(base, SUBLANES), aligned(tile * LANES, LANES)]

        def store(tile, u, base, value):
            out[u, aligned(first + base, SUBLANES), aligned(tile * LANES, LANES)] = value

        own = range(REACH, REACH + tile_u)
        depthwise(padded, taps, begin, store, tile_u, count, first + EDGE - REACH, own, True)


def rim_kernel(
    core_ref, near_left, near_right, far_left, far_right, kernel, inner, out, padded, taps
):
    tile_u, tile_v, channels = inner.shape
    core = core_ref[0]
    far_count = tile_v - near_left.shape[1]
    spread_taps(taps, kernel)
    place = 0
    for near, far in ((near_left, far_left), (near_right, far_right)):
        for u in range(REACH):
            whole_rows(padded, place, near, far, far, u, far_count, core, tile_v)
            place += 1

    def begin(tile, u, base):
        return inner[u, aligned(base, SUBLANES), aligned(tile * LANES, LANES)]

    def store(tile, u, base, value):
        out[aligned(base, SUBLANES), u, aligned(tile * LANES, LANES)] = value

    sides = [*range(REACH), *range(REACH + tile_u, 2 * REACH + tile_u)]
    depthwise(padded, taps, begin, store, tile_u, tile_v, EDGE - REACH, sides, True)


def call(kernel, name, outs, scratch, scalars, arrays, flops, limit, left_in_hbm=()):
    vmem = pl.BlockSpec(memory_space=pltpu.VMEM)
    smem = pl.BlockSpec(memory_space=pltpu.SMEM)
    hbm = pl.BlockSpec(memory_space=pltpu.HBM)
    moved = 1 if flops == 1 else sum(a.size * a.dtype.itemsize for a in [*arrays, *outs])
    arrays = [
        pltpu.with_memory_space_constraint(a, pltpu.HBM) if index in left_in_hbm else a
        for index, a in enumerate(arrays)
    ]
    specs = [hbm if index in left_in_hbm else vmem for index in range(len(arrays))]
    return pl.pallas_call(
        kernel,
        out_shape=tuple(outs),
        in_specs=[smem] * len(scalars) + specs,
        out_specs=(vmem,) * len(outs),
        scratch_shapes=scratch,
        compiler_params=pltpu.CompilerParams(vmem_limit_bytes=limit << 20),
        cost_estimate=pl.CostEstimate(flops=flops, bytes_accessed=moved, transcendentals=0),
        name=name,
    )(*scalars, *arrays)


def send_sides(last, first):
    row_count = lax.axis_size("row")
    forward = [(i, i + 1) for i in range(row_count - 1)]
    backward = [(b, a) for a, b in forward]
    return lax.ppermute(last, "row", forward), lax.ppermute(first, "row", backward)


def with_edge(block, edge):
    return (
        jnp.concatenate([block[-REACH:], edge[-REACH:]], axis=1),
        jnp.concatenate([block[:REACH], edge[:REACH]], axis=1),
    )


def find_target(teacher, proj_weight, core, row, tile_u, tile_v):
    row_count = lax.axis_size("row")
    halves = row_count // 2
    channels = proj_weight.shape[1]
    grid_u = tile_u * row_count
    lines = teacher.shape[0] // grid_u
    scalar = core.astype(jnp.int32)[None]
    half_line = grid_u // 2
    by_half = teacher.reshape(lines, 2, half_line, teacher.shape[1])
    size = (lines * half_line, channels)
    fourth = jax.ShapeDtypeStruct((size[0] // 2, channels), jnp.bfloat16)
    scratch = [
        pltpu.VMEM((lines, half_line, teacher.shape[1]), jnp.bfloat16),
        pltpu.SemaphoreType.DMA((COPIES,)),
    ]
    upper, lower = call(
        functools.partial(project_kernel, True),
        "project_away", [fourth] * 2, scratch, [scalar], [by_half, proj_weight], 1, 12, (0,),
    )
    (home,) = call(
        functools.partial(project_kernel, False),
        "project_home", [jax.ShapeDtypeStruct(size, jnp.float32)],
        scratch, [scalar], [by_half, proj_weight], 1, 12, (0,),
    )
    received = [lax.ppermute(away, "col", SWAP) for away in (upper, lower)]
    turns = [lax.rem(turn + row, halves) * tile_u for turn in range(halves)]
    if lines % 16:
        received = jnp.concatenate(received).astype(jnp.float32)
        summed = (home + received).astype(jnp.bfloat16)
        by_u = summed.reshape(lines, half_line, channels).transpose(1, 0, 2)
        blocks = [lax.dynamic_slice_in_dim(by_u, turn, tile_u) for turn in turns]
    else:
        blocks = call(
            functools.partial(combine_kernel, half_line),
            "combine",
            [jax.ShapeDtypeStruct((tile_u, lines, channels), jnp.bfloat16)] * halves,
            [pltpu.VMEM((channels // LANES, *size[:1], LANES), jnp.float32)],
            [jnp.stack(turns).astype(jnp.int32)],
            [home, *received],
            1,
            8,
        )
    pieces, places = [], []
    for turn in range(halves):
        pairs = []
        for r in range(row_count):
            for c in range(2):
                goal = (halves * c + (turn + r) % halves) * 2 + r // halves
                pairs.append((r * 2 + c, goal))
        pieces.append(lax.ppermute(blocks[turn], ("row", "col"), pairs))
        places.append(lax.rem(row + (halves - turn), halves) * lines)
    places = jnp.stack(places).astype(jnp.int32)
    if lines % 16:
        whole = jnp.zeros((tile_u, tile_v, channels), jnp.bfloat16)
        for index, piece in enumerate(pieces):
            whole = lax.dynamic_update_slice_in_dim(whole, piece, places[index], axis=1)
        return [whole], jnp.zeros((1,), jnp.int32)
    return pieces, places


def on_device(
    teacher,
    proj_weight,
    student,
    dw_kernel,
    dw_bias,
    norm_gain,
    norm_bias,
    w_in,
    b_in,
    w_out,
    b_out,
    layer_scale,
):
    core = lax.axis_index("col")
    row = lax.axis_index("row")
    tile_v, tile_u, channels = student.shape
    hidden = w_in.shape[1]
    tiles = channels // LANES
    wide = tile_v + 2 * EDGE
    scalar = core.astype(jnp.int32)[None]
    f32, bf16 = jnp.float32, jnp.bfloat16
    far_count = tile_v * 3 // 8 // CHUNK * CHUNK
    near_count = tile_v - far_count

    own_edge = jnp.where(core == 0, student[-EDGE:], student[:EDGE]).transpose(1, 0, 2)
    edge = lax.ppermute(own_edge, "col", SWAP)
    middle = student.transpose(1, 0, 2)
    last, first = with_edge(middle, edge)
    left, right = send_sides(last, first)
    held, _, _ = lax.optimization_barrier((proj_weight, last, first))
    targets, places = find_target(teacher, held, core, row, tile_u, tile_v)
    matmul = 2 * tile_u * tile_v * channels * hidden
    whole_tile = (tile_u, tile_v, channels)
    taps = pltpu.VMEM((TAPS * TAPS, tiles, SUBLANES, LANES), f32)

    def padded(places, count):
        return pltpu.VMEM((tiles, places, count + 2 * EDGE, LANES), f32)

    def kept(make, rows):
        return [
            make((rows, channels), f32),
            make((rows, LANES), f32),
            make((rows, hidden), bf16),
            make((rows, hidden), f32),
        ]

    def up_scratch(count):
        return [
            padded(tile_u + 2 * REACH, count), taps, pltpu.VMEM((tile_u * count, channels), bf16)
        ]

    def back_scratch(rows):
        return [
            pltpu.VMEM(whole_tile, bf16),
            pltpu.VMEM((rows, channels), bf16),
            pltpu.VMEM((rows, hidden), bf16),
            pltpu.VMEM((rows, channels), f32),
        ]

    def back_outs(count, sent):
        part, side = (tile_u, count, channels), (REACH, sent, channels)
        kinds = [(part, f32), (part, bf16), (side, bf16), (side, bf16)]
        return [jax.ShapeDtypeStruct(*kind) for kind in kinds]

    conv_args = [left, middle, edge, right, dw_kernel, dw_bias[None], norm_gain[None]]
    conv_args += [norm_bias[None], w_in, b_in[None]]
    near_rows, far_rows = tile_u * near_count, tile_u * far_count
    saved = call(
        functools.partial(near_up_kernel, near_count),
        "near_up",
        kept(jax.ShapeDtypeStruct, near_rows),
        [*up_scratch(near_count), pltpu.VMEM(w_in.shape, bf16), pltpu.SemaphoreType.DMA],
        [scalar],
        conv_args,
        2 * matmul,
        16,
        (8,),
    )
    near_mismatch, near, last, first, own_edge = call(
        functools.partial(near_back_kernel, len(targets), near_count),
        "near_back",
        back_outs(near_count, near_count)
        + [jax.ShapeDtypeStruct((tile_u, EDGE, channels), bf16)],
        back_scratch(near_rows),
        [scalar, places],
        [middle, *saved, norm_gain[None], w_in, w_out, b_out[None], layer_scale[None], *targets],
        1,
        16,
    )
    near_left, near_right = send_sides(last, first)
    d_edge = lax.ppermute(own_edge, "col", SWAP)
    far_mismatch, far, last, first = call(
        functools.partial(far_kernel, len(targets), far_count),
        "far",
        back_outs(far_count, far_count + EDGE),
        [*kept(pltpu.VMEM, far_rows), *up_scratch(far_count), *back_scratch(far_rows)],
        [scalar, places],
        [*conv_args, w_out, b_out[None], layer_scale[None], d_edge, *targets],
        1,
        24,
    )
    far_left, far_right = send_sides(last, first)
    (inner,) = call(
        inner_kernel,
        "inner",
        [jax.ShapeDtypeStruct(whole_tile, f32)],
        [padded(tile_u, tile_v), taps],
        [scalar],
        [near, far, d_edge, dw_kernel, near_mismatch, far_mismatch],
        1,
        8,
    )
    (grad,) = call(
        rim_kernel,
        "rim",
        [jax.ShapeDtypeStruct((tile_v, tile_u, channels), f32)],
        [padded(2 * REACH, tile_v), taps],
        [scalar],
        [near_left, near_right, far_left, far_right, dw_kernel, inner],
        1,
        8,
    )
    return grad


def solution(mesh):
    placed = (
        P(("groups", "row"), "col"),
        P("col", None),
        P(("groups", "col"), "row", None),
        P(),
        P(),
        P(),
        P(),
        P(),
        P(),
        P(),
        P(),
        P(),
    )
    return jax.shard_map(
        on_device,
        mesh=mesh,
        in_specs=placed,
        out_specs=P(("groups", "col"), "row", None),
        check_vma=False,
    )
```

```python
import functools

import jax
import jax.numpy as jnp
from jax import lax
from jax.experimental import pallas as pl
from jax.experimental.pallas import tpu as pltpu
from jax.sharding import PartitionSpec as P

NORM_EPSILON = 1e-06
REACH = 3
TAPS = 2 * REACH + 1
LANES = 128
SUBLANES = 8
EDGE = 8
CHUNK = 16
UNROLL = 16
COPIES = 2
MLP_TILE = 512
CONTRACT_LAST = (((1,), (1,)), ((), ()))
SWAP = [(0, 1), (1, 0)]


def aligned(start, size):
    return pl.ds(pl.multiple_of(start, size), size)


def lane_tile(tile):
    return slice(tile * LANES, (tile + 1) * LANES)


def project_kernel(other, core_ref, teacher_hbm, weight, *rest):
    *outs, rows, sems = rest
    half = 1 - core_ref[0] if other else core_ref[0]
    lines, wide, depth = rows.shape
    copies = []
    for index in range(COPIES):
        here = pl.ds(index * (lines // COPIES), lines // COPIES)
        copy = pltpu.make_async_copy(
            teacher_hbm.at[here, half], rows.at[here], sems.at[index]
        )
        copy.start()
        copies.append(copy)
    size = lines * wide // COPIES
    for index, copy in enumerate(copies):
        copy.wait()
        here = pl.ds(index * (lines // COPIES), lines // COPIES)
        product = jnp.dot(
            rows[here].reshape(size, depth), weight[...], preferred_element_type=jnp.float32
        )
        out = outs[index * len(outs) // COPIES]
        start = index * size % out.shape[0]
        out[start : start + size] = product.astype(out.dtype)


def combine_kernel(wide, turns_ref, home, upper, lower, *rest):
    *blocks, summed = rest
    half = upper.shape[0]
    for tile in range(summed.shape[0]):
        lanes = lane_tile(tile)
        for start, received in ((0, upper), (half, lower)):
            here = slice(start, start + half)
            summed[tile, here] = home[here, lanes] + received[:, lanes].astype(jnp.float32)
    for index, block in enumerate(blocks):
        tile_u, lines, _ = block.shape
        for u in range(tile_u):
            rows = pl.ds(turns_ref[index] + u, lines, stride=wide)
            for tile in range(summed.shape[0]):
                block[u, :, lane_tile(tile)] = summed[tile, rows, :].astype(jnp.bfloat16)


def spread_taps(taps, kernel):
    for row_tap in range(TAPS):
        for col_tap in range(TAPS):
            for tile in range(taps.shape[1]):
                line = kernel[row_tap, col_tap : col_tap + 1, lane_tile(tile)]
                taps[row_tap * TAPS + col_tap, tile] = jnp.broadcast_to(line, (SUBLANES, LANES))


def spread(padded, place, part, source, start, row, count):
    for tile in range(padded.shape[0]):
        padded[tile, place, pl.ds(row, count), :] = part[
            source, pl.ds(start, count), lane_tile(tile)
        ].astype(jnp.float32)


def depthwise(padded, taps, begin, store, tile_u, count, offset, sources, flip):
    tiles = padded.shape[0]
    blocks = count // (2 * SUBLANES)

    def step(index, carry):
        tile = index // blocks
        base = pl.multiple_of((index % blocks) * (2 * SUBLANES), 2 * SUBLANES)
        sums = [
            [begin(tile, u, base + half * SUBLANES) for u in range(tile_u)] for half in range(2)
        ]
        for row_tap in range(TAPS):
            weights = []
            for col_tap in range(TAPS):
                tap = row_tap * TAPS + col_tap
                weights.append(taps[TAPS * TAPS - 1 - tap if flip else tap, tile])
            for place, source in enumerate(sources):
                for half in range(2):
                    row = base + (half * SUBLANES + row_tap) + offset
                    values = padded[tile, place, pl.ds(row, SUBLANES), :]
                    for u in range(max(0, source - TAPS + 1), min(tile_u, source + 1)):
                        term = weights[source - u] * values
                        sums[half][u] = term if sums[half][u] is None else sums[half][u] + term
        for half in range(2):
            for u in range(tile_u):
                store(tile, u, base + half * SUBLANES, sums[half][u])
        return carry

    lax.fori_loop(0, tiles * blocks, step, 0)


def row_parts(rows):
    half = rows // 2 // 16 * 16
    return slice(0, half), slice(half, rows)


def repeat(count, step):
    unroll = max(n for n in range(1, UNROLL + 1) if count % n == 0)

    def body(index, carry):
        step(index)
        return carry

    lax.fori_loop(0, count, body, 0, unroll=unroll)


def fill(padded, parts, core, tile_v):
    place = 0
    for part, edge, start in parts:
        for u in range(part.shape[0]):
            spread(padded, place, part, u, 0, EDGE, tile_v)
            for tile in range(padded.shape[0]):
                rim = edge[u, start : start + EDGE, lane_tile(tile)].astype(jnp.float32)
                nothing = jnp.zeros_like(rim)
                padded[tile, place, 0:EDGE, :] = jnp.where(core == 1, rim, nothing)
                padded[tile, place, EDGE + tile_v : 2 * EDGE + tile_v, :] = jnp.where(
                    core == 0, rim, nothing
                )
            place += 1


def inner_kernel(flip, core_ref, middle, edge, kernel, base_value, out, padded, taps):
    tile_u, tile_v, channels = middle.shape
    spread_taps(taps, kernel)
    fill(padded, [(middle, edge, 0)], core_ref[0], tile_v)

    def place(tile, u, base):
        return aligned(u * tile_v + base, SUBLANES), aligned(tile * LANES, LANES)

    def begin(tile, u, base):
        rows, lanes = place(tile, u, base)
        if base_value.shape[0] == 1:
            return jnp.broadcast_to(base_value[:, lanes], (SUBLANES, LANES))
        return base_value[rows, lanes]

    def store(tile, u, base, value):
        out[place(tile, u, base)] = value

    own = range(REACH, REACH + tile_u)
    depthwise(padded, taps, begin, store, tile_u, tile_v, EDGE - REACH, own, flip)


def rim_conv(flip, core, left, right, left_edge, right_edge, kernel, inner, store, padded, taps):
    sides, tile_v = padded.shape[1], padded.shape[2] - 2 * EDGE
    tile_u = inner.shape[0] // tile_v
    spread_taps(taps, kernel)
    fill(padded, [(left, *left_edge), (right, *right_edge)], core, tile_v)

    def begin(tile, u, base):
        return inner[aligned(u * tile_v + base, SUBLANES), aligned(tile * LANES, LANES)]

    sources = [*range(REACH), *range(REACH + tile_u, 2 * REACH + tile_u)]
    depthwise(padded, taps, begin, store, tile_u, tile_v, EDGE - REACH, sources, flip)


def up_kernel(
    core_ref, left, right, kernel, inner, gain, shift, w_in_hbm, b_in,
    normal_form, inv_scale, activated, slope, padded, taps, normed, w_in, sem,
):
    copy = pltpu.make_async_copy(w_in_hbm, w_in, sem)
    copy.start()
    rows, hidden = activated.shape
    tile_v = padded.shape[2] - 2 * EDGE

    def store(tile, u, base, value):
        row = aligned(u * tile_v + base, SUBLANES)
        normal_form[row, aligned(tile * LANES, LANES)] = value

    left_edge, right_edge = (left, tile_v), (right, tile_v)
    rim_conv(
        False, core_ref[0], left, right, left_edge, right_edge, kernel, inner, store, padded, taps
    )

    def norm_step(index):
        here = aligned(index * CHUNK, CHUNK)
        conv = normal_form[here, :]
        centred = conv - jnp.mean(conv, axis=-1, keepdims=True)
        variance = jnp.mean(centred * centred, axis=-1, keepdims=True)
        inverse = lax.rsqrt(variance + NORM_EPSILON)
        form = centred * inverse
        normal_form[here, :] = form
        inv_scale[here, :] = jnp.broadcast_to(inverse, (CHUNK, LANES))
        normed[here, :] = (form * gain[...] + shift[...]).astype(jnp.bfloat16)

    repeat(rows // CHUNK, norm_step)

    copy.wait()
    for start in range(0, hidden, MLP_TILE):
        tile = slice(start, start + MLP_TILE)
        for here in row_parts(rows):
            pre = (
                jnp.dot(normed[here, :], w_in[:, tile], preferred_element_type=jnp.float32)
                + b_in[:, tile]
            )
            phi = 0.5 * (1.0 + lax.erf(pre * 0.7071067811865476))
            activated[here, tile] = (pre * phi).astype(jnp.bfloat16)
            slope[here, tile] = phi + pre * jnp.exp(-0.5 * pre * pre) * 0.3989422804014327


def back_kernel(
    pieces, places_ref, middle, normal_form, inv_scale, activated, slope,
    gain, w_in, w_out, b_out, scale, *rest,
):
    targets = rest[:pieces]
    mismatch_out, d_out, target, d_branch, d_hidden, d_normed = rest[pieces:]
    tile_u, tile_v, channels = middle.shape
    rows, hidden = activated.shape
    chunks = tile_v // CHUNK
    for index, piece in enumerate(targets):
        target[:, aligned(places_ref[index], piece.shape[1]), :] = piece[...]

    for here in row_parts(rows):
        d_normed[here, :] = jnp.dot(
            activated[here, :], w_out[...], preferred_element_type=jnp.float32
        )

    def mismatch_step(index):
        u = index // chunks
        inside = aligned((index % chunks) * CHUNK, CHUNK)
        here = aligned(index * CHUNK, CHUNK)
        mismatch = (
            middle[u, inside, :].astype(jnp.float32)
            + scale[...] * (d_normed[here, :] + b_out[...])
            - target[u, inside, :].astype(jnp.float32)
        )
        mismatch_out[here, :] = mismatch
        d_branch[here, :] = (scale[...] * mismatch).astype(jnp.bfloat16)

    repeat(tile_u * chunks, mismatch_step)

    for start in range(0, hidden, MLP_TILE):
        tile = slice(start, start + MLP_TILE)
        for here in row_parts(rows):
            d_activated = lax.dot_general(
                d_branch[here, :], w_out[tile, :], CONTRACT_LAST, preferred_element_type=jnp.float32
            )
            d_hidden[here, tile] = (d_activated * slope[here, tile]).astype(jnp.bfloat16)
    for here in row_parts(rows):
        d_normed[here, :] = lax.dot_general(
            d_hidden[here, :], w_in[...], CONTRACT_LAST, preferred_element_type=jnp.float32
        )

    def d_norm_step(index):
        u = index // chunks
        inside = aligned((index % chunks) * CHUNK, CHUNK)
        here = aligned(index * CHUNK, CHUNK)
        scaled = d_normed[here, :] * gain[...]
        form = normal_form[here, :]
        d_conv = inv_scale[here, :1] * (
            scaled
            - jnp.mean(scaled, axis=-1, keepdims=True)
            - form * jnp.mean(scaled * form, axis=-1, keepdims=True)
        )
        d_out[u, inside, :] = d_conv.astype(jnp.bfloat16)

    repeat(tile_u * chunks, d_norm_step)


def last_kernel(
    core_ref, left, right, left_edge, right_edge, kernel, inner, out, padded, taps, turned
):
    tile_v, tile_u, channels = out.shape

    def store(tile, u, base, value):
        turned[tile, aligned(u * tile_v + base, SUBLANES), :] = value

    edges = (left_edge, 0), (right_edge, 0)
    rim_conv(True, core_ref[0], left, right, *edges, kernel, inner, store, padded, taps)

    def turn_step(line):
        for tile in range(turned.shape[0]):
            out[line, :, lane_tile(tile)] = turned[tile, pl.ds(line, tile_u, stride=tile_v), :]

    repeat(tile_v, turn_step)


def call(kernel, name, outs, scratch, scalars, arrays, flops, limit, left_in_hbm=()):
    vmem = pl.BlockSpec(memory_space=pltpu.VMEM)
    smem = pl.BlockSpec(memory_space=pltpu.SMEM)
    hbm = pl.BlockSpec(memory_space=pltpu.HBM)
    moved = 1 if flops == 1 else sum(a.size * a.dtype.itemsize for a in [*arrays, *outs])
    arrays = [
        pltpu.with_memory_space_constraint(a, pltpu.HBM) if index in left_in_hbm else a
        for index, a in enumerate(arrays)
    ]
    specs = [hbm if index in left_in_hbm else vmem for index in range(len(arrays))]
    return pl.pallas_call(
        kernel,
        out_shape=tuple(outs),
        in_specs=[smem] * len(scalars) + specs,
        out_specs=(vmem,) * len(outs),
        scratch_shapes=scratch,
        compiler_params=pltpu.CompilerParams(vmem_limit_bytes=limit << 20),
        cost_estimate=pl.CostEstimate(flops=flops, bytes_accessed=moved, transcendentals=0),
        name=name,
    )(*scalars, *arrays)


def send_sides(last, first):
    row_count = lax.axis_size("row")
    forward = [(i, i + 1) for i in range(row_count - 1)]
    backward = [(b, a) for a, b in forward]
    return lax.ppermute(last, "row", forward), lax.ppermute(first, "row", backward)


def with_edge(block, edge):
    return (
        jnp.concatenate([block[-REACH:], edge[-REACH:]], axis=1),
        jnp.concatenate([block[:REACH], edge[:REACH]], axis=1),
    )


def send_edges(tile, core):
    row_count = lax.axis_size("row")
    own = jnp.where(core == 0, tile[:, -EDGE:], tile[:, :EDGE])
    forward = [(i * 2 + c, i * 2 + 3 - c) for i in range(row_count - 1) for c in range(2)]
    backward = [(b, a) for a, b in forward]
    return (
        lax.ppermute(own[-REACH:], ("row", "col"), forward),
        lax.ppermute(own, "col", SWAP),
        lax.ppermute(own[:REACH], ("row", "col"), backward),
    )


def find_target(teacher, proj_weight, core, row, tile_u, tile_v):
    row_count = lax.axis_size("row")
    halves = row_count // 2
    channels = proj_weight.shape[1]
    grid_u = tile_u * row_count
    lines = teacher.shape[0] // grid_u
    scalar = core.astype(jnp.int32)[None]
    half_line = grid_u // 2
    by_half = teacher.reshape(lines, 2, half_line, teacher.shape[1])
    size = (lines * half_line, channels)
    fourth = jax.ShapeDtypeStruct((size[0] // 2, channels), jnp.bfloat16)
    scratch = [
        pltpu.VMEM((lines, half_line, teacher.shape[1]), jnp.bfloat16),
        pltpu.SemaphoreType.DMA((COPIES,)),
    ]
    upper, lower = call(
        functools.partial(project_kernel, True),
        "project_away", [fourth] * 2, scratch, [scalar], [by_half, proj_weight], 1, 12, (0,),
    )
    (home,) = call(
        functools.partial(project_kernel, False),
        "project_home", [jax.ShapeDtypeStruct(size, jnp.float32)],
        scratch, [scalar], [by_half, proj_weight], 1, 12, (0,),
    )
    received = [lax.ppermute(away, "col", SWAP) for away in (upper, lower)]
    turns = [lax.rem(turn + row, halves) * tile_u for turn in range(halves)]
    if lines % 16:
        received = jnp.concatenate(received).astype(jnp.float32)
        summed = (home + received).astype(jnp.bfloat16)
        by_u = summed.reshape(lines, half_line, channels).transpose(1, 0, 2)
        blocks = [lax.dynamic_slice_in_dim(by_u, turn, tile_u) for turn in turns]
    else:
        blocks = call(
            functools.partial(combine_kernel, half_line),
            "combine",
            [jax.ShapeDtypeStruct((tile_u, lines, channels), jnp.bfloat16)] * halves,
            [pltpu.VMEM((channels // LANES, *size[:1], LANES), jnp.float32)],
            [jnp.stack(turns).astype(jnp.int32)],
            [home, *received],
            1,
            8,
        )
    pieces, places = [], []
    for turn in range(halves):
        pairs = []
        for r in range(row_count):
            for c in range(2):
                goal = (halves * c + (turn + r) % halves) * 2 + r // halves
                pairs.append((r * 2 + c, goal))
        pieces.append(lax.ppermute(blocks[turn], ("row", "col"), pairs))
        places.append(lax.rem(row + (halves - turn), halves) * lines)
    places = jnp.stack(places).astype(jnp.int32)
    if lines % 16:
        whole = jnp.zeros((tile_u, tile_v, channels), jnp.bfloat16)
        for index, piece in enumerate(pieces):
            whole = lax.dynamic_update_slice_in_dim(whole, piece, places[index], axis=1)
        return [whole], jnp.zeros((1,), jnp.int32), blocks[0]
    return pieces, places, blocks[0]


def on_device(
    teacher,
    proj_weight,
    student,
    dw_kernel,
    dw_bias,
    norm_gain,
    norm_bias,
    w_in,
    b_in,
    w_out,
    b_out,
    layer_scale,
):
    core = lax.axis_index("col")
    row = lax.axis_index("row")
    tile_v, tile_u, channels = student.shape
    hidden = w_in.shape[1]
    tiles = channels // LANES
    wide = tile_v + 2 * EDGE
    scalar = core.astype(jnp.int32)[None]
    f32, bf16 = jnp.float32, jnp.bfloat16
    rows = tile_u * tile_v
    own_edge = jnp.where(core == 0, student[-EDGE:], student[:EDGE])
    edge = lax.ppermute(own_edge, "col", SWAP).transpose(1, 0, 2)
    after_edge, _ = lax.optimization_barrier((student, own_edge))
    middle = after_edge.transpose(1, 0, 2)
    last, first = with_edge(middle, edge)
    left, right = send_sides(last, first)
    held, _, _ = lax.optimization_barrier((proj_weight, last, first))
    targets, places, block = find_target(teacher, held, core, row, tile_u, tile_v)
    later, _ = lax.optimization_barrier((dw_bias, block))
    matmul = 2 * rows * channels * hidden
    flat = jax.ShapeDtypeStruct((rows, channels), f32)
    taps = pltpu.VMEM((TAPS * TAPS, tiles, SUBLANES, LANES), f32)
    own_pad, side_pad = (
        pltpu.VMEM((tiles, count, tile_v + 2 * EDGE, LANES), f32) for count in (tile_u, 2 * REACH)
    )
    (inner,) = call(
        functools.partial(inner_kernel, False),
        "inner_up", [flat], [own_pad, taps], [scalar],
        [middle, edge, dw_kernel, later[None]], 1, 8,
    )
    saved = call(
        up_kernel,
        "up",
        [
            flat,
            jax.ShapeDtypeStruct((rows, LANES), f32),
            jax.ShapeDtypeStruct((rows, hidden), bf16),
            jax.ShapeDtypeStruct((rows, hidden), f32),
        ],
        [side_pad, taps, pltpu.VMEM((rows, channels), bf16), pltpu.VMEM(w_in.shape, bf16)]
        + [pltpu.SemaphoreType.DMA],
        [scalar],
        [left, right, dw_kernel, inner, norm_gain[None], norm_bias[None], w_in, b_in[None]],
        4 * matmul,
        16,
        (6,),
    )
    mismatch, d_conv = call(
        functools.partial(back_kernel, len(targets)),
        "back",
        [flat, jax.ShapeDtypeStruct((tile_u, tile_v, channels), bf16)],
        [
            pltpu.VMEM((tile_u, tile_v, channels), bf16),
            pltpu.VMEM((rows, channels), bf16),
            pltpu.VMEM((rows, hidden), bf16),
            pltpu.VMEM((rows, channels), f32),
        ],
        [places],
        [middle, *saved, norm_gain[None], w_in, w_out, b_out[None], layer_scale[None], *targets],
        4 * matmul,
        16,
    )
    left, right = send_sides(d_conv[-REACH:], d_conv[:REACH])
    left_edge, edge, right_edge = send_edges(d_conv, core)
    (inner,) = call(
        functools.partial(inner_kernel, True),
        "inner_last", [flat], [own_pad, taps], [scalar],
        [d_conv, edge, dw_kernel, mismatch], matmul, 8,
    )
    (grad,) = call(
        last_kernel,
        "last",
        [jax.ShapeDtypeStruct((tile_v, tile_u, channels), f32)],
        [side_pad, taps, pltpu.VMEM((tiles, rows, LANES), f32)],
        [scalar],
        [left, right, left_edge, right_edge, dw_kernel, inner],
        matmul,
        8,
    )
    return grad


def solution(mesh):
    placed = (
        P(("groups", "row"), "col"),
        P("col", None),
        P(("groups", "col"), "row", None),
        P(),
        P(),
        P(),
        P(),
        P(),
        P(),
        P(),
        P(),
        P(),
    )
    return jax.shard_map(
        on_device,
        mesh=mesh,
        in_specs=placed,
        out_specs=P(("groups", "col"), "row", None),
        check_vma=False,
    )
```

```python
import functools

import jax
import jax.numpy as jnp
from jax import lax
from jax.experimental import pallas as pl
from jax.experimental.pallas import tpu as pltpu
from jax.sharding import PartitionSpec as P

NORM_EPSILON = 1e-06
REACH = 3
TAPS = 2 * REACH + 1
LANES = 128
SUBLANES = 8
EDGE = 8
CHUNK = 16
UNROLL = 16
COPIES = 2
MLP_TILE = 512
CONTRACT_LAST = (((1,), (1,)), ((), ()))
SWAP = [(0, 1), (1, 0)]


def aligned(start, size):
    return pl.ds(pl.multiple_of(start, size), size)


def lane_tile(tile):
    return slice(tile * LANES, (tile + 1) * LANES)


def project_kernel(other, core_ref, teacher_hbm, weight, *rest):
    *outs, rows, sems = rest
    half = 1 - core_ref[0] if other else core_ref[0]
    lines, wide, depth = rows.shape
    copies = []
    for index in range(COPIES):
        here = pl.ds(index * (lines // COPIES), lines // COPIES)
        copy = pltpu.make_async_copy(
            teacher_hbm.at[here, half], rows.at[here], sems.at[index]
        )
        copy.start()
        copies.append(copy)
    size = lines * wide // COPIES
    for index, copy in enumerate(copies):
        copy.wait()
        here = pl.ds(index * (lines // COPIES), lines // COPIES)
        product = jnp.dot(
            rows[here].reshape(size, depth), weight[...], preferred_element_type=jnp.float32
        )
        out = outs[index * len(outs) // COPIES]
        start = index * size % out.shape[0]
        out[start : start + size] = product.astype(out.dtype)


def combine_kernel(wide, turns_ref, home, upper, lower, *rest):
    *blocks, summed = rest
    half = upper.shape[0]
    for tile in range(summed.shape[0]):
        lanes = lane_tile(tile)
        for start, received in ((0, upper), (half, lower)):
            here = slice(start, start + half)
            summed[tile, here] = home[here, lanes] + received[:, lanes].astype(jnp.float32)
    for index, block in enumerate(blocks):
        tile_u, lines, _ = block.shape
        for u in range(tile_u):
            rows = pl.ds(turns_ref[index] + u, lines, stride=wide)
            for tile in range(summed.shape[0]):
                block[u, :, lane_tile(tile)] = summed[tile, rows, :].astype(jnp.bfloat16)


def spread_taps(taps, kernel):
    for row_tap in range(TAPS):
        for col_tap in range(TAPS):
            for tile in range(taps.shape[1]):
                line = kernel[row_tap, col_tap : col_tap + 1, lane_tile(tile)]
                taps[row_tap * TAPS + col_tap, tile] = jnp.broadcast_to(line, (SUBLANES, LANES))


def spread(padded, place, part, source, start, row, count):
    for tile in range(padded.shape[0]):
        padded[tile, place, pl.ds(row, count), :] = part[
            source, pl.ds(start, count), lane_tile(tile)
        ].astype(jnp.float32)


def depthwise(padded, taps, begin, store, tile_u, count, offset, sources, flip):
    tiles = padded.shape[0]
    blocks = count // (2 * SUBLANES)

    def step(index, carry):
        tile = index // blocks
        base = pl.multiple_of((index % blocks) * (2 * SUBLANES), 2 * SUBLANES)
        sums = [
            [begin(tile, u, base + half * SUBLANES) for u in range(tile_u)] for half in range(2)
        ]
        for row_tap in range(TAPS):
            weights = []
            for col_tap in range(TAPS):
                tap = row_tap * TAPS + col_tap
                weights.append(taps[TAPS * TAPS - 1 - tap if flip else tap, tile])
            for place, source in enumerate(sources):
                for half in range(2):
                    row = base + (half * SUBLANES + row_tap) + offset
                    values = padded[tile, place, pl.ds(row, SUBLANES), :]
                    for u in range(max(0, source - TAPS + 1), min(tile_u, source + 1)):
                        term = weights[source - u] * values
                        sums[half][u] = term if sums[half][u] is None else sums[half][u] + term
        for half in range(2):
            for u in range(tile_u):
                store(tile, u, base + half * SUBLANES, sums[half][u])
        return carry

    lax.fori_loop(0, tiles * blocks, step, 0)


def row_parts(rows):
    half = rows // 2 // 16 * 16
    return slice(0, half), slice(half, rows)


def repeat(count, step):
    unroll = max(n for n in range(1, UNROLL + 1) if count % n == 0)

    def body(index, carry):
        step(index)
        return carry

    lax.fori_loop(0, count, body, 0, unroll=unroll)


def fill(padded, parts, core, tile_v):
    place = 0
    for part, edge, start in parts:
        for u in range(part.shape[0]):
            spread(padded, place, part, u, 0, EDGE, tile_v)
            for tile in range(padded.shape[0]):
                rim = edge[u, start : start + EDGE, lane_tile(tile)].astype(jnp.float32)
                nothing = jnp.zeros_like(rim)
                padded[tile, place, 0:EDGE, :] = jnp.where(core == 1, rim, nothing)
                padded[tile, place, EDGE + tile_v : 2 * EDGE + tile_v, :] = jnp.where(
                    core == 0, rim, nothing
                )
            place += 1


def inner_kernel(flip, core_ref, middle, edge, kernel, base_value, out, padded, taps):
    tile_u, tile_v, channels = middle.shape
    spread_taps(taps, kernel)
    fill(padded, [(middle, edge, 0)], core_ref[0], tile_v)

    def place(tile, u, base):
        return u, aligned(base, SUBLANES), aligned(tile * LANES, LANES)

    def begin(tile, u, base):
        here = place(tile, u, base)
        if len(base_value.shape) == 2:
            return jnp.broadcast_to(base_value[:, here[2]], (SUBLANES, LANES))
        return base_value[here]

    def store(tile, u, base, value):
        out[place(tile, u, base)] = value

    own = range(REACH, REACH + tile_u)
    depthwise(padded, taps, begin, store, tile_u, tile_v, EDGE - REACH, own, flip)


def rim_conv(flip, core, left, right, left_edge, right_edge, kernel, inner, store, padded, taps):
    tile_u, tile_v, _ = inner.shape
    spread_taps(taps, kernel)
    fill(padded, [(left, *left_edge), (right, *right_edge)], core, tile_v)

    def begin(tile, u, base):
        return inner[u, aligned(base, SUBLANES), aligned(tile * LANES, LANES)]

    sources = [*range(REACH), *range(REACH + tile_u, 2 * REACH + tile_u)]
    depthwise(padded, taps, begin, store, tile_u, tile_v, EDGE - REACH, sources, flip)


def up_kernel(
    core_ref, left, right, kernel, inner, gain, shift, w_in_hbm, b_in,
    normal_form, inv_scale, activated, slope, padded, taps, summed, normed, w_in, sem,
):
    copy = pltpu.make_async_copy(w_in_hbm, w_in, sem)
    copy.start()
    rows, hidden = activated.shape
    _, tile_v, _ = inner.shape
    chunks = tile_v // CHUNK

    def store(tile, u, base, value):
        summed[u, aligned(base, SUBLANES), aligned(tile * LANES, LANES)] = value

    left_edge, right_edge = (left, tile_v), (right, tile_v)
    rim_conv(
        False, core_ref[0], left, right, left_edge, right_edge, kernel, inner, store, padded, taps
    )

    def norm_step(index):
        here = aligned(index * CHUNK, CHUNK)
        conv = summed[index // chunks, aligned((index % chunks) * CHUNK, CHUNK), :]
        centred = conv - jnp.mean(conv, axis=-1, keepdims=True)
        variance = jnp.mean(centred * centred, axis=-1, keepdims=True)
        inverse = lax.rsqrt(variance + NORM_EPSILON)
        form = centred * inverse
        normal_form[here, :] = form
        inv_scale[here, :] = jnp.broadcast_to(inverse, (CHUNK, LANES))
        normed[here, :] = (form * gain[...] + shift[...]).astype(jnp.bfloat16)

    repeat(rows // CHUNK, norm_step)

    copy.wait()
    for start in range(0, hidden, MLP_TILE):
        tile = slice(start, start + MLP_TILE)
        for here in row_parts(rows):
            pre = (
                jnp.dot(normed[here, :], w_in[:, tile], preferred_element_type=jnp.float32)
                + b_in[:, tile]
            )
            phi = 0.5 * (1.0 + lax.erf(pre * 0.7071067811865476))
            activated[here, tile] = (pre * phi).astype(jnp.bfloat16)
            rise = phi + pre * jnp.exp(-0.5 * pre * pre) * 0.3989422804014327
            slope[here, tile] = rise.astype(jnp.bfloat16)


def back_kernel(
    pieces, places_ref, middle, normal_form, inv_scale, activated, slope,
    gain, w_in, w_out, b_out, scale, *rest,
):
    targets = rest[:pieces]
    mismatch_out, d_out, target, d_branch, d_hidden, d_normed = rest[pieces:]
    tile_u, tile_v, channels = middle.shape
    rows, hidden = activated.shape
    chunks = tile_v // CHUNK
    for index, piece in enumerate(targets):
        target[:, aligned(places_ref[index], piece.shape[1]), :] = piece[...]

    for here in row_parts(rows):
        d_normed[here, :] = jnp.dot(
            activated[here, :], w_out[...], preferred_element_type=jnp.float32
        )

    def mismatch_step(index):
        u = index // chunks
        inside = aligned((index % chunks) * CHUNK, CHUNK)
        here = aligned(index * CHUNK, CHUNK)
        mismatch = (
            middle[u, inside, :].astype(jnp.float32)
            + scale[...] * (d_normed[here, :] + b_out[...])
            - target[u, inside, :].astype(jnp.float32)
        )
        mismatch_out[u, inside, :] = mismatch
        d_branch[here, :] = (scale[...] * mismatch).astype(jnp.bfloat16)

    repeat(tile_u * chunks, mismatch_step)

    for start in range(0, hidden, MLP_TILE):
        tile = slice(start, start + MLP_TILE)
        for here in row_parts(rows):
            d_activated = lax.dot_general(
                d_branch[here, :], w_out[tile, :], CONTRACT_LAST, preferred_element_type=jnp.float32
            )
            d_hidden[here, tile] = (
                d_activated * slope[here, tile].astype(jnp.float32)
            ).astype(jnp.bfloat16)
    for here in row_parts(rows):
        d_normed[here, :] = lax.dot_general(
            d_hidden[here, :], w_in[...], CONTRACT_LAST, preferred_element_type=jnp.float32
        )

    def d_norm_step(index):
        u = index // chunks
        inside = aligned((index % chunks) * CHUNK, CHUNK)
        here = aligned(index * CHUNK, CHUNK)
        scaled = d_normed[here, :] * gain[...]
        form = normal_form[here, :]
        d_conv = inv_scale[here, :1] * (
            scaled
            - jnp.mean(scaled, axis=-1, keepdims=True)
            - form * jnp.mean(scaled * form, axis=-1, keepdims=True)
        )
        d_out[u, inside, :] = d_conv.astype(jnp.bfloat16)

    repeat(tile_u * chunks, d_norm_step)


def last_kernel(
    core_ref, left, right, left_edge, right_edge, kernel, inner, out, padded, taps, turned
):
    tile_v, tile_u, channels = out.shape

    def store(tile, u, base, value):
        turned[u, aligned(base, SUBLANES), aligned(tile * LANES, LANES)] = value

    edges = (left_edge, 0), (right_edge, 0)
    rim_conv(True, core_ref[0], left, right, *edges, kernel, inner, store, padded, taps)

    for u in range(tile_u):
        out[:, u, :] = turned[u]


def call(kernel, name, outs, scratch, scalars, arrays, flops, limit, left_in_hbm=()):
    vmem = pl.BlockSpec(memory_space=pltpu.VMEM)
    smem = pl.BlockSpec(memory_space=pltpu.SMEM)
    hbm = pl.BlockSpec(memory_space=pltpu.HBM)
    moved = 1 if flops == 1 else sum(a.size * a.dtype.itemsize for a in [*arrays, *outs])
    arrays = [
        pltpu.with_memory_space_constraint(a, pltpu.HBM) if index in left_in_hbm else a
        for index, a in enumerate(arrays)
    ]
    specs = [hbm if index in left_in_hbm else vmem for index in range(len(arrays))]
    return pl.pallas_call(
        kernel,
        out_shape=tuple(outs),
        in_specs=[smem] * len(scalars) + specs,
        out_specs=(vmem,) * len(outs),
        scratch_shapes=scratch,
        compiler_params=pltpu.CompilerParams(vmem_limit_bytes=limit << 20),
        cost_estimate=pl.CostEstimate(flops=flops, bytes_accessed=moved, transcendentals=0),
        name=name,
    )(*scalars, *arrays)


def send_sides(last, first):
    row_count = lax.axis_size("row")
    forward = [(i, i + 1) for i in range(row_count - 1)]
    backward = [(b, a) for a, b in forward]
    return lax.ppermute(last, "row", forward), lax.ppermute(first, "row", backward)


def with_edge(block, edge):
    return (
        jnp.concatenate([block[-REACH:], edge[-REACH:]], axis=1),
        jnp.concatenate([block[:REACH], edge[:REACH]], axis=1),
    )


def send_edges(tile, core):
    row_count = lax.axis_size("row")
    own = jnp.where(core == 0, tile[:, -EDGE:], tile[:, :EDGE])
    forward = [(i * 2 + c, i * 2 + 3 - c) for i in range(row_count - 1) for c in range(2)]
    backward = [(b, a) for a, b in forward]
    return (
        lax.ppermute(own[-REACH:], ("row", "col"), forward),
        lax.ppermute(own, "col", SWAP),
        lax.ppermute(own[:REACH], ("row", "col"), backward),
    )


def find_target(teacher, proj_weight, core, row, tile_u, tile_v):
    row_count = lax.axis_size("row")
    halves = row_count // 2
    channels = proj_weight.shape[1]
    grid_u = tile_u * row_count
    lines = teacher.shape[0] // grid_u
    scalar = core.astype(jnp.int32)[None]
    half_line = grid_u // 2
    by_half = teacher.reshape(lines, 2, half_line, teacher.shape[1])
    size = (lines * half_line, channels)
    fourth = jax.ShapeDtypeStruct((size[0] // 2, channels), jnp.bfloat16)
    scratch = [
        pltpu.VMEM((lines, half_line, teacher.shape[1]), jnp.bfloat16),
        pltpu.SemaphoreType.DMA((COPIES,)),
    ]
    upper, lower = call(
        functools.partial(project_kernel, True),
        "project_away", [fourth] * 2, scratch, [scalar], [by_half, proj_weight], 1, 12, (0,),
    )
    (home,) = call(
        functools.partial(project_kernel, False),
        "project_home", [jax.ShapeDtypeStruct(size, jnp.float32)],
        scratch, [scalar], [by_half, proj_weight], 1, 12, (0,),
    )
    received = [lax.ppermute(away, "col", SWAP) for away in (upper, lower)]
    turns = [lax.rem(turn + row, halves) * tile_u for turn in range(halves)]
    if lines % 16:
        received = jnp.concatenate(received).astype(jnp.float32)
        summed = (home + received).astype(jnp.bfloat16)
        by_u = summed.reshape(lines, half_line, channels).transpose(1, 0, 2)
        blocks = [lax.dynamic_slice_in_dim(by_u, turn, tile_u) for turn in turns]
    else:
        blocks = call(
            functools.partial(combine_kernel, half_line),
            "combine",
            [jax.ShapeDtypeStruct((tile_u, lines, channels), jnp.bfloat16)] * halves,
            [pltpu.VMEM((channels // LANES, *size[:1], LANES), jnp.float32)],
            [jnp.stack(turns).astype(jnp.int32)],
            [home, *received],
            1,
            8,
        )
    pieces, places = [], []
    for turn in range(halves):
        pairs = []
        for r in range(row_count):
            for c in range(2):
                goal = (halves * c + (turn + r) % halves) * 2 + r // halves
                pairs.append((r * 2 + c, goal))
        pieces.append(lax.ppermute(blocks[turn], ("row", "col"), pairs))
        places.append(lax.rem(row + (halves - turn), halves) * lines)
    places = jnp.stack(places).astype(jnp.int32)
    if lines % 16:
        whole = jnp.zeros((tile_u, tile_v, channels), jnp.bfloat16)
        for index, piece in enumerate(pieces):
            whole = lax.dynamic_update_slice_in_dim(whole, piece, places[index], axis=1)
        return [whole], jnp.zeros((1,), jnp.int32), blocks[0]
    return pieces, places, blocks[0]


def on_device(
    teacher,
    proj_weight,
    student,
    dw_kernel,
    dw_bias,
    norm_gain,
    norm_bias,
    w_in,
    b_in,
    w_out,
    b_out,
    layer_scale,
):
    core = lax.axis_index("col")
    row = lax.axis_index("row")
    tile_v, tile_u, channels = student.shape
    hidden = w_in.shape[1]
    tiles = channels // LANES
    wide = tile_v + 2 * EDGE
    scalar = core.astype(jnp.int32)[None]
    f32, bf16 = jnp.float32, jnp.bfloat16
    rows = tile_u * tile_v
    own_edge = jnp.where(core == 0, student[-EDGE:], student[:EDGE])
    edge = lax.ppermute(own_edge, "col", SWAP).transpose(1, 0, 2)
    after_edge, _ = lax.optimization_barrier((student, own_edge))
    middle = after_edge.transpose(1, 0, 2)
    last, first = with_edge(middle, edge)
    left, right = send_sides(last, first)
    held, _, _ = lax.optimization_barrier((proj_weight, last, first))
    targets, places, block = find_target(teacher, held, core, row, tile_u, tile_v)
    later, _ = lax.optimization_barrier((dw_bias, block))
    matmul = 2 * rows * channels * hidden
    whole = (tile_u, tile_v, channels)
    summed = jax.ShapeDtypeStruct(whole, f32)
    taps = pltpu.VMEM((TAPS * TAPS, tiles, SUBLANES, LANES), f32)
    own_pad, side_pad = (
        pltpu.VMEM((tiles, count, tile_v + 2 * EDGE, LANES), f32) for count in (tile_u, 2 * REACH)
    )
    (inner,) = call(
        functools.partial(inner_kernel, False),
        "inner_up", [summed], [own_pad, taps], [scalar],
        [middle, edge, dw_kernel, later[None]], 1, 8,
    )
    saved = call(
        up_kernel,
        "up",
        [
            jax.ShapeDtypeStruct((rows, channels), f32),
            jax.ShapeDtypeStruct((rows, LANES), f32),
            jax.ShapeDtypeStruct((rows, hidden), bf16),
            jax.ShapeDtypeStruct((rows, hidden), bf16),
        ],
        [side_pad, taps, pltpu.VMEM(whole, f32), pltpu.VMEM((rows, channels), bf16)]
        + [pltpu.VMEM(w_in.shape, bf16), pltpu.SemaphoreType.DMA],
        [scalar],
        [left, right, dw_kernel, inner, norm_gain[None], norm_bias[None], w_in, b_in[None]],
        4 * matmul,
        16,
        (6,),
    )
    mismatch, d_conv = call(
        functools.partial(back_kernel, len(targets)),
        "back",
        [summed, jax.ShapeDtypeStruct(whole, bf16)],
        [
            pltpu.VMEM(whole, bf16),
            pltpu.VMEM((rows, channels), bf16),
            pltpu.VMEM((rows, hidden), bf16),
            pltpu.VMEM((rows, channels), f32),
        ],
        [places],
        [middle, *saved, norm_gain[None], w_in, w_out, b_out[None], layer_scale[None], *targets],
        4 * matmul,
        16,
    )
    left, right = send_sides(d_conv[-REACH:], d_conv[:REACH])
    left_edge, edge, right_edge = send_edges(d_conv, core)
    (inner,) = call(
        functools.partial(inner_kernel, True),
        "inner_last", [summed], [own_pad, taps], [scalar],
        [d_conv, edge, dw_kernel, mismatch], matmul, 8,
    )
    (grad,) = call(
        last_kernel,
        "last",
        [jax.ShapeDtypeStruct((tile_v, tile_u, channels), f32)],
        [side_pad, taps, pltpu.VMEM(whole, f32)],
        [scalar],
        [left, right, left_edge, right_edge, dw_kernel, inner],
        matmul,
        8,
    )
    return grad


def solution(mesh):
    placed = (
        P(("groups", "row"), "col"),
        P("col", None),
        P(("groups", "col"), "row", None),
        P(),
        P(),
        P(),
        P(),
        P(),
        P(),
        P(),
        P(),
        P(),
    )
    return jax.shard_map(
        on_device,
        mesh=mesh,
        in_specs=placed,
        out_specs=P(("groups", "col"), "row", None),
        check_vma=False,
    )
```

```python
import functools

import jax
import jax.numpy as jnp
from jax import lax
from jax.experimental import pallas as pl
from jax.experimental.pallas import tpu as pltpu
from jax.sharding import PartitionSpec as P

NORM_EPSILON = 1e-06
REACH = 3
TAPS = 2 * REACH + 1
LANES = 128
SUBLANES = 8
EDGE = 8
CHUNK = 16
UNROLL = 16
COPIES = 8
DOTS = 2
MLP_TILE = 512
CONTRACT_LAST = (((1,), (1,)), ((), ()))
SWAP = [(0, 1), (1, 0)]


def aligned(start, size):
    return pl.ds(pl.multiple_of(start, size), size)


def lane_tile(tile):
    return slice(tile * LANES, (tile + 1) * LANES)


def project_kernel(other, core_ref, teacher_hbm, weight, *rest):
    *outs, rows, sems = rest
    half = 1 - core_ref[0] if other else core_ref[0]
    lines, wide, depth = rows.shape
    count = next(n for n in (COPIES, 4, 2) if lines % n == 0)
    copies = []
    for index in range(count):
        here = pl.ds(index * (lines // count), lines // count)
        copy = pltpu.make_async_copy(teacher_hbm.at[here, half], rows.at[here], sems.at[index])
        copy.start()
        copies.append(copy)
    size = lines * wide // DOTS
    for index in range(DOTS):
        for copy in copies[index * count // DOTS : (index + 1) * count // DOTS]:
            copy.wait()
        here = pl.ds(index * (lines // DOTS), lines // DOTS)
        product = jnp.dot(
            rows[here].reshape(size, depth), weight[...], preferred_element_type=jnp.float32
        )
        out = outs[index * len(outs) // DOTS]
        start = index * size % out.shape[0]
        out[start : start + size] = product.astype(out.dtype)


def combine_kernel(wide, turns_ref, home, upper, lower, *rest):
    *blocks, summed = rest
    half = upper.shape[0]
    for tile in range(summed.shape[0]):
        lanes = lane_tile(tile)
        for start, received in ((0, upper), (half, lower)):
            here = slice(start, start + half)
            summed[tile, here] = home[here, lanes] + received[:, lanes].astype(jnp.float32)
    for index, block in enumerate(blocks):
        tile_u, lines, _ = block.shape
        for u in range(tile_u):
            rows = pl.ds(turns_ref[index] + u, lines, stride=wide)
            for tile in range(summed.shape[0]):
                block[u, :, lane_tile(tile)] = summed[tile, rows, :].astype(jnp.bfloat16)


def spread_taps(taps, kernel):
    for row_tap in range(TAPS):
        for col_tap in range(TAPS):
            for tile in range(taps.shape[1]):
                line = kernel[row_tap, col_tap : col_tap + 1, lane_tile(tile)]
                taps[row_tap * TAPS + col_tap, tile] = jnp.broadcast_to(line, (SUBLANES, LANES))


def spread(padded, place, part, source, start, row, count):
    for tile in range(padded.shape[0]):
        padded[tile, place, pl.ds(row, count), :] = part[
            source, pl.ds(start, count), lane_tile(tile)
        ].astype(jnp.float32)


def depthwise(padded, taps, begin, store, tile_u, count, offset, sources, flip):
    tiles = padded.shape[0]
    blocks = count // (2 * SUBLANES)

    def step(index, carry):
        tile = index // blocks
        base = pl.multiple_of((index % blocks) * (2 * SUBLANES), 2 * SUBLANES)
        sums = [
            [begin(tile, u, base + half * SUBLANES) for u in range(tile_u)] for half in range(2)
        ]
        for row_tap in range(TAPS):
            weights = []
            for col_tap in range(TAPS):
                tap = row_tap * TAPS + col_tap
                weights.append(taps[TAPS * TAPS - 1 - tap if flip else tap, tile])
            for place, source in enumerate(sources):
                for half in range(2):
                    row = base + (half * SUBLANES + row_tap) + offset
                    values = padded[tile, place, pl.ds(row, SUBLANES), :]
                    for u in range(max(0, source - TAPS + 1), min(tile_u, source + 1)):
                        term = weights[source - u] * values
                        sums[half][u] = term if sums[half][u] is None else sums[half][u] + term
        for half in range(2):
            for u in range(tile_u):
                store(tile, u, base + half * SUBLANES, sums[half][u])
        return carry

    lax.fori_loop(0, tiles * blocks, step, 0)


def row_parts(rows):
    half = rows // 2 // 16 * 16
    return slice(0, half), slice(half, rows)


def repeat(count, step):
    unroll = max(n for n in range(1, UNROLL + 1) if count % n == 0)

    def body(index, carry):
        step(index)
        return carry

    lax.fori_loop(0, count, body, 0, unroll=unroll)


def fill(padded, parts, core, tile_v):
    place = 0
    for part, edge, start in parts:
        for u in range(part.shape[0]):
            spread(padded, place, part, u, 0, EDGE, tile_v)
            for tile in range(padded.shape[0]):
                rim = edge[u, start : start + EDGE, lane_tile(tile)].astype(jnp.float32)
                nothing = jnp.zeros_like(rim)
                padded[tile, place, 0:EDGE, :] = jnp.where(core == 1, rim, nothing)
                padded[tile, place, EDGE + tile_v : 2 * EDGE + tile_v, :] = jnp.where(
                    core == 0, rim, nothing
                )
            place += 1


def inner_kernel(flip, core_ref, middle, edge, kernel, base_value, out, padded, taps):
    tile_u, tile_v, channels = middle.shape
    spread_taps(taps, kernel)
    fill(padded, [(middle, edge, 0)], core_ref[0], tile_v)

    def place(tile, u, base):
        return u, aligned(base, SUBLANES), aligned(tile * LANES, LANES)

    def begin(tile, u, base):
        here = place(tile, u, base)
        if len(base_value.shape) == 2:
            return jnp.broadcast_to(base_value[:, here[2]], (SUBLANES, LANES))
        return base_value[here]

    def store(tile, u, base, value):
        out[place(tile, u, base)] = value

    own = range(REACH, REACH + tile_u)
    depthwise(padded, taps, begin, store, tile_u, tile_v, EDGE - REACH, own, flip)


def side_conv(flip, core, on_left, side, edge, kernel, inner, store, padded, taps):
    tile_u, tile_v, _ = inner.shape
    spread_taps(taps, kernel)
    fill(padded, [(side, *edge)], core, tile_v)

    def begin(tile, u, base):
        return inner[u, aligned(base, SUBLANES), aligned(tile * LANES, LANES)]

    for is_left, first in ((True, 0), (False, REACH + tile_u)):
        sources = range(first, first + REACH)

        @pl.when(on_left == is_left)
        def _(sources=sources):
            depthwise(padded, taps, begin, store, tile_u, tile_v, EDGE - REACH, sources, flip)


def side_kernel(flip, place_ref, side, edge, kernel, inner, out, padded, taps):
    tile_v = inner.shape[1]

    def store(tile, u, base, value):
        out[u, aligned(base, SUBLANES), aligned(tile * LANES, LANES)] = value

    start = edge.shape[1] - EDGE
    side_conv(
        flip, place_ref[0], place_ref[1] == 0, side, (edge, start), kernel, inner, store, padded, taps
    )


def up_kernel(
    place_ref, side, kernel, inner, gain, shift, w_in_hbm, b_in,
    normal_form, inv_scale, activated, slope, padded, taps, summed, normed, w_in, sem,
):
    copy = pltpu.make_async_copy(w_in_hbm, w_in, sem)
    copy.start()
    rows, hidden = activated.shape
    _, tile_v, _ = inner.shape
    chunks = tile_v // CHUNK

    def store(tile, u, base, value):
        summed[u, aligned(base, SUBLANES), aligned(tile * LANES, LANES)] = value

    side_conv(
        False, place_ref[0], place_ref[1] == 1, side, (side, tile_v), kernel, inner, store, padded, taps
    )

    def norm_step(index):
        here = aligned(index * CHUNK, CHUNK)
        conv = summed[index // chunks, aligned((index % chunks) * CHUNK, CHUNK), :]
        centred = conv - jnp.mean(conv, axis=-1, keepdims=True)
        variance = jnp.mean(centred * centred, axis=-1, keepdims=True)
        inverse = lax.rsqrt(variance + NORM_EPSILON)
        form = centred * inverse
        normal_form[here, :] = form
        inv_scale[here, :] = jnp.broadcast_to(inverse, (CHUNK, LANES))
        normed[here, :] = (form * gain[...] + shift[...]).astype(jnp.bfloat16)

    repeat(rows // CHUNK, norm_step)

    copy.wait()
    for start in range(0, hidden, MLP_TILE):
        tile = slice(start, start + MLP_TILE)
        for here in row_parts(rows):
            pre = (
                jnp.dot(normed[here, :], w_in[:, tile], preferred_element_type=jnp.float32)
                + b_in[:, tile]
            )
            phi = 0.5 * (1.0 + lax.erf(pre * 0.7071067811865476))
            activated[here, tile] = (pre * phi).astype(jnp.bfloat16)
            rise = phi + pre * jnp.exp(-0.5 * pre * pre) * 0.3989422804014327
            slope[here, tile] = rise.astype(jnp.bfloat16)


def back_kernel(
    pieces, places_ref, middle, normal_form, inv_scale, activated, slope,
    gain, w_in, w_out, b_out, scale, *rest,
):
    targets = rest[:pieces]
    mismatch_out, d_out, target, d_branch, d_hidden, d_normed = rest[pieces:]
    tile_u, tile_v, channels = middle.shape
    rows, hidden = activated.shape
    chunks = tile_v // CHUNK
    for index, piece in enumerate(targets):
        target[:, aligned(places_ref[index], piece.shape[1]), :] = piece[...]

    for here in row_parts(rows):
        d_normed[here, :] = jnp.dot(
            activated[here, :], w_out[...], preferred_element_type=jnp.float32
        )

    def mismatch_step(index):
        u = index // chunks
        inside = aligned((index % chunks) * CHUNK, CHUNK)
        here = aligned(index * CHUNK, CHUNK)
        mismatch = (
            middle[u, inside, :].astype(jnp.float32)
            + scale[...] * (d_normed[here, :] + b_out[...])
            - target[u, inside, :].astype(jnp.float32)
        )
        mismatch_out[u, inside, :] = mismatch
        d_branch[here, :] = (scale[...] * mismatch).astype(jnp.bfloat16)

    repeat(tile_u * chunks, mismatch_step)

    for start in range(0, hidden, MLP_TILE):
        tile = slice(start, start + MLP_TILE)
        for here in row_parts(rows):
            d_activated = lax.dot_general(
                d_branch[here, :], w_out[tile, :], CONTRACT_LAST, preferred_element_type=jnp.float32
            )
            d_hidden[here, tile] = (
                d_activated * slope[here, tile].astype(jnp.float32)
            ).astype(jnp.bfloat16)
    for here in row_parts(rows):
        d_normed[here, :] = lax.dot_general(
            d_hidden[here, :], w_in[...], CONTRACT_LAST, preferred_element_type=jnp.float32
        )

    def d_norm_step(index):
        u = index // chunks
        inside = aligned((index % chunks) * CHUNK, CHUNK)
        here = aligned(index * CHUNK, CHUNK)
        scaled = d_normed[here, :] * gain[...]
        form = normal_form[here, :]
        d_conv = inv_scale[here, :1] * (
            scaled
            - jnp.mean(scaled, axis=-1, keepdims=True)
            - form * jnp.mean(scaled * form, axis=-1, keepdims=True)
        )
        d_out[u, inside, :] = d_conv.astype(jnp.bfloat16)

    repeat(tile_u * chunks, d_norm_step)


def last_kernel(place_ref, side, edge, kernel, inner, out, padded, taps, turned):
    tile_v, tile_u, channels = out.shape

    def store(tile, u, base, value):
        turned[u, aligned(base, SUBLANES), aligned(tile * LANES, LANES)] = value

    side_conv(
        True, place_ref[0], place_ref[1] == 1, side, (edge, 0), kernel, inner, store, padded, taps
    )
    for u in range(tile_u):
        out[:, u, :] = turned[u]


def call(kernel, name, outs, scratch, scalars, arrays, flops, limit, left_in_hbm=()):
    vmem = pl.BlockSpec(memory_space=pltpu.VMEM)
    smem = pl.BlockSpec(memory_space=pltpu.SMEM)
    hbm = pl.BlockSpec(memory_space=pltpu.HBM)
    moved = 1 if flops == 1 else sum(a.size * a.dtype.itemsize for a in [*arrays, *outs])
    arrays = [
        pltpu.with_memory_space_constraint(a, pltpu.HBM) if index in left_in_hbm else a
        for index, a in enumerate(arrays)
    ]
    specs = [hbm if index in left_in_hbm else vmem for index in range(len(arrays))]
    return pl.pallas_call(
        kernel,
        out_shape=tuple(outs),
        in_specs=[smem] * len(scalars) + specs,
        out_specs=(vmem,) * len(outs),
        scratch_shapes=scratch,
        compiler_params=pltpu.CompilerParams(vmem_limit_bytes=limit << 20),
        cost_estimate=pl.CostEstimate(flops=flops, bytes_accessed=moved, transcendentals=0),
        name=name,
    )(*scalars, *arrays)


def row_pairs(odd):
    row_count = lax.axis_size("row")
    lower = range(1 if odd else 0, row_count - 1, 2)
    return [pair for r in lower for pair in ((r, r + 1), (r + 1, r))]


def facing(tile, row, odd):
    to_right = (row % 2 == 1) if odd else (row % 2 == 0)
    return lax.dynamic_slice_in_dim(
        tile, jnp.where(to_right, tile.shape[0] - REACH, 0), REACH
    )


def edge_lines(tile, core):
    return lax.dynamic_slice_in_dim(
        tile, jnp.where(core == 0, tile.shape[1] - EDGE, 0), EDGE, axis=1
    )


def find_target(teacher, proj_weight, core, row, tile_u, tile_v):
    row_count = lax.axis_size("row")
    halves = row_count // 2
    channels = proj_weight.shape[1]
    grid_u = tile_u * row_count
    lines = teacher.shape[0] // grid_u
    scalar = core.astype(jnp.int32)[None]
    half_line = grid_u // 2
    by_half = teacher.reshape(lines, 2, half_line, teacher.shape[1])
    size = (lines * half_line, channels)
    fourth = jax.ShapeDtypeStruct((size[0] // 2, channels), jnp.bfloat16)
    scratch = [
        pltpu.VMEM((lines, half_line, teacher.shape[1]), jnp.bfloat16),
        pltpu.SemaphoreType.DMA((COPIES,)),
    ]
    upper, lower = call(
        functools.partial(project_kernel, True),
        "project_away", [fourth] * 2, scratch, [scalar], [by_half, proj_weight], 1, 12, (0,),
    )
    (home,) = call(
        functools.partial(project_kernel, False),
        "project_home", [jax.ShapeDtypeStruct(size, jnp.float32)],
        scratch, [scalar], [by_half, proj_weight], 1, 12, (0,),
    )
    received = [lax.ppermute(away, "col", SWAP) for away in (upper, lower)]
    turns = [lax.rem(turn + row, halves) * tile_u for turn in range(halves)]
    if lines % 16:
        received = jnp.concatenate(received).astype(jnp.float32)
        summed = (home + received).astype(jnp.bfloat16)
        by_u = summed.reshape(lines, half_line, channels).transpose(1, 0, 2)
        blocks = [lax.dynamic_slice_in_dim(by_u, turn, tile_u) for turn in turns]
    else:
        blocks = call(
            functools.partial(combine_kernel, half_line),
            "combine",
            [jax.ShapeDtypeStruct((tile_u, lines, channels), jnp.bfloat16)] * halves,
            [pltpu.VMEM((channels // LANES, *size[:1], LANES), jnp.float32)],
            [jnp.stack(turns).astype(jnp.int32)],
            [home, *received],
            1,
            8,
        )
    pieces, places = [], []
    for turn in range(halves):
        pairs = []
        for r in range(row_count):
            for c in range(2):
                goal = (halves * c + (turn + r) % halves) * 2 + r // halves
                pairs.append((r * 2 + c, goal))
        pieces.append(lax.ppermute(blocks[turn], ("row", "col"), pairs))
        places.append(lax.rem(row + (halves - turn), halves) * lines)
    places = jnp.stack(places).astype(jnp.int32)
    if lines % 16:
        whole = jnp.zeros((tile_u, tile_v, channels), jnp.bfloat16)
        for index, piece in enumerate(pieces):
            whole = lax.dynamic_update_slice_in_dim(whole, piece, places[index], axis=1)
        return [whole], jnp.zeros((1,), jnp.int32), blocks[0]
    return pieces, places, blocks[0]


def on_device(
    teacher,
    proj_weight,
    student,
    dw_kernel,
    dw_bias,
    norm_gain,
    norm_bias,
    w_in,
    b_in,
    w_out,
    b_out,
    layer_scale,
):
    core = lax.axis_index("col")
    row = lax.axis_index("row")
    tile_v, tile_u, channels = student.shape
    hidden = w_in.shape[1]
    tiles = channels // LANES
    wide = tile_v + 2 * EDGE
    scalar = core.astype(jnp.int32)[None]
    f32, bf16 = jnp.float32, jnp.bfloat16
    rows = tile_u * tile_v
    own_edge = jnp.where(core == 0, student[-EDGE:], student[:EDGE])
    edge = lax.ppermute(own_edge, "col", SWAP).transpose(1, 0, 2)
    after_edge, _ = lax.optimization_barrier((student, own_edge))
    middle = after_edge.transpose(1, 0, 2)
    blocks = []
    for odd in (True, False):
        pieces = [facing(middle, row, odd), facing(edge, row, odd)]
        blocks.append(jnp.concatenate(pieces, axis=1))
    first_side = lax.ppermute(blocks[0], "row", row_pairs(True))
    second_side = lax.ppermute(blocks[1], "row", row_pairs(False))
    held, *_ = lax.optimization_barrier((proj_weight, *blocks))
    targets, places, block = find_target(teacher, held, core, row, tile_u, tile_v)
    later, _ = lax.optimization_barrier((dw_bias, block))
    matmul = 2 * rows * channels * hidden
    whole = (tile_u, tile_v, channels)
    summed = jax.ShapeDtypeStruct(whole, f32)
    taps = pltpu.VMEM((TAPS * TAPS, tiles, SUBLANES, LANES), f32)
    own_pad, side_pad = (
        pltpu.VMEM((tiles, count, tile_v + 2 * EDGE, LANES), f32) for count in (tile_u, REACH)
    )
    place = jnp.stack([core, row % 2]).astype(jnp.int32)
    (inner,) = call(
        functools.partial(inner_kernel, False),
        "inner_up", [summed], [own_pad, taps], [scalar],
        [middle, edge, dw_kernel, later[None]], 1, 8,
    )
    (inner,) = call(
        functools.partial(side_kernel, False),
        "side_up", [summed], [side_pad, taps], [place],
        [first_side, first_side, dw_kernel, inner], 1, 8,
    )
    saved = call(
        up_kernel,
        "up",
        [
            jax.ShapeDtypeStruct((rows, channels), f32),
            jax.ShapeDtypeStruct((rows, LANES), f32),
            jax.ShapeDtypeStruct((rows, hidden), bf16),
            jax.ShapeDtypeStruct((rows, hidden), bf16),
        ],
        [side_pad, taps, pltpu.VMEM(whole, f32), pltpu.VMEM((rows, channels), bf16)]
        + [pltpu.VMEM(w_in.shape, bf16), pltpu.SemaphoreType.DMA],
        [place],
        [second_side, dw_kernel, inner, norm_gain[None], norm_bias[None], w_in, b_in[None]],
        4 * matmul,
        16,
        (5,),
    )
    mismatch, d_conv = call(
        functools.partial(back_kernel, len(targets)),
        "back",
        [summed, jax.ShapeDtypeStruct(whole, bf16)],
        [
            pltpu.VMEM(whole, bf16),
            pltpu.VMEM((rows, channels), bf16),
            pltpu.VMEM((rows, hidden), bf16),
            pltpu.VMEM((rows, channels), f32),
        ],
        [places],
        [middle, *saved, norm_gain[None], w_in, w_out, b_out[None], layer_scale[None], *targets],
        4 * matmul,
        16,
    )
    first_side = lax.ppermute(facing(d_conv, row, True), "row", row_pairs(True))
    second_side = lax.ppermute(facing(d_conv, row, False), "row", row_pairs(False))
    own_edge = edge_lines(d_conv, core)
    edge = lax.ppermute(own_edge, "col", SWAP)
    across = [(a * 2 + c, b * 2 + 1 - c) for a, b in row_pairs(False) for c in range(2)]
    second_edge = lax.ppermute(facing(own_edge, row, False), ("row", "col"), across)
    first_edge = lax.ppermute(edge_lines(first_side, core), "col", SWAP)
    (inner,) = call(
        functools.partial(inner_kernel, True),
        "inner_last", [summed], [own_pad, taps], [scalar],
        [d_conv, edge, dw_kernel, mismatch], matmul, 8,
    )
    (inner,) = call(
        functools.partial(side_kernel, True),
        "side_last", [summed], [side_pad, taps], [place],
        [first_side, first_edge, dw_kernel, inner], 1, 8,
    )
    (grad,) = call(
        last_kernel,
        "last",
        [jax.ShapeDtypeStruct((tile_v, tile_u, channels), f32)],
        [side_pad, taps, pltpu.VMEM(whole, f32)],
        [place],
        [second_side, second_edge, dw_kernel, inner],
        1,
        8,
    )
    return grad


def solution(mesh):
    placed = (
        P(("groups", "row"), "col"),
        P("col", None),
        P(("groups", "col"), "row", None),
        P(),
        P(),
        P(),
        P(),
        P(),
        P(),
        P(),
        P(),
        P(),
    )
    return jax.shard_map(
        on_device,
        mesh=mesh,
        in_specs=placed,
        out_specs=P(("groups", "col"), "row", None),
        check_vma=False,
    )
```

```python
import functools

import jax
import jax.numpy as jnp
from jax import lax
from jax.experimental import pallas as pl
from jax.experimental.pallas import tpu as pltpu
from jax.sharding import PartitionSpec as P

NORM_EPSILON = 1e-06
REACH = 3
TAPS = 2 * REACH + 1
LANES = 128
SUBLANES = 8
EDGE = 8
CHUNK = 16
UNROLL = 16
COPIES = 8
DOTS = 2
MLP_TILE = 512
CONTRACT_LAST = (((1,), (1,)), ((), ()))
SWAP = [(0, 1), (1, 0)]


def aligned(start, size):
    return pl.ds(pl.multiple_of(start, size), size)


def lane_tile(tile):
    return slice(tile * LANES, (tile + 1) * LANES)


def project_kernel(other, core_ref, teacher_hbm, weight, *rest):
    *outs, rows, sems = rest
    half = 1 - core_ref[0] if other else core_ref[0]
    lines, wide, depth = rows.shape
    count = next(n for n in (COPIES, 4, 2) if lines % n == 0)
    copies = []
    for index in range(count):
        here = pl.ds(index * (lines // count), lines // count)
        copy = pltpu.make_async_copy(teacher_hbm.at[here, half], rows.at[here], sems.at[index])
        copy.start()
        copies.append(copy)
    size = lines * wide // DOTS
    for index in range(DOTS):
        for copy in copies[index * count // DOTS : (index + 1) * count // DOTS]:
            copy.wait()
        here = pl.ds(index * (lines // DOTS), lines // DOTS)
        product = jnp.dot(
            rows[here].reshape(size, depth), weight[...], preferred_element_type=jnp.float32
        )
        out = outs[index * len(outs) // DOTS]
        start = index * size % out.shape[0]
        out[start : start + size] = product.astype(out.dtype)


def combine_kernel(wide, turns_ref, home, upper, lower, *rest):
    *blocks, summed = rest
    half = upper.shape[0]
    for tile in range(summed.shape[0]):
        lanes = lane_tile(tile)
        for start, received in ((0, upper), (half, lower)):
            here = slice(start, start + half)
            summed[tile, here] = home[here, lanes] + received[:, lanes].astype(jnp.float32)
    for index, block in enumerate(blocks):
        tile_u, lines, _ = block.shape
        for u in range(tile_u):
            rows = pl.ds(turns_ref[index] + u, lines, stride=wide)
            for tile in range(summed.shape[0]):
                block[u, :, lane_tile(tile)] = summed[tile, rows, :].astype(jnp.bfloat16)


def spread_taps(taps, kernel):
    for row_tap in range(TAPS):
        for col_tap in range(TAPS):
            for tile in range(taps.shape[1]):
                line = kernel[row_tap, col_tap : col_tap + 1, lane_tile(tile)]
                taps[row_tap * TAPS + col_tap, tile] = jnp.broadcast_to(line, (SUBLANES, LANES))


def spread(padded, place, part, source, start, row, count):
    for tile in range(padded.shape[0]):
        padded[tile, place, pl.ds(row, count), :] = part[
            source, pl.ds(start, count), lane_tile(tile)
        ].astype(jnp.float32)


def depthwise(padded, taps, begin, store, tile_u, count, offset, sources, flip):
    tiles = padded.shape[0]
    blocks = count // (2 * SUBLANES)

    def step(index, carry):
        tile = index // blocks
        base = pl.multiple_of((index % blocks) * (2 * SUBLANES), 2 * SUBLANES)
        sums = [
            [begin(tile, u, base + half * SUBLANES) for u in range(tile_u)] for half in range(2)
        ]
        for row_tap in range(TAPS):
            weights = []
            for col_tap in range(TAPS):
                tap = row_tap * TAPS + col_tap
                weights.append(taps[TAPS * TAPS - 1 - tap if flip else tap, tile])
            for place, source in enumerate(sources):
                for half in range(2):
                    row = base + (half * SUBLANES + row_tap) + offset
                    values = padded[tile, place, pl.ds(row, SUBLANES), :]
                    for u in range(max(0, source - TAPS + 1), min(tile_u, source + 1)):
                        term = weights[source - u] * values
                        sums[half][u] = term if sums[half][u] is None else sums[half][u] + term
        for half in range(2):
            for u in range(tile_u):
                store(tile, u, base + half * SUBLANES, sums[half][u])
        return carry

    lax.fori_loop(0, tiles * blocks, step, 0)


def row_parts(rows):
    half = rows // 2 // 16 * 16
    return slice(0, half), slice(half, rows)


def repeat(count, step):
    unroll = max(n for n in range(1, UNROLL + 1) if count % n == 0)

    def body(index, carry):
        step(index)
        return carry

    lax.fori_loop(0, count, body, 0, unroll=unroll)


def fill(padded, parts, core, tile_v):
    place = 0
    for part, edge, start in parts:
        for u in range(part.shape[0]):
            spread(padded, place, part, u, 0, EDGE, tile_v)
            for tile in range(padded.shape[0]):
                rim = edge[u, start : start + EDGE, lane_tile(tile)].astype(jnp.float32)
                nothing = jnp.zeros_like(rim)
                padded[tile, place, 0:EDGE, :] = jnp.where(core == 1, rim, nothing)
                padded[tile, place, EDGE + tile_v : 2 * EDGE + tile_v, :] = jnp.where(
                    core == 0, rim, nothing
                )
            place += 1


def inner_kernel(flip, core_ref, middle, edge, kernel, base_value, out, padded, taps, *fetch):
    tile_u, tile_v, channels = middle.shape
    copies = []
    if fetch:
        copies.append(pltpu.make_async_copy(base_value, *fetch))
        copies[0].start()
        base_value = fetch[0]
    spread_taps(taps, kernel)
    fill(padded, [(middle, edge, 0)], core_ref[0], tile_v)

    def place(tile, u, base):
        return u, aligned(base, SUBLANES), aligned(tile * LANES, LANES)

    def begin(tile, u, base):
        here = place(tile, u, base)
        if len(base_value.shape) == 2:
            return jnp.broadcast_to(base_value[:, here[2]], (SUBLANES, LANES))
        return base_value[here]

    def store(tile, u, base, value):
        out[place(tile, u, base)] = value

    for copy in copies:
        copy.wait()
    own = range(REACH, REACH + tile_u)
    depthwise(padded, taps, begin, store, tile_u, tile_v, EDGE - REACH, own, flip)


def side_conv(flip, core, on_left, side, edge, kernel, inner, store, padded, taps):
    tile_u, tile_v, _ = inner.shape
    spread_taps(taps, kernel)
    fill(padded, [(side, *edge)], core, tile_v)

    def begin(tile, u, base):
        return inner[u, aligned(base, SUBLANES), aligned(tile * LANES, LANES)]

    for is_left, first in ((True, 0), (False, REACH + tile_u)):
        sources = range(first, first + REACH)

        @pl.when(on_left == is_left)
        def _(sources=sources):
            depthwise(padded, taps, begin, store, tile_u, tile_v, EDGE - REACH, sources, flip)


def side_kernel(flip, place_ref, side, edge, kernel, inner, out, padded, taps):
    tile_v = inner.shape[1]

    def store(tile, u, base, value):
        out[u, aligned(base, SUBLANES), aligned(tile * LANES, LANES)] = value

    start = edge.shape[1] - EDGE
    side_conv(
        flip, place_ref[0], place_ref[1] == 0, side, (edge, start), kernel, inner, store, padded, taps
    )


def up_kernel(
    place_ref, side, kernel, inner, gain, shift, w_in_hbm, b_in,
    normal_form, inv_scale, activated, slope, padded, taps, summed, normed, w_in, sem,
):
    copy = pltpu.make_async_copy(w_in_hbm, w_in, sem)
    copy.start()
    rows, hidden = activated.shape
    _, tile_v, _ = inner.shape
    chunks = tile_v // CHUNK

    def store(tile, u, base, value):
        summed[u, aligned(base, SUBLANES), aligned(tile * LANES, LANES)] = value

    side_conv(
        False, place_ref[0], place_ref[1] == 1, side, (side, tile_v), kernel, inner, store, padded, taps
    )

    def norm_step(index):
        here = aligned(index * CHUNK, CHUNK)
        conv = summed[index // chunks, aligned((index % chunks) * CHUNK, CHUNK), :]
        centred = conv - jnp.mean(conv, axis=-1, keepdims=True)
        variance = jnp.mean(centred * centred, axis=-1, keepdims=True)
        inverse = lax.rsqrt(variance + NORM_EPSILON)
        form = centred * inverse
        normal_form[here, :] = form
        inv_scale[here, :] = jnp.broadcast_to(inverse, (CHUNK, LANES))
        normed[here, :] = (form * gain[...] + shift[...]).astype(jnp.bfloat16)

    repeat(rows // CHUNK, norm_step)

    copy.wait()
    for start in range(0, hidden, MLP_TILE):
        tile = slice(start, start + MLP_TILE)
        for here in row_parts(rows):
            pre = (
                jnp.dot(normed[here, :], w_in[:, tile], preferred_element_type=jnp.float32)
                + b_in[:, tile]
            )
            phi = 0.5 * (1.0 + lax.erf(pre * 0.7071067811865476))
            activated[here, tile] = (pre * phi).astype(jnp.bfloat16)
            rise = phi + pre * jnp.exp(-0.5 * pre * pre) * 0.3989422804014327
            slope[here, tile] = rise.astype(jnp.bfloat16)


def back_kernel(
    pieces, places_ref, middle, normal_form, inv_scale, activated, slope,
    gain, w_in, w_out, b_out, scale, *rest,
):
    targets = rest[:pieces]
    mismatch_hbm, d_out, mismatch_out, sem, target, d_branch, d_hidden, d_normed = rest[pieces:]
    tile_u, tile_v, channels = middle.shape
    rows, hidden = activated.shape
    chunks = tile_v // CHUNK
    for index, piece in enumerate(targets):
        target[:, aligned(places_ref[index], piece.shape[1]), :] = piece[...]

    for here in row_parts(rows):
        d_normed[here, :] = jnp.dot(
            activated[here, :], w_out[...], preferred_element_type=jnp.float32
        )

    def mismatch_step(index):
        u = index // chunks
        inside = aligned((index % chunks) * CHUNK, CHUNK)
        here = aligned(index * CHUNK, CHUNK)
        mismatch = (
            middle[u, inside, :].astype(jnp.float32)
            + scale[...] * (d_normed[here, :] + b_out[...])
            - target[u, inside, :].astype(jnp.float32)
        )
        mismatch_out[u, inside, :] = mismatch
        d_branch[here, :] = (scale[...] * mismatch).astype(jnp.bfloat16)

    repeat(tile_u * chunks, mismatch_step)
    copy = pltpu.make_async_copy(mismatch_out, mismatch_hbm, sem)
    copy.start()

    for start in range(0, hidden, MLP_TILE):
        tile = slice(start, start + MLP_TILE)
        for here in row_parts(rows):
            d_activated = lax.dot_general(
                d_branch[here, :], w_out[tile, :], CONTRACT_LAST, preferred_element_type=jnp.float32
            )
            d_hidden[here, tile] = (
                d_activated * slope[here, tile].astype(jnp.float32)
            ).astype(jnp.bfloat16)
    for here in row_parts(rows):
        d_normed[here, :] = lax.dot_general(
            d_hidden[here, :], w_in[...], CONTRACT_LAST, preferred_element_type=jnp.float32
        )

    def d_norm_step(index):
        u = index // chunks
        inside = aligned((index % chunks) * CHUNK, CHUNK)
        here = aligned(index * CHUNK, CHUNK)
        scaled = d_normed[here, :] * gain[...]
        form = normal_form[here, :]
        d_conv = inv_scale[here, :1] * (
            scaled
            - jnp.mean(scaled, axis=-1, keepdims=True)
            - form * jnp.mean(scaled * form, axis=-1, keepdims=True)
        )
        d_out[u, inside, :] = d_conv.astype(jnp.bfloat16)

    repeat(tile_u * chunks, d_norm_step)
    copy.wait()


def last_kernel(place_ref, side, edge, kernel, inner, out, padded, taps, turned):
    tile_v, tile_u, channels = out.shape

    def store(tile, u, base, value):
        turned[u, aligned(base, SUBLANES), aligned(tile * LANES, LANES)] = value

    side_conv(
        True, place_ref[0], place_ref[1] == 1, side, (edge, 0), kernel, inner, store, padded, taps
    )
    for u in range(tile_u):
        out[:, u, :] = turned[u]


def call(
    kernel, name, outs, scratch, scalars, arrays, flops, limit, left_in_hbm=(), out_in_hbm=()
):
    vmem = pl.BlockSpec(memory_space=pltpu.VMEM)
    smem = pl.BlockSpec(memory_space=pltpu.SMEM)
    hbm = pl.BlockSpec(memory_space=pltpu.HBM)
    moved = 1 if flops == 1 else sum(a.size * a.dtype.itemsize for a in [*arrays, *outs])
    arrays = [
        pltpu.with_memory_space_constraint(a, pltpu.HBM) if index in left_in_hbm else a
        for index, a in enumerate(arrays)
    ]
    specs = [hbm if index in left_in_hbm else vmem for index in range(len(arrays))]
    return pl.pallas_call(
        kernel,
        out_shape=tuple(outs),
        in_specs=[smem] * len(scalars) + specs,
        out_specs=tuple(hbm if index in out_in_hbm else vmem for index in range(len(outs))),
        scratch_shapes=scratch,
        compiler_params=pltpu.CompilerParams(vmem_limit_bytes=limit << 20),
        cost_estimate=pl.CostEstimate(flops=flops, bytes_accessed=moved, transcendentals=0),
        name=name,
    )(*scalars, *arrays)


def row_pairs(odd):
    row_count = lax.axis_size("row")
    lower = range(1 if odd else 0, row_count - 1, 2)
    return [pair for r in lower for pair in ((r, r + 1), (r + 1, r))]


def facing(tile, row, odd):
    to_right = (row % 2 == 1) if odd else (row % 2 == 0)
    return lax.dynamic_slice_in_dim(
        tile, jnp.where(to_right, tile.shape[0] - REACH, 0), REACH
    )


def edge_lines(tile, core):
    return lax.dynamic_slice_in_dim(
        tile, jnp.where(core == 0, tile.shape[1] - EDGE, 0), EDGE, axis=1
    )


def around(tile, core, row):
    first_side = lax.ppermute(facing(tile, row, True), "row", row_pairs(True))
    second_side = lax.ppermute(facing(tile, row, False), "row", row_pairs(False))
    own_edge = edge_lines(tile, core)
    edge = lax.ppermute(own_edge, "col", SWAP)
    across = [(a * 2 + c, b * 2 + 1 - c) for a, b in row_pairs(False) for c in range(2)]
    second_edge = lax.ppermute(facing(own_edge, row, False), ("row", "col"), across)
    first_edge = lax.ppermute(edge_lines(first_side, core), "col", SWAP)
    return first_side, second_side, edge, first_edge, second_edge


def find_target(teacher, proj_weight, core, row, tile_u, tile_v):
    row_count = lax.axis_size("row")
    halves = row_count // 2
    channels = proj_weight.shape[1]
    grid_u = tile_u * row_count
    lines = teacher.shape[0] // grid_u
    scalar = core.astype(jnp.int32)[None]
    half_line = grid_u // 2
    by_half = teacher.reshape(lines, 2, half_line, teacher.shape[1])
    size = (lines * half_line, channels)
    fourth = jax.ShapeDtypeStruct((size[0] // 2, channels), jnp.bfloat16)
    scratch = [
        pltpu.VMEM((lines, half_line, teacher.shape[1]), jnp.bfloat16),
        pltpu.SemaphoreType.DMA((COPIES,)),
    ]
    upper, lower = call(
        functools.partial(project_kernel, True),
        "project_away", [fourth] * 2, scratch, [scalar], [by_half, proj_weight], 1, 12, (0,),
    )
    (home,) = call(
        functools.partial(project_kernel, False),
        "project_home", [jax.ShapeDtypeStruct(size, jnp.float32)],
        scratch, [scalar], [by_half, proj_weight], 1, 12, (0,),
    )
    received = [lax.ppermute(away, "col", SWAP) for away in (upper, lower)]
    turns = [lax.rem(turn + row, halves) * tile_u for turn in range(halves)]
    if lines % 16:
        received = jnp.concatenate(received).astype(jnp.float32)
        summed = (home + received).astype(jnp.bfloat16)
        by_u = summed.reshape(lines, half_line, channels).transpose(1, 0, 2)
        blocks = [lax.dynamic_slice_in_dim(by_u, turn, tile_u) for turn in turns]
    else:
        blocks = call(
            functools.partial(combine_kernel, half_line),
            "combine",
            [jax.ShapeDtypeStruct((tile_u, lines, channels), jnp.bfloat16)] * halves,
            [pltpu.VMEM((channels // LANES, *size[:1], LANES), jnp.float32)],
            [jnp.stack(turns).astype(jnp.int32)],
            [home, *received],
            1,
            8,
        )
    pieces, places = [], []
    for turn in range(halves):
        pairs = []
        for r in range(row_count):
            for c in range(2):
                goal = (halves * c + (turn + r) % halves) * 2 + r // halves
                pairs.append((r * 2 + c, goal))
        pieces.append(lax.ppermute(blocks[turn], ("row", "col"), pairs))
        places.append(lax.rem(row + (halves - turn), halves) * lines)
    places = jnp.stack(places).astype(jnp.int32)
    if lines % 16:
        whole = jnp.zeros((tile_u, tile_v, channels), jnp.bfloat16)
        for index, piece in enumerate(pieces):
            whole = lax.dynamic_update_slice_in_dim(whole, piece, places[index], axis=1)
        return [whole], jnp.zeros((1,), jnp.int32), blocks[0]
    return pieces, places, blocks[0]


def on_device(
    teacher,
    proj_weight,
    student,
    dw_kernel,
    dw_bias,
    norm_gain,
    norm_bias,
    w_in,
    b_in,
    w_out,
    b_out,
    layer_scale,
):
    core = lax.axis_index("col")
    row = lax.axis_index("row")
    tile_v, tile_u, channels = student.shape
    hidden = w_in.shape[1]
    tiles = channels // LANES
    wide = tile_v + 2 * EDGE
    scalar = core.astype(jnp.int32)[None]
    f32, bf16 = jnp.float32, jnp.bfloat16
    rows = tile_u * tile_v
    middle = student.transpose(1, 0, 2)
    first_block = facing(middle, row, True)
    first_side = lax.ppermute(first_block, "row", row_pairs(True))
    edge = lax.ppermute(edge_lines(middle, core), "col", SWAP)
    second_block = jnp.concatenate(
        [facing(middle, row, False), facing(edge, row, False)], axis=1
    )
    second_side = lax.ppermute(second_block, "row", row_pairs(False))
    held, *_ = lax.optimization_barrier((proj_weight, first_block, second_block))
    targets, places, block = find_target(teacher, held, core, row, tile_u, tile_v)
    later, _ = lax.optimization_barrier((dw_bias, block))
    matmul = 2 * rows * channels * hidden
    whole = (tile_u, tile_v, channels)
    summed = jax.ShapeDtypeStruct(whole, f32)
    taps = pltpu.VMEM((TAPS * TAPS, tiles, SUBLANES, LANES), f32)
    own_pad, side_pad = (
        pltpu.VMEM((tiles, count, tile_v + 2 * EDGE, LANES), f32) for count in (tile_u, REACH)
    )
    place = jnp.stack([core, row % 2]).astype(jnp.int32)
    (inner,) = call(
        functools.partial(inner_kernel, False),
        "inner_up", [summed], [own_pad, taps], [scalar],
        [middle, edge, dw_kernel, later[None]], 1, 8,
    )
    arrived, _ = lax.optimization_barrier((first_side, inner))
    first_edge = lax.ppermute(edge_lines(arrived, core), "col", SWAP)
    (inner,) = call(
        functools.partial(side_kernel, False),
        "side_up", [summed], [side_pad, taps], [place],
        [first_side, first_edge, dw_kernel, inner], 1, 8,
    )
    saved = call(
        up_kernel,
        "up",
        [
            jax.ShapeDtypeStruct((rows, channels), f32),
            jax.ShapeDtypeStruct((rows, LANES), f32),
            jax.ShapeDtypeStruct((rows, hidden), bf16),
            jax.ShapeDtypeStruct((rows, hidden), bf16),
        ],
        [side_pad, taps, pltpu.VMEM(whole, f32), pltpu.VMEM((rows, channels), bf16)]
        + [pltpu.VMEM(w_in.shape, bf16), pltpu.SemaphoreType.DMA],
        [place],
        [second_side, dw_kernel, inner, norm_gain[None], norm_bias[None], w_in, b_in[None]],
        4 * matmul,
        16,
        (5,),
    )
    mismatch, d_conv = call(
        functools.partial(back_kernel, len(targets)),
        "back",
        [summed, jax.ShapeDtypeStruct(whole, bf16)],
        [
            pltpu.VMEM(whole, f32),
            pltpu.SemaphoreType.DMA,
            pltpu.VMEM(whole, bf16),
            pltpu.VMEM((rows, channels), bf16),
            pltpu.VMEM((rows, hidden), bf16),
            pltpu.VMEM((rows, channels), f32),
        ],
        [places],
        [middle, *saved, norm_gain[None], w_in, w_out, b_out[None], layer_scale[None], *targets],
        4 * matmul,
        16,
        out_in_hbm=(0,),
    )
    first_side, second_side, edge, first_edge, second_edge = around(d_conv, core, row)
    (inner,) = call(
        functools.partial(inner_kernel, True),
        "inner_last", [summed],
        [own_pad, taps, pltpu.VMEM(whole, f32), pltpu.SemaphoreType.DMA], [scalar],
        [d_conv, edge, dw_kernel, mismatch], matmul, 8, (3,),
    )
    (inner,) = call(
        functools.partial(side_kernel, True),
        "side_last", [summed], [side_pad, taps], [place],
        [first_side, first_edge, dw_kernel, inner], 1, 8,
    )
    (grad,) = call(
        last_kernel,
        "last",
        [jax.ShapeDtypeStruct((tile_v, tile_u, channels), f32)],
        [side_pad, taps, pltpu.VMEM(whole, f32)],
        [place],
        [second_side, second_edge, dw_kernel, inner],
        1,
        8,
    )
    return grad


def solution(mesh):
    placed = (
        P(("groups", "row"), "col"),
        P("col", None),
        P(("groups", "col"), "row", None),
        P(),
        P(),
        P(),
        P(),
        P(),
        P(),
        P(),
        P(),
        P(),
    )
    return jax.shard_map(
        on_device,
        mesh=mesh,
        in_specs=placed,
        out_specs=P(("groups", "col"), "row", None),
        check_vma=False,
    )
```

```python
import functools

import jax
import jax.numpy as jnp
from jax import lax
from jax.experimental import pallas as pl
from jax.experimental.pallas import tpu as pltpu
from jax.sharding import PartitionSpec as P

NORM_EPSILON = 1e-06
REACH = 3
TAPS = 2 * REACH + 1
LANES = 128
SUBLANES = 8
EDGE = 8
CHUNK = 16
UNROLL = 16
COPIES = 8
DOTS = 2
MLP_TILE = 512
CONTRACT_LAST = (((1,), (1,)), ((), ()))
SWAP = [(0, 1), (1, 0)]


def aligned(start, size):
    return pl.ds(pl.multiple_of(start, size), size)


def lane_tile(tile):
    return slice(tile * LANES, (tile + 1) * LANES)


def project_kernel(other, core_ref, teacher_hbm, weight, *rest):
    *outs, rows, sems = rest
    half = 1 - core_ref[0] if other else core_ref[0]
    lines, wide, depth = rows.shape
    count = next(n for n in (COPIES, 4, 2) if lines % n == 0)
    copies = []
    for index in range(count):
        here = pl.ds(index * (lines // count), lines // count)
        copy = pltpu.make_async_copy(teacher_hbm.at[here, half], rows.at[here], sems.at[index])
        copy.start()
        copies.append(copy)
    size = lines * wide // DOTS
    for index in range(DOTS):
        for copy in copies[index * count // DOTS : (index + 1) * count // DOTS]:
            copy.wait()
        here = pl.ds(index * (lines // DOTS), lines // DOTS)
        product = jnp.dot(
            rows[here].reshape(size, depth), weight[...], preferred_element_type=jnp.float32
        )
        out = outs[index * len(outs) // DOTS]
        start = index * size % out.shape[0]
        out[start : start + size] = product.astype(out.dtype)


def combine_kernel(wide, turns_ref, home, upper, lower, *rest):
    *blocks, summed = rest
    half = upper.shape[0]
    for tile in range(summed.shape[0]):
        lanes = lane_tile(tile)
        for start, received in ((0, upper), (half, lower)):
            here = slice(start, start + half)
            summed[tile, here] = home[here, lanes] + received[:, lanes].astype(jnp.float32)
    for index, block in enumerate(blocks):
        tile_u, lines, _ = block.shape
        for u in range(tile_u):
            rows = pl.ds(turns_ref[index] + u, lines, stride=wide)
            for tile in range(summed.shape[0]):
                block[u, :, lane_tile(tile)] = summed[tile, rows, :].astype(jnp.bfloat16)


def spread_taps(taps, kernel):
    for row_tap in range(TAPS):
        for col_tap in range(TAPS):
            for tile in range(taps.shape[1]):
                line = kernel[row_tap, col_tap : col_tap + 1, lane_tile(tile)]
                taps[row_tap * TAPS + col_tap, tile] = jnp.broadcast_to(line, (SUBLANES, LANES))


def spread(padded, place, part, source, start, row, count):
    for tile in range(padded.shape[0]):
        padded[tile, place, pl.ds(row, count), :] = part[
            source, pl.ds(start, count), lane_tile(tile)
        ].astype(jnp.float32)


def depthwise(padded, taps, begin, store, tile_u, count, offset, sources, flip):
    tiles = padded.shape[0]
    blocks = count // (2 * SUBLANES)

    def step(index, carry):
        tile = index // blocks
        base = pl.multiple_of((index % blocks) * (2 * SUBLANES), 2 * SUBLANES)
        sums = [
            [begin(tile, u, base + half * SUBLANES) for u in range(tile_u)] for half in range(2)
        ]
        for row_tap in range(TAPS):
            weights = []
            for col_tap in range(TAPS):
                tap = row_tap * TAPS + col_tap
                weights.append(taps[TAPS * TAPS - 1 - tap if flip else tap, tile])
            for place, source in enumerate(sources):
                for half in range(2):
                    row = base + (half * SUBLANES + row_tap) + offset
                    values = padded[tile, place, pl.ds(row, SUBLANES), :]
                    for u in range(max(0, source - TAPS + 1), min(tile_u, source + 1)):
                        term = weights[source - u] * values
                        sums[half][u] = term if sums[half][u] is None else sums[half][u] + term
        for half in range(2):
            for u in range(tile_u):
                store(tile, u, base + half * SUBLANES, sums[half][u])
        return carry

    lax.fori_loop(0, tiles * blocks, step, 0)


def row_parts(rows):
    half = rows // 2 // 16 * 16
    return slice(0, half), slice(half, rows)


def repeat(count, step):
    unroll = max(n for n in range(1, UNROLL + 1) if count % n == 0)

    def body(index, carry):
        step(index)
        return carry

    lax.fori_loop(0, count, body, 0, unroll=unroll)


def fill(padded, parts, core, tile_v):
    place = 0
    for part, edge, start in parts:
        for u in range(part.shape[0]):
            spread(padded, place, part, u, 0, EDGE, tile_v)
            for tile in range(padded.shape[0]):
                rim = edge[u, start : start + EDGE, lane_tile(tile)].astype(jnp.float32)
                nothing = jnp.zeros_like(rim)
                padded[tile, place, 0:EDGE, :] = jnp.where(core == 1, rim, nothing)
                padded[tile, place, EDGE + tile_v : 2 * EDGE + tile_v, :] = jnp.where(
                    core == 0, rim, nothing
                )
            place += 1


def inner_kernel(flip, core_ref, middle, edge, kernel, base_value, out, padded, taps, *fetch):
    tile_u, tile_v, channels = middle.shape
    copies = []
    if fetch:
        copies.append(pltpu.make_async_copy(base_value, *fetch))
        copies[0].start()
        base_value = fetch[0]
    spread_taps(taps, kernel)
    fill(padded, [(middle, edge, 0)], core_ref[0], tile_v)

    def place(tile, u, base):
        return u, aligned(base, SUBLANES), aligned(tile * LANES, LANES)

    def begin(tile, u, base):
        here = place(tile, u, base)
        if len(base_value.shape) == 2:
            return jnp.broadcast_to(base_value[:, here[2]], (SUBLANES, LANES))
        return base_value[here]

    def store(tile, u, base, value):
        out[place(tile, u, base)] = value

    for copy in copies:
        copy.wait()
    own = range(REACH, REACH + tile_u)
    depthwise(padded, taps, begin, store, tile_u, tile_v, EDGE - REACH, own, flip)


def side_conv(flip, core, on_left, side, edge, kernel, inner, store, padded, taps):
    tile_u, tile_v, _ = inner.shape
    spread_taps(taps, kernel)
    fill(padded, [(side, *edge)], core, tile_v)

    def begin(tile, u, base):
        return inner[u, aligned(base, SUBLANES), aligned(tile * LANES, LANES)]

    for is_left, first in ((True, 0), (False, REACH + tile_u)):
        sources = range(first, first + REACH)

        @pl.when(on_left == is_left)
        def _(sources=sources):
            depthwise(padded, taps, begin, store, tile_u, tile_v, EDGE - REACH, sources, flip)


def side_kernel(flip, place_ref, side, edge, kernel, inner, out, padded, taps):
    tile_v = inner.shape[1]

    def store(tile, u, base, value):
        out[u, aligned(base, SUBLANES), aligned(tile * LANES, LANES)] = value

    start = edge.shape[1] - EDGE
    side_conv(
        flip, place_ref[0], place_ref[1] == 0, side, (edge, start), kernel, inner, store, padded, taps
    )


def up_kernel(
    place_ref, side, kernel, inner, gain, shift, w_in_hbm, b_in,
    normal_form, inv_scale, activated, slope, padded, taps, summed, normed, w_in, sem,
):
    copy = pltpu.make_async_copy(w_in_hbm, w_in, sem)
    copy.start()
    rows, hidden = activated.shape
    _, tile_v, _ = inner.shape
    chunks = tile_v // CHUNK

    def store(tile, u, base, value):
        summed[u, aligned(base, SUBLANES), aligned(tile * LANES, LANES)] = value

    side_conv(
        False, place_ref[0], place_ref[1] == 1, side, (side, tile_v), kernel, inner, store, padded, taps
    )

    def norm_step(index):
        here = aligned(index * CHUNK, CHUNK)
        conv = summed[index // chunks, aligned((index % chunks) * CHUNK, CHUNK), :]
        centred = conv - jnp.mean(conv, axis=-1, keepdims=True)
        variance = jnp.mean(centred * centred, axis=-1, keepdims=True)
        inverse = lax.rsqrt(variance + NORM_EPSILON)
        form = centred * inverse
        normal_form[here, :] = form
        inv_scale[here, :] = jnp.broadcast_to(inverse, (CHUNK, LANES))
        normed[here, :] = (form * gain[...] + shift[...]).astype(jnp.bfloat16)

    repeat(rows // CHUNK, norm_step)

    copy.wait()
    for start in range(0, hidden, MLP_TILE):
        tile = slice(start, start + MLP_TILE)
        for here in row_parts(rows):
            pre = (
                jnp.dot(normed[here, :], w_in[:, tile], preferred_element_type=jnp.float32)
                + b_in[:, tile]
            )
            phi = 0.5 * (1.0 + lax.erf(pre * 0.7071067811865476))
            activated[here, tile] = (pre * phi).astype(jnp.bfloat16)
            rise = phi + pre * jnp.exp(-0.5 * pre * pre) * 0.3989422804014327
            slope[here, tile] = rise.astype(jnp.bfloat16)


def back_kernel(
    pieces, place_ref, places_ref, middle, normal_form, inv_scale, activated, slope,
    gain, w_in, w_out, b_out, scale, *rest,
):
    targets = rest[:pieces]
    mismatch_hbm, d_out, even, odd, edge, even_edge, odd_edge, *scratch = rest[pieces:]
    mismatch_out, sem, target, d_branch, d_hidden, d_normed = scratch
    tile_u, tile_v, channels = middle.shape
    rows, hidden = activated.shape
    chunks = tile_v // CHUNK
    for index, piece in enumerate(targets):
        target[:, aligned(places_ref[index], piece.shape[1]), :] = piece[...]

    for here in row_parts(rows):
        d_normed[here, :] = jnp.dot(
            activated[here, :], w_out[...], preferred_element_type=jnp.float32
        )

    def mismatch_step(index):
        u = index // chunks
        inside = aligned((index % chunks) * CHUNK, CHUNK)
        here = aligned(index * CHUNK, CHUNK)
        mismatch = (
            middle[u, inside, :].astype(jnp.float32)
            + scale[...] * (d_normed[here, :] + b_out[...])
            - target[u, inside, :].astype(jnp.float32)
        )
        mismatch_out[u, inside, :] = mismatch
        d_branch[here, :] = (scale[...] * mismatch).astype(jnp.bfloat16)

    repeat(tile_u * chunks, mismatch_step)
    copy = pltpu.make_async_copy(mismatch_out, mismatch_hbm, sem)
    copy.start()

    for start in range(0, hidden, MLP_TILE):
        tile = slice(start, start + MLP_TILE)
        for here in row_parts(rows):
            d_activated = lax.dot_general(
                d_branch[here, :], w_out[tile, :], CONTRACT_LAST, preferred_element_type=jnp.float32
            )
            d_hidden[here, tile] = (
                d_activated * slope[here, tile].astype(jnp.float32)
            ).astype(jnp.bfloat16)
    for here in row_parts(rows):
        d_normed[here, :] = lax.dot_general(
            d_hidden[here, :], w_in[...], CONTRACT_LAST, preferred_element_type=jnp.float32
        )

    def d_norm_step(index):
        u = index // chunks
        inside = aligned((index % chunks) * CHUNK, CHUNK)
        here = aligned(index * CHUNK, CHUNK)
        scaled = d_normed[here, :] * gain[...]
        form = normal_form[here, :]
        d_conv = inv_scale[here, :1] * (
            scaled
            - jnp.mean(scaled, axis=-1, keepdims=True)
            - form * jnp.mean(scaled * form, axis=-1, keepdims=True)
        )
        d_out[u, inside, :] = d_conv.astype(jnp.bfloat16)

    repeat(tile_u * chunks, d_norm_step)
    edge[...] = d_out[:, pl.ds(pl.multiple_of((1 - place_ref[0]) * (tile_v - EDGE), EDGE), EDGE), :]
    for block, block_edge, from_left in ((even, even_edge, place_ref[1]), (odd, odd_edge, 1 - place_ref[1])):
        columns = pl.ds((1 - from_left) * (tile_u - REACH), REACH)
        block[...] = d_out[columns]
        block_edge[...] = edge[columns]
    copy.wait()


def last_kernel(
    place_ref, even, odd, even_edge, odd_edge, kernel, inner, out, padded, taps, turned
):
    tile_v, tile_u, channels = out.shape
    spread_taps(taps, kernel)
    sides = (even, even_edge, 0), (odd, odd_edge, 0)
    for parity in range(2):

        @pl.when(place_ref[1] == parity)
        def _(left=sides[1 - parity], right=sides[parity]):
            fill(padded, [left, right], place_ref[0], tile_v)

    def begin(tile, u, base):
        return inner[u, aligned(base, SUBLANES), aligned(tile * LANES, LANES)]

    def store(tile, u, base, value):
        turned[u, aligned(base, SUBLANES), aligned(tile * LANES, LANES)] = value

    sources = [*range(REACH), *range(REACH + tile_u, 2 * REACH + tile_u)]
    depthwise(padded, taps, begin, store, tile_u, tile_v, EDGE - REACH, sources, True)
    for u in range(tile_u):
        out[:, u, :] = turned[u]


def call(
    kernel, name, outs, scratch, scalars, arrays, flops, limit, left_in_hbm=(), anywhere=(), out_anywhere=()
):
    vmem = pl.BlockSpec(memory_space=pltpu.VMEM)
    smem = pl.BlockSpec(memory_space=pltpu.SMEM)
    hbm = pl.BlockSpec(memory_space=pltpu.HBM)
    moved = 1 if flops == 1 else sum(a.size * a.dtype.itemsize for a in [*arrays, *outs])
    arrays = [
        pltpu.with_memory_space_constraint(a, pltpu.HBM) if index in left_in_hbm else a
        for index, a in enumerate(arrays)
    ]
    free = pl.BlockSpec(memory_space=pl.ANY)
    specs = [
        hbm if index in left_in_hbm else free if index in anywhere else vmem
        for index in range(len(arrays))
    ]
    return pl.pallas_call(
        kernel,
        out_shape=tuple(outs),
        in_specs=[smem] * len(scalars) + specs,
        out_specs=tuple(free if index in out_anywhere else vmem for index in range(len(outs))),
        scratch_shapes=scratch,
        compiler_params=pltpu.CompilerParams(vmem_limit_bytes=limit << 20),
        cost_estimate=pl.CostEstimate(flops=flops, bytes_accessed=moved, transcendentals=0),
        name=name,
    )(*scalars, *arrays)


def row_pairs(odd):
    row_count = lax.axis_size("row")
    lower = range(1 if odd else 0, row_count - 1, 2)
    return [pair for r in lower for pair in ((r, r + 1), (r + 1, r))]


def facing(tile, row, odd):
    to_right = (row % 2 == 1) if odd else (row % 2 == 0)
    return lax.dynamic_slice_in_dim(
        tile, jnp.where(to_right, tile.shape[0] - REACH, 0), REACH
    )


def edge_lines(tile, core):
    return lax.dynamic_slice_in_dim(
        tile, jnp.where(core == 0, tile.shape[1] - EDGE, 0), EDGE, axis=1
    )


def across(pairs):
    return [(a * 2 + c, b * 2 + 1 - c) for a, b in pairs for c in range(2)]


def find_target(teacher, proj_weight, core, row, tile_u, tile_v):
    row_count = lax.axis_size("row")
    halves = row_count // 2
    channels = proj_weight.shape[1]
    grid_u = tile_u * row_count
    lines = teacher.shape[0] // grid_u
    scalar = core.astype(jnp.int32)[None]
    half_line = grid_u // 2
    by_half = teacher.reshape(lines, 2, half_line, teacher.shape[1])
    size = (lines * half_line, channels)
    fourth = jax.ShapeDtypeStruct((size[0] // 2, channels), jnp.bfloat16)
    scratch = [
        pltpu.VMEM((lines, half_line, teacher.shape[1]), jnp.bfloat16),
        pltpu.SemaphoreType.DMA((COPIES,)),
    ]
    upper, lower = call(
        functools.partial(project_kernel, True),
        "project_away", [fourth] * 2, scratch, [scalar], [by_half, proj_weight], 1, 12, (0,),
    )
    (home,) = call(
        functools.partial(project_kernel, False),
        "project_home", [jax.ShapeDtypeStruct(size, jnp.float32)],
        scratch, [scalar], [by_half, proj_weight], 1, 12, (0,),
    )
    received = [lax.ppermute(away, "col", SWAP) for away in (upper, lower)]
    turns = [lax.rem(turn + row, halves) * tile_u for turn in range(halves)]
    if lines % 16:
        received = jnp.concatenate(received).astype(jnp.float32)
        summed = (home + received).astype(jnp.bfloat16)
        by_u = summed.reshape(lines, half_line, channels).transpose(1, 0, 2)
        blocks = [lax.dynamic_slice_in_dim(by_u, turn, tile_u) for turn in turns]
    else:
        blocks = call(
            functools.partial(combine_kernel, half_line),
            "combine",
            [jax.ShapeDtypeStruct((tile_u, lines, channels), jnp.bfloat16)] * halves,
            [pltpu.VMEM((channels // LANES, *size[:1], LANES), jnp.float32)],
            [jnp.stack(turns).astype(jnp.int32)],
            [home, *received],
            1,
            8,
        )
    pieces, places = [], []
    for turn in range(halves):
        pairs = []
        for r in range(row_count):
            for c in range(2):
                goal = (halves * c + (turn + r) % halves) * 2 + r // halves
                pairs.append((r * 2 + c, goal))
        pieces.append(lax.ppermute(blocks[turn], ("row", "col"), pairs))
        places.append(lax.rem(row + (halves - turn), halves) * lines)
    places = jnp.stack(places).astype(jnp.int32)
    if lines % 16:
        whole = jnp.zeros((tile_u, tile_v, channels), jnp.bfloat16)
        for index, piece in enumerate(pieces):
            whole = lax.dynamic_update_slice_in_dim(whole, piece, places[index], axis=1)
        return [whole], jnp.zeros((1,), jnp.int32), blocks[0]
    return pieces, places, blocks[0]


def on_device(
    teacher,
    proj_weight,
    student,
    dw_kernel,
    dw_bias,
    norm_gain,
    norm_bias,
    w_in,
    b_in,
    w_out,
    b_out,
    layer_scale,
):
    core = lax.axis_index("col")
    row = lax.axis_index("row")
    tile_v, tile_u, channels = student.shape
    hidden = w_in.shape[1]
    tiles = channels // LANES
    wide = tile_v + 2 * EDGE
    scalar = core.astype(jnp.int32)[None]
    f32, bf16 = jnp.float32, jnp.bfloat16
    rows = tile_u * tile_v
    middle = student.transpose(1, 0, 2)
    first_block = facing(middle, row, True)
    first_side = lax.ppermute(first_block, "row", row_pairs(True))
    edge = lax.ppermute(edge_lines(middle, core), "col", SWAP)
    second_block = jnp.concatenate(
        [facing(middle, row, False), facing(edge, row, False)], axis=1
    )
    second_side = lax.ppermute(second_block, "row", row_pairs(False))
    held, *_ = lax.optimization_barrier((proj_weight, first_block, second_block))
    targets, places, block = find_target(teacher, held, core, row, tile_u, tile_v)
    later, _ = lax.optimization_barrier((dw_bias, block))
    matmul = 2 * rows * channels * hidden
    whole = (tile_u, tile_v, channels)
    summed = jax.ShapeDtypeStruct(whole, f32)
    taps = pltpu.VMEM((TAPS * TAPS, tiles, SUBLANES, LANES), f32)
    own_pad, side_pad, rim_pad = (
        pltpu.VMEM((tiles, count, tile_v + 2 * EDGE, LANES), f32)
        for count in (tile_u, REACH, 2 * REACH)
    )
    place = jnp.stack([core, row % 2]).astype(jnp.int32)
    (inner,) = call(
        functools.partial(inner_kernel, False),
        "inner_up", [summed], [own_pad, taps], [scalar],
        [middle, edge, dw_kernel, later[None]], 1, 8,
    )
    arrived, _ = lax.optimization_barrier((first_side, inner))
    first_edge = lax.ppermute(edge_lines(arrived, core), "col", SWAP)
    (inner,) = call(
        functools.partial(side_kernel, False),
        "side_up", [summed], [side_pad, taps], [place],
        [first_side, first_edge, dw_kernel, inner], 1, 8,
    )
    saved = call(
        up_kernel,
        "up",
        [
            jax.ShapeDtypeStruct((rows, channels), f32),
            jax.ShapeDtypeStruct((rows, LANES), f32),
            jax.ShapeDtypeStruct((rows, hidden), bf16),
            jax.ShapeDtypeStruct((rows, hidden), bf16),
        ],
        [side_pad, taps, pltpu.VMEM(whole, f32), pltpu.VMEM((rows, channels), bf16)]
        + [pltpu.VMEM(w_in.shape, bf16), pltpu.SemaphoreType.DMA],
        [place],
        [second_side, dw_kernel, inner, norm_gain[None], norm_bias[None], w_in, b_in[None]],
        4 * matmul,
        16,
        (5,),
    )
    side, rim = (REACH, tile_v, channels), (REACH, EDGE, channels)
    sent = [side, side, (tile_u, EDGE, channels), rim, rim]
    mismatch, d_conv, even, odd, edge, even_edge, odd_edge = call(
        functools.partial(back_kernel, len(targets)),
        "back",
        [summed] + [jax.ShapeDtypeStruct(shape, bf16) for shape in (whole, *sent)],
        [
            pltpu.VMEM(whole, f32),
            pltpu.SemaphoreType.DMA,
            pltpu.VMEM(whole, bf16),
            pltpu.VMEM((rows, channels), bf16),
            pltpu.VMEM((rows, hidden), bf16),
            pltpu.VMEM((rows, channels), f32),
        ],
        [place, places],
        [middle, *saved, norm_gain[None], w_in, w_out, b_out[None], layer_scale[None], *targets],
        4 * matmul,
        16,
        out_anywhere=(0,),
    )
    even = lax.ppermute(even, "row", row_pairs(False))
    odd = lax.ppermute(odd, "row", row_pairs(True))
    edge = lax.ppermute(edge, "col", SWAP)
    even_edge = lax.ppermute(even_edge, ("row", "col"), across(row_pairs(False)))
    odd_edge = lax.ppermute(odd_edge, ("row", "col"), across(row_pairs(True)))
    (inner,) = call(
        functools.partial(inner_kernel, True),
        "inner_last", [summed],
        [own_pad, taps, pltpu.VMEM(whole, f32), pltpu.SemaphoreType.DMA], [scalar],
        [d_conv, edge, dw_kernel, mismatch], matmul, 8, anywhere=(3,),
    )
    (grad,) = call(
        last_kernel,
        "last",
        [jax.ShapeDtypeStruct((tile_v, tile_u, channels), f32)],
        [rim_pad, taps, pltpu.VMEM(whole, f32)],
        [place],
        [even, odd, even_edge, odd_edge, dw_kernel, inner],
        1,
        8,
    )
    return grad


def solution(mesh):
    placed = (
        P(("groups", "row"), "col"),
        P("col", None),
        P(("groups", "col"), "row", None),
        P(),
        P(),
        P(),
        P(),
        P(),
        P(),
        P(),
        P(),
        P(),
    )
    return jax.shard_map(
        on_device,
        mesh=mesh,
        in_specs=placed,
        out_specs=P(("groups", "col"), "row", None),
        check_vma=False,
    )
```

```python
import functools

import jax
import jax.numpy as jnp
from jax import lax
from jax.experimental import pallas as pl
from jax.experimental.pallas import tpu as pltpu
from jax.sharding import PartitionSpec as P

NORM_EPSILON = 1e-06
REACH = 3
TAPS = 2 * REACH + 1
LANES = 128
SUBLANES = 8
EDGE = 8
CHUNK = 16
UNROLL = 16
COPIES = 8
DOTS = 2
MLP_TILE = 512
CONTRACT_LAST = (((1,), (1,)), ((), ()))
SWAP = [(0, 1), (1, 0)]


def aligned(start, size):
    return pl.ds(pl.multiple_of(start, size), size)


def lane_tile(tile):
    return slice(tile * LANES, (tile + 1) * LANES)


def project_kernel(other, core_ref, teacher_hbm, weight, *rest):
    *outs, rows, sems = rest
    half = 1 - core_ref[0] if other else core_ref[0]
    lines, wide, depth = rows.shape
    count = next(n for n in (COPIES, 4, 2) if lines % n == 0)
    copies = []
    for index in range(count):
        here = pl.ds(index * (lines // count), lines // count)
        copy = pltpu.make_async_copy(teacher_hbm.at[here, half], rows.at[here], sems.at[index])
        copy.start()
        copies.append(copy)
    size = lines * wide // DOTS
    for index in range(DOTS):
        for copy in copies[index * count // DOTS : (index + 1) * count // DOTS]:
            copy.wait()
        here = pl.ds(index * (lines // DOTS), lines // DOTS)
        product = jnp.dot(
            rows[here].reshape(size, depth), weight[...], preferred_element_type=jnp.float32
        )
        out = outs[index * len(outs) // DOTS]
        start = index * size % out.shape[0]
        out[start : start + size] = product.astype(out.dtype)


def combine_kernel(wide, turns_ref, home, upper, lower, *rest):
    *blocks, summed = rest
    half = upper.shape[0]
    for tile in range(summed.shape[0]):
        lanes = lane_tile(tile)
        for start, received in ((0, upper), (half, lower)):
            here = slice(start, start + half)
            summed[tile, here] = home[here, lanes] + received[:, lanes].astype(jnp.float32)
    for index, block in enumerate(blocks):
        tile_u, lines, _ = block.shape
        for u in range(tile_u):
            rows = pl.ds(turns_ref[index] + u, lines, stride=wide)
            for tile in range(summed.shape[0]):
                block[u, :, lane_tile(tile)] = summed[tile, rows, :].astype(jnp.bfloat16)


def spread_taps(taps, kernel):
    for row_tap in range(TAPS):
        for col_tap in range(TAPS):
            for tile in range(taps.shape[1]):
                line = kernel[row_tap, col_tap : col_tap + 1, lane_tile(tile)]
                taps[row_tap * TAPS + col_tap, tile] = jnp.broadcast_to(line, (SUBLANES, LANES))


def spread(padded, place, part, source, start, row, count):
    for tile in range(padded.shape[0]):
        padded[tile, place, pl.ds(row, count), :] = part[
            source, pl.ds(start, count), lane_tile(tile)
        ].astype(jnp.float32)


def depthwise(padded, taps, begin, store, tile_u, count, offset, sources, flip):
    tiles = padded.shape[0]
    blocks = count // (2 * SUBLANES)

    def step(index, carry):
        tile = index // blocks
        base = pl.multiple_of((index % blocks) * (2 * SUBLANES), 2 * SUBLANES)
        sums = [
            [begin(tile, u, base + half * SUBLANES) for u in range(tile_u)] for half in range(2)
        ]
        for row_tap in range(TAPS):
            weights = []
            for col_tap in range(TAPS):
                tap = row_tap * TAPS + col_tap
                weights.append(taps[TAPS * TAPS - 1 - tap if flip else tap, tile])
            for place, source in enumerate(sources):
                for half in range(2):
                    row = base + (half * SUBLANES + row_tap) + offset
                    values = padded[tile, place, pl.ds(row, SUBLANES), :]
                    for u in range(max(0, source - TAPS + 1), min(tile_u, source + 1)):
                        term = weights[source - u] * values
                        sums[half][u] = term if sums[half][u] is None else sums[half][u] + term
        for half in range(2):
            for u in range(tile_u):
                store(tile, u, base + half * SUBLANES, sums[half][u])
        return carry

    lax.fori_loop(0, tiles * blocks, step, 0)


def row_parts(rows):
    half = rows // 2 // 16 * 16
    return slice(0, half), slice(half, rows)


def repeat(count, step):
    unroll = max(n for n in range(1, UNROLL + 1) if count % n == 0)

    def body(index, carry):
        step(index)
        return carry

    lax.fori_loop(0, count, body, 0, unroll=unroll)


def fill(padded, parts, core, tile_v):
    place = 0
    for part, edge, start in parts:
        for u in range(part.shape[0]):
            spread(padded, place, part, u, 0, EDGE, tile_v)
            for tile in range(padded.shape[0]):
                rim = edge[u, start : start + EDGE, lane_tile(tile)].astype(jnp.float32)
                nothing = jnp.zeros_like(rim)
                padded[tile, place, 0:EDGE, :] = jnp.where(core == 1, rim, nothing)
                padded[tile, place, EDGE + tile_v : 2 * EDGE + tile_v, :] = jnp.where(
                    core == 0, rim, nothing
                )
            place += 1


def inner_kernel(flip, core_ref, middle, edge, kernel, base_value, out, padded, taps, *fetch):
    tile_u, tile_v, channels = middle.shape
    copies = []
    if fetch:
        copies.append(pltpu.make_async_copy(base_value, *fetch))
        copies[0].start()
        base_value = fetch[0]
    spread_taps(taps, kernel)
    fill(padded, [(middle, edge, 0)], core_ref[0], tile_v)

    def place(tile, u, base):
        return u, aligned(base, SUBLANES), aligned(tile * LANES, LANES)

    def begin(tile, u, base):
        here = place(tile, u, base)
        if len(base_value.shape) == 2:
            return jnp.broadcast_to(base_value[:, here[2]], (SUBLANES, LANES))
        return base_value[here]

    def store(tile, u, base, value):
        out[place(tile, u, base)] = value

    for copy in copies:
        copy.wait()
    own = range(REACH, REACH + tile_u)
    depthwise(padded, taps, begin, store, tile_u, tile_v, EDGE - REACH, own, flip)


def side_conv(flip, core, on_left, side, edge, kernel, inner, store, padded, taps):
    tile_u, tile_v, _ = inner.shape
    spread_taps(taps, kernel)
    fill(padded, [(side, *edge)], core, tile_v)

    def begin(tile, u, base):
        return inner[u, aligned(base, SUBLANES), aligned(tile * LANES, LANES)]

    for is_left, first in ((True, 0), (False, REACH + tile_u)):
        sources = range(first, first + REACH)

        @pl.when(on_left == is_left)
        def _(sources=sources):
            depthwise(padded, taps, begin, store, tile_u, tile_v, EDGE - REACH, sources, flip)


def side_kernel(flip, place_ref, side, edge, kernel, inner, out, padded, taps):
    tile_v = inner.shape[1]

    def store(tile, u, base, value):
        out[u, aligned(base, SUBLANES), aligned(tile * LANES, LANES)] = value

    start = edge.shape[1] - EDGE
    side_conv(
        flip, place_ref[0], place_ref[1] == 1, side, (edge, start), kernel, inner, store, padded, taps
    )


def up_kernel(
    place_ref, side, kernel, inner, gain, shift, w_in_hbm, b_in,
    normal_form, inv_scale, activated, slope, padded, taps, summed, normed, w_in, sem,
):
    copy = pltpu.make_async_copy(w_in_hbm, w_in, sem)
    copy.start()
    rows, hidden = activated.shape
    _, tile_v, _ = inner.shape
    chunks = tile_v // CHUNK

    def store(tile, u, base, value):
        summed[u, aligned(base, SUBLANES), aligned(tile * LANES, LANES)] = value

    side_conv(
        False, place_ref[0], place_ref[1] == 0, side, (side, tile_v), kernel, inner, store, padded, taps
    )

    def norm_step(index):
        here = aligned(index * CHUNK, CHUNK)
        conv = summed[index // chunks, aligned((index % chunks) * CHUNK, CHUNK), :]
        centred = conv - jnp.mean(conv, axis=-1, keepdims=True)
        variance = jnp.mean(centred * centred, axis=-1, keepdims=True)
        inverse = lax.rsqrt(variance + NORM_EPSILON)
        form = centred * inverse
        normal_form[here, :] = form
        inv_scale[here, :] = jnp.broadcast_to(inverse, (CHUNK, LANES))
        normed[here, :] = (form * gain[...] + shift[...]).astype(jnp.bfloat16)

    repeat(rows // CHUNK, norm_step)

    copy.wait()
    for start in range(0, hidden, MLP_TILE):
        tile = slice(start, start + MLP_TILE)
        for here in row_parts(rows):
            pre = (
                jnp.dot(normed[here, :], w_in[:, tile], preferred_element_type=jnp.float32)
                + b_in[:, tile]
            )
            phi = 0.5 * (1.0 + lax.erf(pre * 0.7071067811865476))
            activated[here, tile] = (pre * phi).astype(jnp.bfloat16)
            rise = phi + pre * jnp.exp(-0.5 * pre * pre) * 0.3989422804014327
            slope[here, tile] = rise.astype(jnp.bfloat16)


def back_kernel(
    pieces, place_ref, places_ref, middle, normal_form, inv_scale, activated, slope,
    gain, w_in, w_out, b_out, scale, *rest,
):
    targets = rest[:pieces]
    mismatch_hbm, d_out, even, odd, edge, even_edge, odd_edge, *scratch = rest[pieces:]
    mismatch_out, sem, target, d_branch, d_hidden, d_normed = scratch
    tile_u, tile_v, channels = middle.shape
    rows, hidden = activated.shape
    chunks = tile_v // CHUNK
    for index, piece in enumerate(targets):
        target[:, aligned(places_ref[index], piece.shape[1]), :] = piece[...]

    for here in row_parts(rows):
        d_normed[here, :] = jnp.dot(
            activated[here, :], w_out[...], preferred_element_type=jnp.float32
        )

    def mismatch_step(index):
        u = index // chunks
        inside = aligned((index % chunks) * CHUNK, CHUNK)
        here = aligned(index * CHUNK, CHUNK)
        mismatch = (
            middle[u, inside, :].astype(jnp.float32)
            + scale[...] * (d_normed[here, :] + b_out[...])
            - target[u, inside, :].astype(jnp.float32)
        )
        mismatch_out[u, inside, :] = mismatch
        d_branch[here, :] = (scale[...] * mismatch).astype(jnp.bfloat16)

    repeat(tile_u * chunks, mismatch_step)
    copy = pltpu.make_async_copy(mismatch_out, mismatch_hbm, sem)
    copy.start()

    for start in range(0, hidden, MLP_TILE):
        tile = slice(start, start + MLP_TILE)
        for here in row_parts(rows):
            d_activated = lax.dot_general(
                d_branch[here, :], w_out[tile, :], CONTRACT_LAST, preferred_element_type=jnp.float32
            )
            d_hidden[here, tile] = (
                d_activated * slope[here, tile].astype(jnp.float32)
            ).astype(jnp.bfloat16)
    for here in row_parts(rows):
        d_normed[here, :] = lax.dot_general(
            d_hidden[here, :], w_in[...], CONTRACT_LAST, preferred_element_type=jnp.float32
        )

    def d_norm_step(index):
        u = index // chunks
        inside = aligned((index % chunks) * CHUNK, CHUNK)
        here = aligned(index * CHUNK, CHUNK)
        scaled = d_normed[here, :] * gain[...]
        form = normal_form[here, :]
        d_conv = inv_scale[here, :1] * (
            scaled
            - jnp.mean(scaled, axis=-1, keepdims=True)
            - form * jnp.mean(scaled * form, axis=-1, keepdims=True)
        )
        d_out[u, inside, :] = d_conv.astype(jnp.bfloat16)

    repeat(tile_u * chunks, d_norm_step)
    edge[...] = d_out[:, pl.ds(pl.multiple_of((1 - place_ref[0]) * (tile_v - EDGE), EDGE), EDGE), :]
    for block, block_edge, from_left in ((even, even_edge, place_ref[1]), (odd, odd_edge, 1 - place_ref[1])):
        columns = pl.ds((1 - from_left) * (tile_u - REACH), REACH)
        block[...] = d_out[columns]
        block_edge[...] = edge[columns]
    copy.wait()


def last_kernel(
    place_ref, even, odd, even_edge, odd_edge, kernel, inner, out, padded, taps, turned
):
    tile_v, tile_u, channels = out.shape
    spread_taps(taps, kernel)
    sides = (even, even_edge, 0), (odd, odd_edge, 0)
    for parity in range(2):

        @pl.when(place_ref[1] == parity)
        def _(left=sides[1 - parity], right=sides[parity]):
            fill(padded, [left, right], place_ref[0], tile_v)

    def begin(tile, u, base):
        return inner[u, aligned(base, SUBLANES), aligned(tile * LANES, LANES)]

    def store(tile, u, base, value):
        turned[u, aligned(base, SUBLANES), aligned(tile * LANES, LANES)] = value

    sources = [*range(REACH), *range(REACH + tile_u, 2 * REACH + tile_u)]
    depthwise(padded, taps, begin, store, tile_u, tile_v, EDGE - REACH, sources, True)
    for u in range(tile_u):
        out[:, u, :] = turned[u]


def call(
    kernel, name, outs, scratch, scalars, arrays, flops, limit, left_in_hbm=(), anywhere=(), out_anywhere=()
):
    vmem = pl.BlockSpec(memory_space=pltpu.VMEM)
    smem = pl.BlockSpec(memory_space=pltpu.SMEM)
    hbm = pl.BlockSpec(memory_space=pltpu.HBM)
    moved = 1 if flops == 1 else sum(a.size * a.dtype.itemsize for a in [*arrays, *outs])
    arrays = [
        pltpu.with_memory_space_constraint(a, pltpu.HBM) if index in left_in_hbm else a
        for index, a in enumerate(arrays)
    ]
    free = pl.BlockSpec(memory_space=pl.ANY)
    specs = [
        hbm if index in left_in_hbm else free if index in anywhere else vmem
        for index in range(len(arrays))
    ]
    return pl.pallas_call(
        kernel,
        out_shape=tuple(outs),
        in_specs=[smem] * len(scalars) + specs,
        out_specs=tuple(free if index in out_anywhere else vmem for index in range(len(outs))),
        scratch_shapes=scratch,
        compiler_params=pltpu.CompilerParams(vmem_limit_bytes=limit << 20),
        cost_estimate=pl.CostEstimate(flops=flops, bytes_accessed=moved, transcendentals=0),
        name=name,
    )(*scalars, *arrays)


def row_pairs(odd):
    row_count = lax.axis_size("row")
    lower = range(1 if odd else 0, row_count - 1, 2)
    return [pair for r in lower for pair in ((r, r + 1), (r + 1, r))]


def facing(tile, row, odd):
    to_right = (row % 2 == 1) if odd else (row % 2 == 0)
    return lax.dynamic_slice_in_dim(
        tile, jnp.where(to_right, tile.shape[0] - REACH, 0), REACH
    )


def edge_lines(tile, core):
    return lax.dynamic_slice_in_dim(
        tile, jnp.where(core == 0, tile.shape[1] - EDGE, 0), EDGE, axis=1
    )


def across(pairs):
    return [(a * 2 + c, b * 2 + 1 - c) for a, b in pairs for c in range(2)]


def find_target(teacher, proj_weight, core, row, tile_u, tile_v):
    row_count = lax.axis_size("row")
    halves = row_count // 2
    channels = proj_weight.shape[1]
    grid_u = tile_u * row_count
    lines = teacher.shape[0] // grid_u
    scalar = core.astype(jnp.int32)[None]
    half_line = grid_u // 2
    by_half = teacher.reshape(lines, 2, half_line, teacher.shape[1])
    size = (lines * half_line, channels)
    fourth = jax.ShapeDtypeStruct((size[0] // 2, channels), jnp.bfloat16)
    scratch = [
        pltpu.VMEM((lines, half_line, teacher.shape[1]), jnp.bfloat16),
        pltpu.SemaphoreType.DMA((COPIES,)),
    ]
    upper, lower = call(
        functools.partial(project_kernel, True),
        "project_away", [fourth] * 2, scratch, [scalar], [by_half, proj_weight], 1, 12, (0,),
    )
    (home,) = call(
        functools.partial(project_kernel, False),
        "project_home", [jax.ShapeDtypeStruct(size, jnp.float32)],
        scratch, [scalar], [by_half, proj_weight], 1, 12, (0,),
    )
    received = [lax.ppermute(away, "col", SWAP) for away in (upper, lower)]
    turns = [lax.rem(turn + row, halves) * tile_u for turn in range(halves)]
    if lines % 16:
        received = jnp.concatenate(received).astype(jnp.float32)
        summed = (home + received).astype(jnp.bfloat16)
        by_u = summed.reshape(lines, half_line, channels).transpose(1, 0, 2)
        blocks = [lax.dynamic_slice_in_dim(by_u, turn, tile_u) for turn in turns]
    else:
        blocks = call(
            functools.partial(combine_kernel, half_line),
            "combine",
            [jax.ShapeDtypeStruct((tile_u, lines, channels), jnp.bfloat16)] * halves,
            [pltpu.VMEM((channels // LANES, *size[:1], LANES), jnp.float32)],
            [jnp.stack(turns).astype(jnp.int32)],
            [home, *received],
            1,
            8,
        )
    pieces, places = [], []
    for turn in range(halves):
        pairs = []
        for r in range(row_count):
            for c in range(2):
                goal = (halves * c + (turn + r) % halves) * 2 + r // halves
                pairs.append((r * 2 + c, goal))
        pieces.append(lax.ppermute(blocks[turn], ("row", "col"), pairs))
        places.append(lax.rem(row + (halves - turn), halves) * lines)
    places = jnp.stack(places).astype(jnp.int32)
    if lines % 16:
        whole = jnp.zeros((tile_u, tile_v, channels), jnp.bfloat16)
        for index, piece in enumerate(pieces):
            whole = lax.dynamic_update_slice_in_dim(whole, piece, places[index], axis=1)
        return [whole], jnp.zeros((1,), jnp.int32), blocks[0]
    return pieces, places, blocks[0]


def on_device(
    teacher,
    proj_weight,
    student,
    dw_kernel,
    dw_bias,
    norm_gain,
    norm_bias,
    w_in,
    b_in,
    w_out,
    b_out,
    layer_scale,
):
    core = lax.axis_index("col")
    row = lax.axis_index("row")
    tile_v, tile_u, channels = student.shape
    hidden = w_in.shape[1]
    tiles = channels // LANES
    wide = tile_v + 2 * EDGE
    scalar = core.astype(jnp.int32)[None]
    f32, bf16 = jnp.float32, jnp.bfloat16
    rows = tile_u * tile_v
    middle = student.transpose(1, 0, 2)
    first_block = facing(middle, row, False)
    first_side = lax.ppermute(first_block, "row", row_pairs(False))
    edge = lax.ppermute(edge_lines(middle, core), "col", SWAP)
    second_block = jnp.concatenate(
        [facing(middle, row, True), facing(edge, row, True)], axis=1
    )
    second_side = lax.ppermute(second_block, "row", row_pairs(True))
    held, *_ = lax.optimization_barrier((proj_weight, first_block, second_block))
    targets, places, block = find_target(teacher, held, core, row, tile_u, tile_v)
    later, _ = lax.optimization_barrier((dw_bias, block))
    matmul = 2 * rows * channels * hidden
    whole = (tile_u, tile_v, channels)
    summed = jax.ShapeDtypeStruct(whole, f32)
    taps = pltpu.VMEM((TAPS * TAPS, tiles, SUBLANES, LANES), f32)
    own_pad, side_pad, rim_pad = (
        pltpu.VMEM((tiles, count, tile_v + 2 * EDGE, LANES), f32)
        for count in (tile_u, REACH, 2 * REACH)
    )
    place = jnp.stack([core, row % 2]).astype(jnp.int32)
    (inner,) = call(
        functools.partial(inner_kernel, False),
        "inner_up", [summed], [own_pad, taps], [scalar],
        [middle, edge, dw_kernel, later[None]], 1, 8,
    )
    arrived, _ = lax.optimization_barrier((first_side, inner))
    first_edge = lax.ppermute(edge_lines(arrived, core), "col", SWAP)
    (inner,) = call(
        functools.partial(side_kernel, False),
        "side_up", [summed], [side_pad, taps], [place],
        [first_side, first_edge, dw_kernel, inner], 1, 8,
    )
    saved = call(
        up_kernel,
        "up",
        [
            jax.ShapeDtypeStruct((rows, channels), f32),
            jax.ShapeDtypeStruct((rows, LANES), f32),
            jax.ShapeDtypeStruct((rows, hidden), bf16),
            jax.ShapeDtypeStruct((rows, hidden), bf16),
        ],
        [side_pad, taps, pltpu.VMEM(whole, f32), pltpu.VMEM((rows, channels), bf16)]
        + [pltpu.VMEM(w_in.shape, bf16), pltpu.SemaphoreType.DMA],
        [place],
        [second_side, dw_kernel, inner, norm_gain[None], norm_bias[None], w_in, b_in[None]],
        4 * matmul,
        16,
        (5,),
    )
    side, rim = (REACH, tile_v, channels), (REACH, EDGE, channels)
    sent = [side, side, (tile_u, EDGE, channels), rim, rim]
    mismatch, d_conv, even, odd, edge, even_edge, odd_edge = call(
        functools.partial(back_kernel, len(targets)),
        "back",
        [summed] + [jax.ShapeDtypeStruct(shape, bf16) for shape in (whole, *sent)],
        [
            pltpu.VMEM(whole, f32),
            pltpu.SemaphoreType.DMA,
            pltpu.VMEM(whole, bf16),
            pltpu.VMEM((rows, channels), bf16),
            pltpu.VMEM((rows, hidden), bf16),
            pltpu.VMEM((rows, channels), f32),
        ],
        [place, places],
        [middle, *saved, norm_gain[None], w_in, w_out, b_out[None], layer_scale[None], *targets],
        4 * matmul,
        16,
        out_anywhere=(0,),
    )
    even = lax.ppermute(even, "row", row_pairs(False))
    odd = lax.ppermute(odd, "row", row_pairs(True))
    edge = lax.ppermute(edge, "col", SWAP)
    even_edge = lax.ppermute(even_edge, ("row", "col"), across(row_pairs(False)))
    odd_edge = lax.ppermute(odd_edge, ("row", "col"), across(row_pairs(True)))
    (inner,) = call(
        functools.partial(inner_kernel, True),
        "inner_last", [summed],
        [own_pad, taps, pltpu.VMEM(whole, f32), pltpu.SemaphoreType.DMA], [scalar],
        [d_conv, edge, dw_kernel, mismatch], matmul, 8, anywhere=(3,),
    )
    (grad,) = call(
        last_kernel,
        "last",
        [jax.ShapeDtypeStruct((tile_v, tile_u, channels), f32)],
        [rim_pad, taps, pltpu.VMEM(whole, f32)],
        [place],
        [even, odd, even_edge, odd_edge, dw_kernel, inner],
        1,
        8,
    )
    return grad


def solution(mesh):
    placed = (
        P(("groups", "row"), "col"),
        P("col", None),
        P(("groups", "col"), "row", None),
        P(),
        P(),
        P(),
        P(),
        P(),
        P(),
        P(),
        P(),
        P(),
    )
    return jax.shard_map(
        on_device,
        mesh=mesh,
        in_specs=placed,
        out_specs=P(("groups", "col"), "row", None),
        check_vma=False,
    )
```

```python
import functools

import jax
import jax.numpy as jnp
from jax import lax
from jax.experimental import pallas as pl
from jax.experimental.pallas import tpu as pltpu
from jax.sharding import PartitionSpec as P

NORM_EPSILON = 1e-06
REACH = 3
TAPS = 2 * REACH + 1
LANES = 128
SUBLANES = 8
EDGE = 8
CHUNK = 16
UNROLL = 16
COPIES = 8
MLP_TILE = 512
CONTRACT_LAST = (((1,), (1,)), ((), ()))
SWAP = [(0, 1), (1, 0)]


def aligned(start, size):
    return pl.ds(pl.multiple_of(start, size), size)


def lane_tile(tile):
    return slice(tile * LANES, (tile + 1) * LANES)


def project_kernel(
    core_ref, teacher_hbm, weight, upper, lower, home_anywhere, rows, sems, home, home_sems
):
    core = core_ref[0]
    _, lines, wide, depth = rows.shape
    count = next(n for n in (COPIES, 4, 2) if lines % n == 0)
    copies = []
    for slot, half in enumerate((1 - core, core)):
        for index in range(count):
            here = pl.ds(index * (lines // count), lines // count)
            copy = pltpu.make_async_copy(
                teacher_hbm.at[here, half], rows.at[slot, here], sems.at[slot, index]
            )
            copy.start()
            copies.append(copy)
    size = lines * wide // 2
    leaving = []
    for slot in range(2):
        for index in range(2):
            first = slot * count + index * count // 2
            for copy in copies[first : first + count // 2]:
                copy.wait()
            here = pl.ds(index * (lines // 2), lines // 2)
            product = jnp.dot(
                rows[slot, here].reshape(size, depth),
                weight[...],
                preferred_element_type=jnp.float32,
            )
            if slot:
                here = pl.ds(index * size, size)
                home[here] = product
                leaving.append(
                    pltpu.make_async_copy(home.at[here], home_anywhere.at[here], home_sems.at[index])
                )
                leaving[-1].start()
            else:
                (upper, lower)[index][...] = product.astype(upper.dtype)
    for copy in leaving:
        copy.wait()


def combine_kernel(wide, turns_ref, home_anywhere, upper, lower, *rest):
    *blocks, summed, home, sem = rest
    copy = pltpu.make_async_copy(home_anywhere, home, sem)
    copy.start()
    copy.wait()
    half = upper.shape[0]
    for tile in range(summed.shape[0]):
        lanes = lane_tile(tile)
        for start, received in ((0, upper), (half, lower)):
            here = slice(start, start + half)
            summed[tile, here] = home[here, lanes] + received[:, lanes].astype(jnp.float32)
    for index, block in enumerate(blocks):
        tile_u, lines, _ = block.shape
        for u in range(tile_u):
            rows = pl.ds(turns_ref[index] + u, lines, stride=wide)
            for tile in range(summed.shape[0]):
                block[u, :, lane_tile(tile)] = summed[tile, rows, :].astype(jnp.bfloat16)


def spread_taps(taps, kernel):
    for row_tap in range(TAPS):
        for col_tap in range(TAPS):
            for tile in range(taps.shape[1]):
                line = kernel[row_tap, col_tap : col_tap + 1, lane_tile(tile)]
                taps[row_tap * TAPS + col_tap, tile] = jnp.broadcast_to(line, (SUBLANES, LANES))


def spread(padded, place, part, source, start, row, count):
    for tile in range(padded.shape[0]):
        padded[tile, place, pl.ds(row, count), :] = part[
            source, pl.ds(start, count), lane_tile(tile)
        ].astype(jnp.float32)


def depthwise(padded, taps, begin, store, tile_u, count, offset, sources, flip):
    tiles = padded.shape[0]
    blocks = count // (2 * SUBLANES)

    def step(index, carry):
        tile = index // blocks
        base = pl.multiple_of((index % blocks) * (2 * SUBLANES), 2 * SUBLANES)
        sums = [
            [begin(tile, u, base + half * SUBLANES) for u in range(tile_u)] for half in range(2)
        ]
        for row_tap in range(TAPS):
            weights = []
            for col_tap in range(TAPS):
                tap = row_tap * TAPS + col_tap
                weights.append(taps[TAPS * TAPS - 1 - tap if flip else tap, tile])
            for place, source in enumerate(sources):
                for half in range(2):
                    row = base + (half * SUBLANES + row_tap) + offset
                    values = padded[tile, place, pl.ds(row, SUBLANES), :]
                    for u in range(max(0, source - TAPS + 1), min(tile_u, source + 1)):
                        term = weights[source - u] * values
                        sums[half][u] = term if sums[half][u] is None else sums[half][u] + term
        for half in range(2):
            for u in range(tile_u):
                store(tile, u, base + half * SUBLANES, sums[half][u])
        return carry

    lax.fori_loop(0, tiles * blocks, step, 0)


def row_parts(rows):
    half = rows // 2 // 16 * 16
    return slice(0, half), slice(half, rows)


def repeat(count, step):
    unroll = max(n for n in range(1, UNROLL + 1) if count % n == 0)

    def body(index, carry):
        step(index)
        return carry

    lax.fori_loop(0, count, body, 0, unroll=unroll)


def fill(padded, parts, core, tile_v):
    place = 0
    for part, edge, start in parts:
        for u in range(part.shape[0]):
            spread(padded, place, part, u, 0, EDGE, tile_v)
            for tile in range(padded.shape[0]):
                rim = edge[u, start : start + EDGE, lane_tile(tile)].astype(jnp.float32)
                nothing = jnp.zeros_like(rim)
                padded[tile, place, 0:EDGE, :] = jnp.where(core == 1, rim, nothing)
                padded[tile, place, EDGE + tile_v : 2 * EDGE + tile_v, :] = jnp.where(
                    core == 0, rim, nothing
                )
            place += 1


def inner_kernel(flip, core_ref, middle, edge, kernel, base_value, out, *scratch):
    tile_u, tile_v, channels = middle.shape
    copies = []
    if flip:
        padded, *fetch = scratch
        taps = kernel
        copies.append(pltpu.make_async_copy(base_value, *fetch))
        copies[0].start()
        base_value = fetch[0]
    else:
        taps, padded = scratch
        spread_taps(taps, kernel)
    fill(padded, [(middle, edge, 0)], core_ref[0], tile_v)

    def place(tile, u, base):
        return u, aligned(base, SUBLANES), aligned(tile * LANES, LANES)

    def begin(tile, u, base):
        here = place(tile, u, base)
        if len(base_value.shape) == 2:
            return jnp.broadcast_to(base_value[:, here[2]], (SUBLANES, LANES))
        return base_value[here]

    def store(tile, u, base, value):
        out[place(tile, u, base)] = value

    for copy in copies:
        copy.wait()
    own = range(REACH, REACH + tile_u)
    depthwise(padded, taps, begin, store, tile_u, tile_v, EDGE - REACH, own, flip)


def side_conv(flip, core, on_left, side, edge, taps, inner, store, padded):
    tile_u, tile_v, _ = inner.shape
    fill(padded, [(side, *edge)], core, tile_v)

    def begin(tile, u, base):
        return inner[u, aligned(base, SUBLANES), aligned(tile * LANES, LANES)]

    for is_left, first in ((True, 0), (False, REACH + tile_u)):
        sources = range(first, first + REACH)

        @pl.when(on_left == is_left)
        def _(sources=sources):
            depthwise(padded, taps, begin, store, tile_u, tile_v, EDGE - REACH, sources, flip)


def side_kernel(flip, place_ref, side, edge, taps, inner, out, padded):
    tile_v = inner.shape[1]

    def store(tile, u, base, value):
        out[u, aligned(base, SUBLANES), aligned(tile * LANES, LANES)] = value

    start = edge.shape[1] - EDGE
    side_conv(
        flip, place_ref[0], place_ref[1] == 0, side, (edge, start), taps, inner, store, padded
    )


def up_kernel(
    place_ref, side, taps, inner, gain, shift, w_in_hbm, b_in,
    normal_form, inv_scale, activated, slope, padded, summed, normed, w_in, sem,
):
    copy = pltpu.make_async_copy(w_in_hbm, w_in, sem)
    copy.start()
    rows, hidden = activated.shape
    _, tile_v, _ = inner.shape
    chunks = tile_v // CHUNK

    def store(tile, u, base, value):
        summed[u, aligned(base, SUBLANES), aligned(tile * LANES, LANES)] = value

    side_conv(
        False, place_ref[0], place_ref[1] == 1, side, (side, tile_v), taps, inner, store, padded
    )

    def norm_step(index):
        here = aligned(index * CHUNK, CHUNK)
        conv = summed[index // chunks, aligned((index % chunks) * CHUNK, CHUNK), :]
        centred = conv - jnp.mean(conv, axis=-1, keepdims=True)
        variance = jnp.mean(centred * centred, axis=-1, keepdims=True)
        inverse = lax.rsqrt(variance + NORM_EPSILON)
        form = centred * inverse
        normal_form[here, :] = form
        inv_scale[here, :] = jnp.broadcast_to(inverse, (CHUNK, LANES))
        normed[here, :] = (form * gain[...] + shift[...]).astype(jnp.bfloat16)

    repeat(rows // CHUNK, norm_step)

    copy.wait()
    for start in range(0, hidden, MLP_TILE):
        tile = slice(start, start + MLP_TILE)
        for here in row_parts(rows):
            pre = (
                jnp.dot(normed[here, :], w_in[:, tile], preferred_element_type=jnp.float32)
                + b_in[:, tile]
            )
            phi = 0.5 * (1.0 + lax.erf(pre * 0.7071067811865476))
            activated[here, tile] = (pre * phi).astype(jnp.bfloat16)
            rise = phi + pre * jnp.exp(-0.5 * pre * pre) * 0.3989422804014327
            slope[here, tile] = rise.astype(jnp.bfloat16)


def back_kernel(
    pieces, place_ref, places_ref, middle, normal_form, inv_scale, activated, slope,
    gain, w_in, w_out, b_out, scale, *rest,
):
    targets = rest[:pieces]
    mismatch_hbm, d_out, even, odd, edge, even_edge, odd_edge, *scratch = rest[pieces:]
    mismatch_out, sem, target, d_branch, d_hidden, d_normed = scratch
    tile_u, tile_v, channels = middle.shape
    rows, hidden = activated.shape
    chunks = tile_v // CHUNK
    for index, piece in enumerate(targets):
        target[:, aligned(places_ref[index], piece.shape[1]), :] = piece[...]

    for here in row_parts(rows):
        d_normed[here, :] = jnp.dot(
            activated[here, :], w_out[...], preferred_element_type=jnp.float32
        )

    def mismatch_step(index):
        u = index // chunks
        inside = aligned((index % chunks) * CHUNK, CHUNK)
        here = aligned(index * CHUNK, CHUNK)
        mismatch = (
            middle[u, inside, :].astype(jnp.float32)
            + scale[...] * (d_normed[here, :] + b_out[...])
            - target[u, inside, :].astype(jnp.float32)
        )
        mismatch_out[u, inside, :] = mismatch
        d_branch[here, :] = (scale[...] * mismatch).astype(jnp.bfloat16)

    repeat(tile_u * chunks, mismatch_step)
    copy = pltpu.make_async_copy(mismatch_out, mismatch_hbm, sem)
    copy.start()

    for start in range(0, hidden, MLP_TILE):
        tile = slice(start, start + MLP_TILE)
        for here in row_parts(rows):
            d_activated = lax.dot_general(
                d_branch[here, :], w_out[tile, :], CONTRACT_LAST, preferred_element_type=jnp.float32
            )
            d_hidden[here, tile] = (
                d_activated * slope[here, tile].astype(jnp.float32)
            ).astype(jnp.bfloat16)
    for here in row_parts(rows):
        d_normed[here, :] = lax.dot_general(
            d_hidden[here, :], w_in[...], CONTRACT_LAST, preferred_element_type=jnp.float32
        )

    def d_norm_step(index):
        u = index // chunks
        inside = aligned((index % chunks) * CHUNK, CHUNK)
        here = aligned(index * CHUNK, CHUNK)
        scaled = d_normed[here, :] * gain[...]
        form = normal_form[here, :]
        d_conv = inv_scale[here, :1] * (
            scaled
            - jnp.mean(scaled, axis=-1, keepdims=True)
            - form * jnp.mean(scaled * form, axis=-1, keepdims=True)
        )
        d_out[u, inside, :] = d_conv.astype(jnp.bfloat16)

    repeat(tile_u * chunks, d_norm_step)
    edge[...] = d_out[:, pl.ds(pl.multiple_of((1 - place_ref[0]) * (tile_v - EDGE), EDGE), EDGE), :]
    for block, block_edge, from_left in ((even, even_edge, place_ref[1]), (odd, odd_edge, 1 - place_ref[1])):
        columns = pl.ds((1 - from_left) * (tile_u - REACH), REACH)
        block[...] = d_out[columns]
        block_edge[...] = edge[columns]
    copy.wait()


def last_kernel(
    place_ref, even, odd, even_edge, odd_edge, taps, inner, out, padded, turned
):
    tile_v, tile_u, channels = out.shape
    sides = (even, even_edge, 0), (odd, odd_edge, 0)
    for parity in range(2):

        @pl.when(place_ref[1] == parity)
        def _(left=sides[1 - parity], right=sides[parity]):
            fill(padded, [left, right], place_ref[0], tile_v)

    def begin(tile, u, base):
        return inner[u, aligned(base, SUBLANES), aligned(tile * LANES, LANES)]

    def store(tile, u, base, value):
        turned[u, aligned(base, SUBLANES), aligned(tile * LANES, LANES)] = value

    sources = [*range(REACH), *range(REACH + tile_u, 2 * REACH + tile_u)]
    depthwise(padded, taps, begin, store, tile_u, tile_v, EDGE - REACH, sources, True)
    for u in range(tile_u):
        out[:, u, :] = turned[u]


def call(
    kernel, name, outs, scratch, scalars, arrays, flops, limit, left_in_hbm=(), anywhere=(), out_anywhere=()
):
    vmem = pl.BlockSpec(memory_space=pltpu.VMEM)
    smem = pl.BlockSpec(memory_space=pltpu.SMEM)
    hbm = pl.BlockSpec(memory_space=pltpu.HBM)
    moved = 1 if flops == 1 else sum(a.size * a.dtype.itemsize for a in [*arrays, *outs])
    arrays = [
        pltpu.with_memory_space_constraint(a, pltpu.HBM) if index in left_in_hbm else a
        for index, a in enumerate(arrays)
    ]
    free = pl.BlockSpec(memory_space=pl.ANY)
    specs = [
        hbm if index in left_in_hbm else free if index in anywhere else vmem
        for index in range(len(arrays))
    ]
    return pl.pallas_call(
        kernel,
        out_shape=tuple(outs),
        in_specs=[smem] * len(scalars) + specs,
        out_specs=tuple(free if index in out_anywhere else vmem for index in range(len(outs))),
        scratch_shapes=scratch,
        compiler_params=pltpu.CompilerParams(vmem_limit_bytes=limit << 20),
        cost_estimate=pl.CostEstimate(flops=flops, bytes_accessed=moved, transcendentals=0),
        name=name,
    )(*scalars, *arrays)


def row_pairs(odd):
    row_count = lax.axis_size("row")
    lower = range(1 if odd else 0, row_count - 1, 2)
    return [pair for r in lower for pair in ((r, r + 1), (r + 1, r))]


def facing(tile, row, odd):
    to_right = (row % 2 == 1) if odd else (row % 2 == 0)
    return lax.dynamic_slice_in_dim(
        tile, jnp.where(to_right, tile.shape[0] - REACH, 0), REACH
    )


def edge_lines(tile, core):
    return lax.dynamic_slice_in_dim(
        tile, jnp.where(core == 0, tile.shape[1] - EDGE, 0), EDGE, axis=1
    )


def across(pairs):
    return [(a * 2 + c, b * 2 + 1 - c) for a, b in pairs for c in range(2)]


def find_target(teacher, proj_weight, core, row, tile_u, tile_v):
    row_count = lax.axis_size("row")
    halves = row_count // 2
    channels = proj_weight.shape[1]
    grid_u = tile_u * row_count
    lines = teacher.shape[0] // grid_u
    scalar = core.astype(jnp.int32)[None]
    half_line = grid_u // 2
    by_half = teacher.reshape(lines, 2, half_line, teacher.shape[1])
    size = (lines * half_line, channels)
    fourth = jax.ShapeDtypeStruct((size[0] // 2, channels), jnp.bfloat16)
    upper, lower, home = call(
        project_kernel,
        "project",
        [fourth, fourth, jax.ShapeDtypeStruct(size, jnp.float32)],
        [
            pltpu.VMEM((2, lines, half_line, teacher.shape[1]), jnp.bfloat16),
            pltpu.SemaphoreType.DMA((2, COPIES)),
            pltpu.VMEM(size, jnp.float32),
            pltpu.SemaphoreType.DMA((2,)),
        ],
        [scalar], [by_half, proj_weight], 1, 16, (0,), out_anywhere=(2,),
    )
    received = [lax.ppermute(away, "col", SWAP) for away in (upper, lower)]
    turns = [lax.rem(turn + row, halves) * tile_u for turn in range(halves)]
    if lines % 16:
        received = jnp.concatenate(received).astype(jnp.float32)
        summed = (home + received).astype(jnp.bfloat16)
        by_u = summed.reshape(lines, half_line, channels).transpose(1, 0, 2)
        blocks = [lax.dynamic_slice_in_dim(by_u, turn, tile_u) for turn in turns]
    else:
        blocks = call(
            functools.partial(combine_kernel, half_line),
            "combine",
            [jax.ShapeDtypeStruct((tile_u, lines, channels), jnp.bfloat16)] * halves,
            [
                pltpu.VMEM((channels // LANES, *size[:1], LANES), jnp.float32),
                pltpu.VMEM(size, jnp.float32),
                pltpu.SemaphoreType.DMA,
            ],
            [jnp.stack(turns).astype(jnp.int32)],
            [home, *received],
            1,
            8,
            anywhere=(0,),
        )
    pieces, places = [], []
    for turn in range(halves):
        pairs = []
        for r in range(row_count):
            for c in range(2):
                goal = (halves * c + (turn + r) % halves) * 2 + r // halves
                pairs.append((r * 2 + c, goal))
        pieces.append(lax.ppermute(blocks[turn], ("row", "col"), pairs))
        places.append(lax.rem(row + (halves - turn), halves) * lines)
    places = jnp.stack(places).astype(jnp.int32)
    if lines % 16:
        whole = jnp.zeros((tile_u, tile_v, channels), jnp.bfloat16)
        for index, piece in enumerate(pieces):
            whole = lax.dynamic_update_slice_in_dim(whole, piece, places[index], axis=1)
        return [whole], jnp.zeros((1,), jnp.int32), home
    return pieces, places, home


def on_device(
    teacher,
    proj_weight,
    student,
    dw_kernel,
    dw_bias,
    norm_gain,
    norm_bias,
    w_in,
    b_in,
    w_out,
    b_out,
    layer_scale,
):
    core = lax.axis_index("col")
    row = lax.axis_index("row")
    tile_v, tile_u, channels = student.shape
    hidden = w_in.shape[1]
    tiles = channels // LANES
    wide = tile_v + 2 * EDGE
    scalar = core.astype(jnp.int32)[None]
    f32, bf16 = jnp.float32, jnp.bfloat16
    rows = tile_u * tile_v
    columns = jnp.where(row % 2 == 1, tile_u - REACH, 0)
    first_block = lax.dynamic_slice_in_dim(student, columns, REACH, axis=1).transpose(1, 0, 2)
    after_block, _ = lax.optimization_barrier((student, first_block))
    middle = after_block.transpose(1, 0, 2)
    first_side = lax.ppermute(first_block, "row", row_pairs(True))
    edge = lax.ppermute(edge_lines(middle, core), "col", SWAP)
    second_block = jnp.concatenate(
        [facing(middle, row, False), facing(edge, row, False)], axis=1
    )
    second_side = lax.ppermute(second_block, "row", row_pairs(False))
    held, *_ = lax.optimization_barrier((proj_weight, first_block, second_block))
    targets, places, home = find_target(teacher, held, core, row, tile_u, tile_v)
    later, _ = lax.optimization_barrier((dw_bias, home))
    matmul = 2 * rows * channels * hidden
    whole = (tile_u, tile_v, channels)
    summed = jax.ShapeDtypeStruct(whole, f32)
    taps = jax.ShapeDtypeStruct((TAPS * TAPS, tiles, SUBLANES, LANES), f32)
    own_pad, side_pad, rim_pad = (
        pltpu.VMEM((tiles, count, tile_v + 2 * EDGE, LANES), f32)
        for count in (tile_u, REACH, 2 * REACH)
    )
    place = jnp.stack([core, row % 2]).astype(jnp.int32)
    inner, taps = call(
        functools.partial(inner_kernel, False),
        "inner_up", [summed, taps], [own_pad], [scalar],
        [middle, edge, dw_kernel, later[None]], 1, 8,
    )
    arrived, _ = lax.optimization_barrier((first_side, inner))
    first_edge = lax.ppermute(edge_lines(arrived, core), "col", SWAP)
    (inner,) = call(
        functools.partial(side_kernel, False),
        "side_up", [summed], [side_pad], [place],
        [first_side, first_edge, taps, inner], 1, 8,
    )
    saved = call(
        up_kernel,
        "up",
        [
            jax.ShapeDtypeStruct((rows, channels), f32),
            jax.ShapeDtypeStruct((rows, LANES), f32),
            jax.ShapeDtypeStruct((rows, hidden), bf16),
            jax.ShapeDtypeStruct((rows, hidden), bf16),
        ],
        [side_pad, pltpu.VMEM(whole, f32), pltpu.VMEM((rows, channels), bf16)]
        + [pltpu.VMEM(w_in.shape, bf16), pltpu.SemaphoreType.DMA],
        [place],
        [second_side, taps, inner, norm_gain[None], norm_bias[None], w_in, b_in[None]],
        4 * matmul,
        16,
        (5,),
    )
    side, rim = (REACH, tile_v, channels), (REACH, EDGE, channels)
    sent = [side, side, (tile_u, EDGE, channels), rim, rim]
    mismatch, d_conv, even, odd, edge, even_edge, odd_edge = call(
        functools.partial(back_kernel, len(targets)),
        "back",
        [summed] + [jax.ShapeDtypeStruct(shape, bf16) for shape in (whole, *sent)],
        [
            pltpu.VMEM(whole, f32),
            pltpu.SemaphoreType.DMA,
            pltpu.VMEM(whole, bf16),
            pltpu.VMEM((rows, channels), bf16),
            pltpu.VMEM((rows, hidden), bf16),
            pltpu.VMEM((rows, channels), f32),
        ],
        [place, places],
        [middle, *saved, norm_gain[None], w_in, w_out, b_out[None], layer_scale[None], *targets],
        4 * matmul,
        16,
        out_anywhere=(0,),
    )
    even = lax.ppermute(even, "row", row_pairs(False))
    odd = lax.ppermute(odd, "row", row_pairs(True))
    edge = lax.ppermute(edge, "col", SWAP)
    even_edge = lax.ppermute(even_edge, ("row", "col"), across(row_pairs(False)))
    odd_edge = lax.ppermute(odd_edge, ("row", "col"), across(row_pairs(True)))
    (inner,) = call(
        functools.partial(inner_kernel, True),
        "inner_last", [summed],
        [own_pad, pltpu.VMEM(whole, f32), pltpu.SemaphoreType.DMA], [scalar],
        [d_conv, edge, taps, mismatch], matmul, 8, anywhere=(3,),
    )
    (grad,) = call(
        last_kernel,
        "last",
        [jax.ShapeDtypeStruct((tile_v, tile_u, channels), f32)],
        [rim_pad, pltpu.VMEM(whole, f32)],
        [place],
        [even, odd, even_edge, odd_edge, taps, inner],
        1,
        8,
    )
    return grad


def solution(mesh):
    placed = (
        P(("groups", "row"), "col"),
        P("col", None),
        P(("groups", "col"), "row", None),
        P(),
        P(),
        P(),
        P(),
        P(),
        P(),
        P(),
        P(),
        P(),
    )
    return jax.shard_map(
        on_device,
        mesh=mesh,
        in_specs=placed,
        out_specs=P(("groups", "col"), "row", None),
        check_vma=False,
    )
```

```python
import functools

import jax
import jax.numpy as jnp
from jax import lax
from jax.experimental import pallas as pl
from jax.experimental.pallas import tpu as pltpu
from jax.sharding import PartitionSpec as P

NORM_EPSILON = 1e-06
REACH = 3
TAPS = 2 * REACH + 1
LANES = 128
SUBLANES = 8
EDGE = 8
CHUNK = 16
UNROLL = 32
GROUP = 4
COPIES = 8
DOTS = 2
MLP_TILE = 512
CONTRACT_LAST = (((1,), (1,)), ((), ()))
SWAP = [(0, 1), (1, 0)]


def aligned(start, size):
    return pl.ds(pl.multiple_of(start, size), size)


def lane_tile(tile):
    return slice(tile * LANES, (tile + 1) * LANES)


def project_kernel(other, core_ref, teacher_hbm, weight, *rest):
    *outs, rows, sems = rest
    half = 1 - core_ref[0] if other else core_ref[0]
    lines, wide, depth = rows.shape
    count = next(n for n in (COPIES, 4, 2) if lines % n == 0)
    copies = []
    for index in range(count):
        here = pl.ds(index * (lines // count), lines // count)
        copy = pltpu.make_async_copy(teacher_hbm.at[here, half], rows.at[here], sems.at[index])
        copy.start()
        copies.append(copy)
    size = lines * wide // DOTS
    for index in range(DOTS):
        for copy in copies[index * count // DOTS : (index + 1) * count // DOTS]:
            copy.wait()
        here = pl.ds(index * (lines // DOTS), lines // DOTS)
        product = jnp.dot(
            rows[here].reshape(size, depth), weight[...], preferred_element_type=jnp.float32
        )
        out = outs[index * len(outs) // DOTS]
        start = index * size % out.shape[0]
        out[start : start + size] = product.astype(out.dtype)


def combine_kernel(wide, turns_ref, home, upper, lower, *rest):
    *blocks, summed = rest
    half = upper.shape[0]
    for tile in range(summed.shape[0]):
        lanes = lane_tile(tile)
        for start, received in ((0, upper), (half, lower)):
            here = slice(start, start + half)
            summed[tile, here] = home[here, lanes] + received[:, lanes].astype(jnp.float32)
    for index, block in enumerate(blocks):
        tile_u, lines, _ = block.shape
        for u in range(tile_u):
            rows = pl.ds(turns_ref[index] + u, lines, stride=wide)
            for tile in range(summed.shape[0]):
                block[u, :, lane_tile(tile)] = summed[tile, rows, :].astype(jnp.bfloat16)


def spread_taps(taps, kernel):
    for row_tap in range(TAPS):
        for col_tap in range(TAPS):
            for tile in range(taps.shape[1]):
                line = kernel[row_tap, col_tap : col_tap + 1, lane_tile(tile)]
                taps[row_tap * TAPS + col_tap, tile] = jnp.broadcast_to(line, (SUBLANES, LANES))


def spread(padded, place, part, source, start, row, count):
    for tile in range(padded.shape[0]):
        padded[tile, place, pl.ds(row, count), :] = part[
            source, pl.ds(start, count), lane_tile(tile)
        ].astype(jnp.float32)


def depthwise(padded, taps, begin, store, tile_u, count, offset, sources, flip):
    tiles = padded.shape[0]
    blocks = count // (GROUP * SUBLANES)

    def step(index, carry):
        tile = index // blocks
        base = pl.multiple_of((index % blocks) * (GROUP * SUBLANES), GROUP * SUBLANES)
        sums = [
            [begin(tile, u, base + half * SUBLANES) for u in range(tile_u)] for half in range(GROUP)
        ]
        for row_tap in range(TAPS):
            weights = []
            for col_tap in range(TAPS):
                tap = row_tap * TAPS + col_tap
                weights.append(taps[TAPS * TAPS - 1 - tap if flip else tap, tile])
            for place, source in enumerate(sources):
                for half in range(GROUP):
                    row = base + (half * SUBLANES + row_tap) + offset
                    values = padded[tile, place, pl.ds(row, SUBLANES), :]
                    for u in range(max(0, source - TAPS + 1), min(tile_u, source + 1)):
                        term = weights[source - u] * values
                        sums[half][u] = term if sums[half][u] is None else sums[half][u] + term
        for half in range(GROUP):
            for u in range(tile_u):
                store(tile, u, base + half * SUBLANES, sums[half][u])
        return carry

    lax.fori_loop(0, tiles * blocks, step, 0)


def row_parts(rows):
    half = rows // 2 // 16 * 16
    return slice(0, half), slice(half, rows)


def repeat(count, step):
    unroll = max(n for n in range(1, UNROLL + 1) if count % n == 0)

    def body(index, carry):
        step(index)
        return carry

    lax.fori_loop(0, count, body, 0, unroll=unroll)


def fill(padded, parts, core, tile_v):
    place = 0
    for part, edge, start in parts:
        for u in range(part.shape[0]):
            spread(padded, place, part, u, 0, EDGE, tile_v)
            for tile in range(padded.shape[0]):
                rim = edge[u, start : start + EDGE, lane_tile(tile)].astype(jnp.float32)
                nothing = jnp.zeros_like(rim)
                padded[tile, place, 0:EDGE, :] = jnp.where(core == 1, rim, nothing)
                padded[tile, place, EDGE + tile_v : 2 * EDGE + tile_v, :] = jnp.where(
                    core == 0, rim, nothing
                )
            place += 1


def inner_kernel(flip, core_ref, middle, edge, kernel, base_value, out, padded, taps, *fetch):
    tile_u, tile_v, channels = middle.shape
    copies = []
    if fetch:
        copies.append(pltpu.make_async_copy(base_value, *fetch))
        copies[0].start()
        base_value = fetch[0]
    spread_taps(taps, kernel)
    fill(padded, [(middle, edge, 0)], core_ref[0], tile_v)

    def place(tile, u, base):
        return u, aligned(base, SUBLANES), aligned(tile * LANES, LANES)

    def begin(tile, u, base):
        here = place(tile, u, base)
        if len(base_value.shape) == 2:
            return jnp.broadcast_to(base_value[:, here[2]], (SUBLANES, LANES))
        return base_value[here]

    def store(tile, u, base, value):
        out[place(tile, u, base)] = value

    for copy in copies:
        copy.wait()
    own = range(REACH, REACH + tile_u)
    depthwise(padded, taps, begin, store, tile_u, tile_v, EDGE - REACH, own, flip)


def side_conv(flip, core, on_left, side, edge, kernel, inner, store, padded, taps):
    tile_u, tile_v, _ = inner.shape
    spread_taps(taps, kernel)
    fill(padded, [(side, *edge)], core, tile_v)

    def begin(tile, u, base):
        return inner[u, aligned(base, SUBLANES), aligned(tile * LANES, LANES)]

    for is_left, first in ((True, 0), (False, REACH + tile_u)):
        sources = range(first, first + REACH)

        @pl.when(on_left == is_left)
        def _(sources=sources):
            depthwise(padded, taps, begin, store, tile_u, tile_v, EDGE - REACH, sources, flip)


def side_kernel(flip, place_ref, side, edge, kernel, inner, out, padded, taps):
    tile_v = inner.shape[1]

    def store(tile, u, base, value):
        out[u, aligned(base, SUBLANES), aligned(tile * LANES, LANES)] = value

    start = edge.shape[1] - EDGE
    side_conv(
        flip, place_ref[0], place_ref[1] == 0, side, (edge, start), kernel, inner, store, padded, taps
    )


def up_kernel(
    place_ref, side, kernel, inner, gain, shift, w_in_hbm, b_in,
    normal_form, inv_scale, activated, slope, padded, taps, summed, normed, w_in, sem,
):
    copy = pltpu.make_async_copy(w_in_hbm, w_in, sem)
    copy.start()
    rows, hidden = activated.shape
    _, tile_v, _ = inner.shape
    chunks = tile_v // CHUNK

    def store(tile, u, base, value):
        summed[u, aligned(base, SUBLANES), aligned(tile * LANES, LANES)] = value

    side_conv(
        False, place_ref[0], place_ref[1] == 1, side, (side, tile_v), kernel, inner, store, padded, taps
    )

    def norm_step(index):
        here = aligned(index * CHUNK, CHUNK)
        conv = summed[index // chunks, aligned((index % chunks) * CHUNK, CHUNK), :]
        centred = conv - jnp.mean(conv, axis=-1, keepdims=True)
        variance = jnp.mean(centred * centred, axis=-1, keepdims=True)
        inverse = lax.rsqrt(variance + NORM_EPSILON)
        form = centred * inverse
        normal_form[here, :] = form
        inv_scale[here, :] = jnp.broadcast_to(inverse, (CHUNK, LANES))
        normed[here, :] = (form * gain[...] + shift[...]).astype(jnp.bfloat16)

    repeat(rows // CHUNK, norm_step)

    copy.wait()
    for start in range(0, hidden, MLP_TILE):
        tile = slice(start, start + MLP_TILE)
        for here in row_parts(rows):
            pre = (
                jnp.dot(normed[here, :], w_in[:, tile], preferred_element_type=jnp.float32)
                + b_in[:, tile]
            )
            phi = 0.5 * (1.0 + lax.erf(pre * 0.7071067811865476))
            activated[here, tile] = (pre * phi).astype(jnp.bfloat16)
            rise = phi + pre * jnp.exp(-0.5 * pre * pre) * 0.3989422804014327
            slope[here, tile] = rise.astype(jnp.bfloat16)


def back_kernel(
    pieces, place_ref, places_ref, middle, normal_form, inv_scale, activated, slope,
    gain, w_in, w_out, b_out, scale, *rest,
):
    targets = rest[:pieces]
    mismatch_hbm, d_out, even, odd, edge, even_edge, odd_edge, *scratch = rest[pieces:]
    mismatch_out, sem, target, d_branch, d_hidden, d_normed = scratch
    tile_u, tile_v, channels = middle.shape
    rows, hidden = activated.shape
    chunks = tile_v // CHUNK
    for index, piece in enumerate(targets):
        target[:, aligned(places_ref[index], piece.shape[1]), :] = piece[...]

    for here in row_parts(rows):
        d_normed[here, :] = jnp.dot(
            activated[here, :], w_out[...], preferred_element_type=jnp.float32
        )

    def mismatch_step(index):
        u = index // chunks
        inside = aligned((index % chunks) * CHUNK, CHUNK)
        here = aligned(index * CHUNK, CHUNK)
        mismatch = (
            middle[u, inside, :].astype(jnp.float32)
            + scale[...] * (d_normed[here, :] + b_out[...])
            - target[u, inside, :].astype(jnp.float32)
        )
        mismatch_out[u, inside, :] = mismatch
        d_branch[here, :] = (scale[...] * mismatch).astype(jnp.bfloat16)

    repeat(tile_u * chunks, mismatch_step)
    copy = pltpu.make_async_copy(mismatch_out, mismatch_hbm, sem)
    copy.start()

    for start in range(0, hidden, MLP_TILE):
        tile = slice(start, start + MLP_TILE)
        for here in row_parts(rows):
            d_activated = lax.dot_general(
                d_branch[here, :], w_out[tile, :], CONTRACT_LAST, preferred_element_type=jnp.float32
            )
            d_hidden[here, tile] = (
                d_activated * slope[here, tile].astype(jnp.float32)
            ).astype(jnp.bfloat16)
    for here in row_parts(rows):
        d_normed[here, :] = lax.dot_general(
            d_hidden[here, :], w_in[...], CONTRACT_LAST, preferred_element_type=jnp.float32
        )

    def d_norm_step(index):
        u = index // chunks
        inside = aligned((index % chunks) * CHUNK, CHUNK)
        here = aligned(index * CHUNK, CHUNK)
        scaled = d_normed[here, :] * gain[...]
        form = normal_form[here, :]
        d_conv = inv_scale[here, :1] * (
            scaled
            - jnp.mean(scaled, axis=-1, keepdims=True)
            - form * jnp.mean(scaled * form, axis=-1, keepdims=True)
        )
        d_out[u, inside, :] = d_conv.astype(jnp.bfloat16)

    repeat(tile_u * chunks, d_norm_step)
    edge[...] = d_out[:, pl.ds(pl.multiple_of((1 - place_ref[0]) * (tile_v - EDGE), EDGE), EDGE), :]
    for block, block_edge, from_left in ((even, even_edge, place_ref[1]), (odd, odd_edge, 1 - place_ref[1])):
        columns = pl.ds((1 - from_left) * (tile_u - REACH), REACH)
        block[...] = d_out[columns]
        block_edge[...] = edge[columns]
    copy.wait()


def last_kernel(
    place_ref, even, odd, even_edge, odd_edge, kernel, inner, out, padded, taps, turned
):
    tile_v, tile_u, channels = out.shape
    spread_taps(taps, kernel)
    sides = (even, even_edge, 0), (odd, odd_edge, 0)
    for parity in range(2):

        @pl.when(place_ref[1] == parity)
        def _(left=sides[1 - parity], right=sides[parity]):
            fill(padded, [left, right], place_ref[0], tile_v)

    def begin(tile, u, base):
        return inner[u, aligned(base, SUBLANES), aligned(tile * LANES, LANES)]

    def store(tile, u, base, value):
        turned[u, aligned(base, SUBLANES), aligned(tile * LANES, LANES)] = value

    sources = [*range(REACH), *range(REACH + tile_u, 2 * REACH + tile_u)]
    depthwise(padded, taps, begin, store, tile_u, tile_v, EDGE - REACH, sources, True)
    for u in range(tile_u):
        out[:, u, :] = turned[u]


def call(
    kernel, name, outs, scratch, scalars, arrays, flops, limit, left_in_hbm=(), anywhere=(), out_anywhere=()
):
    vmem = pl.BlockSpec(memory_space=pltpu.VMEM)
    smem = pl.BlockSpec(memory_space=pltpu.SMEM)
    hbm = pl.BlockSpec(memory_space=pltpu.HBM)
    moved = 1 if flops == 1 else sum(a.size * a.dtype.itemsize for a in [*arrays, *outs])
    arrays = [
        pltpu.with_memory_space_constraint(a, pltpu.HBM) if index in left_in_hbm else a
        for index, a in enumerate(arrays)
    ]
    free = pl.BlockSpec(memory_space=pl.ANY)
    specs = [
        hbm if index in left_in_hbm else free if index in anywhere else vmem
        for index in range(len(arrays))
    ]
    return pl.pallas_call(
        kernel,
        out_shape=tuple(outs),
        in_specs=[smem] * len(scalars) + specs,
        out_specs=tuple(free if index in out_anywhere else vmem for index in range(len(outs))),
        scratch_shapes=scratch,
        compiler_params=pltpu.CompilerParams(vmem_limit_bytes=limit << 20),
        cost_estimate=pl.CostEstimate(flops=flops, bytes_accessed=moved, transcendentals=0),
        name=name,
    )(*scalars, *arrays)


def row_pairs(odd):
    row_count = lax.axis_size("row")
    lower = range(1 if odd else 0, row_count - 1, 2)
    return [pair for r in lower for pair in ((r, r + 1), (r + 1, r))]


def facing(tile, row, odd):
    to_right = (row % 2 == 1) if odd else (row % 2 == 0)
    return lax.dynamic_slice_in_dim(
        tile, jnp.where(to_right, tile.shape[0] - REACH, 0), REACH
    )


def edge_lines(tile, core):
    return lax.dynamic_slice_in_dim(
        tile, jnp.where(core == 0, tile.shape[1] - EDGE, 0), EDGE, axis=1
    )


def across(pairs):
    return [(a * 2 + c, b * 2 + 1 - c) for a, b in pairs for c in range(2)]


def find_target(teacher, proj_weight, core, row, tile_u, tile_v):
    row_count = lax.axis_size("row")
    halves = row_count // 2
    channels = proj_weight.shape[1]
    grid_u = tile_u * row_count
    lines = teacher.shape[0] // grid_u
    scalar = core.astype(jnp.int32)[None]
    half_line = grid_u // 2
    by_half = teacher.reshape(lines, 2, half_line, teacher.shape[1])
    size = (lines * half_line, channels)
    fourth = jax.ShapeDtypeStruct((size[0] // 2, channels), jnp.bfloat16)
    scratch = [
        pltpu.VMEM((lines, half_line, teacher.shape[1]), jnp.bfloat16),
        pltpu.SemaphoreType.DMA((COPIES,)),
    ]
    upper, lower = call(
        functools.partial(project_kernel, True),
        "project_away", [fourth] * 2, scratch, [scalar], [by_half, proj_weight], 1, 12, (0,),
    )
    (home,) = call(
        functools.partial(project_kernel, False),
        "project_home", [jax.ShapeDtypeStruct(size, jnp.float32)],
        scratch, [scalar], [by_half, proj_weight], 1, 12, (0,),
    )
    received = [lax.ppermute(away, "col", SWAP) for away in (upper, lower)]
    turns = [lax.rem(turn + row, halves) * tile_u for turn in range(halves)]
    if lines % 16:
        received = jnp.concatenate(received).astype(jnp.float32)
        summed = (home + received).astype(jnp.bfloat16)
        by_u = summed.reshape(lines, half_line, channels).transpose(1, 0, 2)
        blocks = [lax.dynamic_slice_in_dim(by_u, turn, tile_u) for turn in turns]
    else:
        blocks = call(
            functools.partial(combine_kernel, half_line),
            "combine",
            [jax.ShapeDtypeStruct((tile_u, lines, channels), jnp.bfloat16)] * halves,
            [pltpu.VMEM((channels // LANES, *size[:1], LANES), jnp.float32)],
            [jnp.stack(turns).astype(jnp.int32)],
            [home, *received],
            1,
            8,
        )
    pieces, places = [], []
    for turn in range(halves):
        pairs = []
        for r in range(row_count):
            for c in range(2):
                goal = (halves * c + (turn + r) % halves) * 2 + r // halves
                pairs.append((r * 2 + c, goal))
        pieces.append(lax.ppermute(blocks[turn], ("row", "col"), pairs))
        places.append(lax.rem(row + (halves - turn), halves) * lines)
    places = jnp.stack(places).astype(jnp.int32)
    if lines % 16:
        whole = jnp.zeros((tile_u, tile_v, channels), jnp.bfloat16)
        for index, piece in enumerate(pieces):
            whole = lax.dynamic_update_slice_in_dim(whole, piece, places[index], axis=1)
        return [whole], jnp.zeros((1,), jnp.int32), blocks[0]
    return pieces, places, blocks[0]


def on_device(
    teacher,
    proj_weight,
    student,
    dw_kernel,
    dw_bias,
    norm_gain,
    norm_bias,
    w_in,
    b_in,
    w_out,
    b_out,
    layer_scale,
):
    core = lax.axis_index("col")
    row = lax.axis_index("row")
    tile_v, tile_u, channels = student.shape
    hidden = w_in.shape[1]
    tiles = channels // LANES
    wide = tile_v + 2 * EDGE
    scalar = core.astype(jnp.int32)[None]
    f32, bf16 = jnp.float32, jnp.bfloat16
    rows = tile_u * tile_v
    middle = student.transpose(1, 0, 2)
    first_block = facing(middle, row, True)
    first_side = lax.ppermute(first_block, "row", row_pairs(True))
    edge = lax.ppermute(edge_lines(middle, core), "col", SWAP)
    second_block = jnp.concatenate(
        [facing(middle, row, False), facing(edge, row, False)], axis=1
    )
    second_side = lax.ppermute(second_block, "row", row_pairs(False))
    held, *_ = lax.optimization_barrier((proj_weight, first_block, second_block))
    targets, places, block = find_target(teacher, held, core, row, tile_u, tile_v)
    later, _ = lax.optimization_barrier((dw_bias, block))
    matmul = 2 * rows * channels * hidden
    whole = (tile_u, tile_v, channels)
    summed = jax.ShapeDtypeStruct(whole, f32)
    taps = pltpu.VMEM((TAPS * TAPS, tiles, SUBLANES, LANES), f32)
    own_pad, side_pad, rim_pad = (
        pltpu.VMEM((tiles, count, tile_v + 2 * EDGE, LANES), f32)
        for count in (tile_u, REACH, 2 * REACH)
    )
    place = jnp.stack([core, row % 2]).astype(jnp.int32)
    (inner,) = call(
        functools.partial(inner_kernel, False),
        "inner_up", [summed], [own_pad, taps], [scalar],
        [middle, edge, dw_kernel, later[None]], 1, 8,
    )
    arrived, _ = lax.optimization_barrier((first_side, inner))
    first_edge = lax.ppermute(edge_lines(arrived, core), "col", SWAP)
    (inner,) = call(
        functools.partial(side_kernel, False),
        "side_up", [summed], [side_pad, taps], [place],
        [first_side, first_edge, dw_kernel, inner], 1, 8,
    )
    saved = call(
        up_kernel,
        "up",
        [
            jax.ShapeDtypeStruct((rows, channels), f32),
            jax.ShapeDtypeStruct((rows, LANES), f32),
            jax.ShapeDtypeStruct((rows, hidden), bf16),
            jax.ShapeDtypeStruct((rows, hidden), bf16),
        ],
        [side_pad, taps, pltpu.VMEM(whole, f32), pltpu.VMEM((rows, channels), bf16)]
        + [pltpu.VMEM(w_in.shape, bf16), pltpu.SemaphoreType.DMA],
        [place],
        [second_side, dw_kernel, inner, norm_gain[None], norm_bias[None], w_in, b_in[None]],
        4 * matmul,
        16,
        (5,),
    )
    side, rim = (REACH, tile_v, channels), (REACH, EDGE, channels)
    sent = [side, side, (tile_u, EDGE, channels), rim, rim]
    mismatch, d_conv, even, odd, edge, even_edge, odd_edge = call(
        functools.partial(back_kernel, len(targets)),
        "back",
        [summed] + [jax.ShapeDtypeStruct(shape, bf16) for shape in (whole, *sent)],
        [
            pltpu.VMEM(whole, f32),
            pltpu.SemaphoreType.DMA,
            pltpu.VMEM(whole, bf16),
            pltpu.VMEM((rows, channels), bf16),
            pltpu.VMEM((rows, hidden), bf16),
            pltpu.VMEM((rows, channels), f32),
        ],
        [place, places],
        [middle, *saved, norm_gain[None], w_in, w_out, b_out[None], layer_scale[None], *targets],
        4 * matmul,
        16,
        out_anywhere=(0,),
    )
    even = lax.ppermute(even, "row", row_pairs(False))
    odd = lax.ppermute(odd, "row", row_pairs(True))
    edge = lax.ppermute(edge, "col", SWAP)
    even_edge = lax.ppermute(even_edge, ("row", "col"), across(row_pairs(False)))
    odd_edge = lax.ppermute(odd_edge, ("row", "col"), across(row_pairs(True)))
    (inner,) = call(
        functools.partial(inner_kernel, True),
        "inner_last", [summed],
        [own_pad, taps, pltpu.VMEM(whole, f32), pltpu.SemaphoreType.DMA], [scalar],
        [d_conv, edge, dw_kernel, mismatch], matmul, 8, anywhere=(3,),
    )
    (grad,) = call(
        last_kernel,
        "last",
        [jax.ShapeDtypeStruct((tile_v, tile_u, channels), f32)],
        [rim_pad, taps, pltpu.VMEM(whole, f32)],
        [place],
        [even, odd, even_edge, odd_edge, dw_kernel, inner],
        1,
        8,
    )
    return grad


def solution(mesh):
    placed = (
        P(("groups", "row"), "col"),
        P("col", None),
        P(("groups", "col"), "row", None),
        P(),
        P(),
        P(),
        P(),
        P(),
        P(),
        P(),
        P(),
        P(),
    )
    return jax.shard_map(
        on_device,
        mesh=mesh,
        in_specs=placed,
        out_specs=P(("groups", "col"), "row", None),
        check_vma=False,
    )
```

```python
import functools

import jax
import jax.numpy as jnp
from jax import lax
from jax.experimental import pallas as pl
from jax.experimental.pallas import tpu as pltpu
from jax.sharding import PartitionSpec as P

NORM_EPSILON = 1e-06
REACH = 3
TAPS = 2 * REACH + 1
LANES = 128
SUBLANES = 8
EDGE = 8
CHUNK = 16
UNROLL = 32
GROUP = 4
COPIES = 8
DOTS = 2
MLP_TILE = 512
CONTRACT_LAST = (((1,), (1,)), ((), ()))
SWAP = [(0, 1), (1, 0)]


def aligned(start, size):
    return pl.ds(pl.multiple_of(start, size), size)


def lane_tile(tile):
    return slice(tile * LANES, (tile + 1) * LANES)


def project_kernel(other, core_ref, teacher_hbm, weight, *rest):
    *outs, rows, sems = rest
    half = 1 - core_ref[0] if other else core_ref[0]
    lines, wide, depth = rows.shape
    count = next(n for n in (COPIES, 4, 2) if lines % n == 0)
    copies = []
    for index in range(count):
        here = pl.ds(index * (lines // count), lines // count)
        copy = pltpu.make_async_copy(teacher_hbm.at[here, half], rows.at[here], sems.at[index])
        copy.start()
        copies.append(copy)
    size = lines * wide // DOTS
    for index in range(DOTS):
        for copy in copies[index * count // DOTS : (index + 1) * count // DOTS]:
            copy.wait()
        here = pl.ds(index * (lines // DOTS), lines // DOTS)
        product = jnp.dot(
            rows[here].reshape(size, depth), weight[...], preferred_element_type=jnp.float32
        )
        out = outs[index * len(outs) // DOTS]
        start = index * size % out.shape[0]
        out[start : start + size] = product.astype(out.dtype)


def combine_kernel(wide, turns_ref, home, upper, lower, *rest):
    *blocks, summed = rest
    half = upper.shape[0]
    for tile in range(summed.shape[0]):
        lanes = lane_tile(tile)
        for start, received in ((0, upper), (half, lower)):
            here = slice(start, start + half)
            summed[tile, here] = home[here, lanes] + received[:, lanes].astype(jnp.float32)
    for index, block in enumerate(blocks):
        tile_u, lines, _ = block.shape
        for u in range(tile_u):
            rows = pl.ds(turns_ref[index] + u, lines, stride=wide)
            for tile in range(summed.shape[0]):
                block[u, :, lane_tile(tile)] = summed[tile, rows, :].astype(jnp.bfloat16)


def spread_taps(taps, kernel):
    for row_tap in range(TAPS):
        for col_tap in range(TAPS):
            for tile in range(taps.shape[1]):
                line = kernel[row_tap, col_tap : col_tap + 1, lane_tile(tile)]
                taps[row_tap * TAPS + col_tap, tile] = jnp.broadcast_to(line, (SUBLANES, LANES))


def spread(padded, place, part, source, start, row, count):
    for tile in range(padded.shape[0]):
        padded[tile, place, pl.ds(row, count), :] = part[
            source, pl.ds(start, count), lane_tile(tile)
        ].astype(jnp.float32)


def depthwise(padded, taps, begin, store, tile_u, count, offset, sources, flip):
    tiles = padded.shape[0]
    blocks = count // (GROUP * SUBLANES)

    def step(index, carry):
        tile = index // blocks
        base = pl.multiple_of((index % blocks) * (GROUP * SUBLANES), GROUP * SUBLANES)
        sums = [
            [begin(tile, u, base + half * SUBLANES) for u in range(tile_u)] for half in range(GROUP)
        ]
        for row_tap in range(TAPS):
            weights = []
            for col_tap in range(TAPS):
                tap = row_tap * TAPS + col_tap
                weights.append(taps[TAPS * TAPS - 1 - tap if flip else tap, tile])
            for place, source in enumerate(sources):
                for half in range(GROUP):
                    row = base + (half * SUBLANES + row_tap) + offset
                    values = padded[tile, place, pl.ds(row, SUBLANES), :]
                    for u in range(max(0, source - TAPS + 1), min(tile_u, source + 1)):
                        term = weights[source - u] * values
                        sums[half][u] = term if sums[half][u] is None else sums[half][u] + term
        for half in range(GROUP):
            for u in range(tile_u):
                store(tile, u, base + half * SUBLANES, sums[half][u])
        return carry

    lax.fori_loop(0, tiles * blocks, step, 0)


def row_parts(rows):
    half = rows // 2 // 16 * 16
    return slice(0, half), slice(half, rows)


def repeat(count, step):
    unroll = max(n for n in range(1, UNROLL + 1) if count % n == 0)

    def body(index, carry):
        step(index)
        return carry

    lax.fori_loop(0, count, body, 0, unroll=unroll)


def fill(padded, parts, core, tile_v):
    place = 0
    for part, edge, start in parts:
        for u in range(part.shape[0]):
            spread(padded, place, part, u, 0, EDGE, tile_v)
            for tile in range(padded.shape[0]):
                rim = edge[u, start : start + EDGE, lane_tile(tile)].astype(jnp.float32)
                nothing = jnp.zeros_like(rim)
                padded[tile, place, 0:EDGE, :] = jnp.where(core == 1, rim, nothing)
                padded[tile, place, EDGE + tile_v : 2 * EDGE + tile_v, :] = jnp.where(
                    core == 0, rim, nothing
                )
            place += 1


def inner_kernel(flip, core_ref, middle, edge, kernel, base_value, out, padded, taps, *fetch):
    tile_u, tile_v, channels = middle.shape
    copies = []
    if fetch:
        copies.append(pltpu.make_async_copy(base_value, *fetch))
        copies[0].start()
        base_value = fetch[0]
    spread_taps(taps, kernel)
    fill(padded, [(middle, edge, 0)], core_ref[0], tile_v)

    def place(tile, u, base):
        return u, aligned(base, SUBLANES), aligned(tile * LANES, LANES)

    def begin(tile, u, base):
        here = place(tile, u, base)
        if len(base_value.shape) == 2:
            return jnp.broadcast_to(base_value[:, here[2]], (SUBLANES, LANES))
        return base_value[here]

    def store(tile, u, base, value):
        out[place(tile, u, base)] = value

    for copy in copies:
        copy.wait()
    own = range(REACH, REACH + tile_u)
    depthwise(padded, taps, begin, store, tile_u, tile_v, EDGE - REACH, own, flip)


def side_conv(flip, core, on_left, side, edge, kernel, inner, store, padded, taps):
    tile_u, tile_v, _ = inner.shape
    spread_taps(taps, kernel)
    fill(padded, [(side, *edge)], core, tile_v)

    def begin(tile, u, base):
        return inner[u, aligned(base, SUBLANES), aligned(tile * LANES, LANES)]

    for is_left, first in ((True, 0), (False, REACH + tile_u)):
        sources = range(first, first + REACH)

        @pl.when(on_left == is_left)
        def _(sources=sources):
            depthwise(padded, taps, begin, store, tile_u, tile_v, EDGE - REACH, sources, flip)


def side_kernel(flip, place_ref, side, edge, kernel, inner, out, padded, taps):
    tile_v = inner.shape[1]

    def store(tile, u, base, value):
        out[u, aligned(base, SUBLANES), aligned(tile * LANES, LANES)] = value

    start = edge.shape[1] - EDGE
    side_conv(
        flip, place_ref[0], place_ref[1] == 0, side, (edge, start), kernel, inner, store, padded, taps
    )


def up_kernel(
    place_ref, side, kernel, inner, gain, shift, w_in_hbm, b_in,
    normal_form, inv_scale, activated, slope, padded, taps, summed, normed, w_in, sem,
):
    copy = pltpu.make_async_copy(w_in_hbm, w_in, sem)
    copy.start()
    rows, hidden = activated.shape
    _, tile_v, _ = inner.shape
    chunks = tile_v // CHUNK

    def store(tile, u, base, value):
        summed[u, aligned(base, SUBLANES), aligned(tile * LANES, LANES)] = value

    side_conv(
        False, place_ref[0], place_ref[1] == 1, side, (side, tile_v), kernel, inner, store, padded, taps
    )

    def norm_step(index):
        here = aligned(index * CHUNK, CHUNK)
        conv = summed[index // chunks, aligned((index % chunks) * CHUNK, CHUNK), :]
        centred = conv - jnp.mean(conv, axis=-1, keepdims=True)
        variance = jnp.mean(centred * centred, axis=-1, keepdims=True)
        inverse = lax.rsqrt(variance + NORM_EPSILON)
        form = centred * inverse
        normal_form[here, :] = form
        inv_scale[here, :] = jnp.broadcast_to(inverse, (CHUNK, LANES))
        normed[here, :] = (form * gain[...] + shift[...]).astype(jnp.bfloat16)

    repeat(rows // CHUNK, norm_step)

    copy.wait()
    for start in range(0, hidden, MLP_TILE):
        tile = slice(start, start + MLP_TILE)
        for here in row_parts(rows):
            pre = (
                jnp.dot(normed[here, :], w_in[:, tile], preferred_element_type=jnp.float32)
                + b_in[:, tile]
            )
            phi = 0.5 * (1.0 + lax.erf(pre * 0.7071067811865476))
            activated[here, tile] = (pre * phi).astype(jnp.bfloat16)
            rise = phi + pre * jnp.exp(-0.5 * pre * pre) * 0.3989422804014327
            slope[here, tile] = rise.astype(jnp.bfloat16)


def back_kernel(
    pieces, place_ref, places_ref, middle, normal_form, inv_scale, activated, slope,
    gain, w_in, w_out, b_out, scale, *rest,
):
    targets = rest[:pieces]
    mismatch_hbm, d_out, even, odd, edge, even_edge, odd_edge, *scratch = rest[pieces:]
    mismatch_out, sem, target, d_branch, d_hidden, d_normed = scratch
    tile_u, tile_v, channels = middle.shape
    rows, hidden = activated.shape
    chunks = tile_v // CHUNK
    for index, piece in enumerate(targets):
        target[:, aligned(places_ref[index], piece.shape[1]), :] = piece[...]

    for here in row_parts(rows):
        d_normed[here, :] = jnp.dot(
            activated[here, :], w_out[...], preferred_element_type=jnp.float32
        )

    def mismatch_step(index):
        u = index // chunks
        inside = aligned((index % chunks) * CHUNK, CHUNK)
        here = aligned(index * CHUNK, CHUNK)
        mismatch = (
            middle[u, inside, :].astype(jnp.float32)
            + scale[...] * (d_normed[here, :] + b_out[...])
            - target[u, inside, :].astype(jnp.float32)
        )
        mismatch_out[u, inside, :] = mismatch
        d_branch[here, :] = (scale[...] * mismatch).astype(jnp.bfloat16)

    repeat(tile_u * chunks, mismatch_step)
    copy = pltpu.make_async_copy(mismatch_out, mismatch_hbm, sem)
    copy.start()

    for start in range(0, hidden, MLP_TILE):
        tile = slice(start, start + MLP_TILE)
        for here in row_parts(rows):
            d_activated = lax.dot_general(
                d_branch[here, :], w_out[tile, :], CONTRACT_LAST, preferred_element_type=jnp.float32
            )
            d_hidden[here, tile] = (
                d_activated * slope[here, tile].astype(jnp.float32)
            ).astype(jnp.bfloat16)
    for here in row_parts(rows):
        d_normed[here, :] = lax.dot_general(
            d_hidden[here, :], w_in[...], CONTRACT_LAST, preferred_element_type=jnp.float32
        )

    def d_norm_step(index):
        u = index // chunks
        inside = aligned((index % chunks) * CHUNK, CHUNK)
        here = aligned(index * CHUNK, CHUNK)
        scaled = d_normed[here, :] * gain[...]
        form = normal_form[here, :]
        d_conv = inv_scale[here, :1] * (
            scaled
            - jnp.mean(scaled, axis=-1, keepdims=True)
            - form * jnp.mean(scaled * form, axis=-1, keepdims=True)
        )
        d_out[u, inside, :] = d_conv.astype(jnp.bfloat16)

    repeat(tile_u * chunks, d_norm_step)
    edge[...] = d_out[:, pl.ds(pl.multiple_of((1 - place_ref[0]) * (tile_v - EDGE), EDGE), EDGE), :]
    for block, block_edge, from_left in ((even, even_edge, place_ref[1]), (odd, odd_edge, 1 - place_ref[1])):
        columns = pl.ds((1 - from_left) * (tile_u - REACH), REACH)
        block[...] = d_out[columns]
        block_edge[...] = edge[columns]
    copy.wait()


def last_kernel(
    place_ref, even, odd, even_edge, odd_edge, kernel, inner, out,
    padded, taps, turned, staged, sems,
):
    tile_v, tile_u, channels = out.shape
    spread_taps(taps, kernel)
    sides = (even, even_edge, 0), (odd, odd_edge, 0)
    for parity in range(2):

        @pl.when(place_ref[1] == parity)
        def _(left=sides[1 - parity], right=sides[parity]):
            fill(padded, [left, right], place_ref[0], tile_v)

    sources = [*range(REACH), *range(REACH + tile_u, 2 * REACH + tile_u)]
    lines = GROUP * SUBLANES
    copies = []
    for first in range(0, tile_v, lines):

        def place(tile, u, base, first=first):
            return u, aligned(first + base, SUBLANES), aligned(tile * LANES, LANES)

        def begin(tile, u, base, place=place):
            return inner[place(tile, u, base)]

        def store(tile, u, base, value, place=place):
            turned[place(tile, u, base)] = value

        offset = first + EDGE - REACH
        depthwise(padded, taps, begin, store, tile_u, lines, offset, sources, True)
        here = pl.ds(first, lines)
        for u in range(tile_u):
            staged[here, u, :] = turned[u, here, :]
        copies.append(
            pltpu.make_async_copy(staged.at[here], out.at[here], sems.at[first // lines])
        )
        copies[-1].start()
    for copy in copies:
        copy.wait()


def call(
    kernel, name, outs, scratch, scalars, arrays, flops, limit, left_in_hbm=(), anywhere=(), out_anywhere=()
):
    vmem = pl.BlockSpec(memory_space=pltpu.VMEM)
    smem = pl.BlockSpec(memory_space=pltpu.SMEM)
    hbm = pl.BlockSpec(memory_space=pltpu.HBM)
    moved = 1 if flops == 1 else sum(a.size * a.dtype.itemsize for a in [*arrays, *outs])
    arrays = [
        pltpu.with_memory_space_constraint(a, pltpu.HBM) if index in left_in_hbm else a
        for index, a in enumerate(arrays)
    ]
    free = pl.BlockSpec(memory_space=pl.ANY)
    specs = [
        hbm if index in left_in_hbm else free if index in anywhere else vmem
        for index in range(len(arrays))
    ]
    return pl.pallas_call(
        kernel,
        out_shape=tuple(outs),
        in_specs=[smem] * len(scalars) + specs,
        out_specs=tuple(free if index in out_anywhere else vmem for index in range(len(outs))),
        scratch_shapes=scratch,
        compiler_params=pltpu.CompilerParams(vmem_limit_bytes=limit << 20),
        cost_estimate=pl.CostEstimate(flops=flops, bytes_accessed=moved, transcendentals=0),
        name=name,
    )(*scalars, *arrays)


def row_pairs(odd):
    row_count = lax.axis_size("row")
    lower = range(1 if odd else 0, row_count - 1, 2)
    return [pair for r in lower for pair in ((r, r + 1), (r + 1, r))]


def facing(tile, row, odd):
    to_right = (row % 2 == 1) if odd else (row % 2 == 0)
    return lax.dynamic_slice_in_dim(
        tile, jnp.where(to_right, tile.shape[0] - REACH, 0), REACH
    )


def edge_lines(tile, core):
    return lax.dynamic_slice_in_dim(
        tile, jnp.where(core == 0, tile.shape[1] - EDGE, 0), EDGE, axis=1
    )


def across(pairs):
    return [(a * 2 + c, b * 2 + 1 - c) for a, b in pairs for c in range(2)]


def find_target(teacher, proj_weight, core, row, tile_u, tile_v):
    row_count = lax.axis_size("row")
    halves = row_count // 2
    channels = proj_weight.shape[1]
    grid_u = tile_u * row_count
    lines = teacher.shape[0] // grid_u
    scalar = core.astype(jnp.int32)[None]
    half_line = grid_u // 2
    by_half = teacher.reshape(lines, 2, half_line, teacher.shape[1])
    size = (lines * half_line, channels)
    fourth = jax.ShapeDtypeStruct((size[0] // 2, channels), jnp.bfloat16)
    scratch = [
        pltpu.VMEM((lines, half_line, teacher.shape[1]), jnp.bfloat16),
        pltpu.SemaphoreType.DMA((COPIES,)),
    ]
    upper, lower = call(
        functools.partial(project_kernel, True),
        "project_away", [fourth] * 2, scratch, [scalar], [by_half, proj_weight], 1, 12, (0,),
    )
    (home,) = call(
        functools.partial(project_kernel, False),
        "project_home", [jax.ShapeDtypeStruct(size, jnp.float32)],
        scratch, [scalar], [by_half, proj_weight], 1, 12, (0,),
    )
    received = [lax.ppermute(away, "col", SWAP) for away in (upper, lower)]
    turns = [lax.rem(turn + row, halves) * tile_u for turn in range(halves)]
    if lines % 16:
        received = jnp.concatenate(received).astype(jnp.float32)
        summed = (home + received).astype(jnp.bfloat16)
        by_u = summed.reshape(lines, half_line, channels).transpose(1, 0, 2)
        blocks = [lax.dynamic_slice_in_dim(by_u, turn, tile_u) for turn in turns]
    else:
        blocks = call(
            functools.partial(combine_kernel, half_line),
            "combine",
            [jax.ShapeDtypeStruct((tile_u, lines, channels), jnp.bfloat16)] * halves,
            [pltpu.VMEM((channels // LANES, *size[:1], LANES), jnp.float32)],
            [jnp.stack(turns).astype(jnp.int32)],
            [home, *received],
            1,
            8,
        )
    pieces, places = [], []
    for turn in range(halves):
        pairs = []
        for r in range(row_count):
            for c in range(2):
                goal = (halves * c + (turn + r) % halves) * 2 + r // halves
                pairs.append((r * 2 + c, goal))
        pieces.append(lax.ppermute(blocks[turn], ("row", "col"), pairs))
        places.append(lax.rem(row + (halves - turn), halves) * lines)
    places = jnp.stack(places).astype(jnp.int32)
    if lines % 16:
        whole = jnp.zeros((tile_u, tile_v, channels), jnp.bfloat16)
        for index, piece in enumerate(pieces):
            whole = lax.dynamic_update_slice_in_dim(whole, piece, places[index], axis=1)
        return [whole], jnp.zeros((1,), jnp.int32), blocks[0]
    return pieces, places, blocks[0]


def on_device(
    teacher,
    proj_weight,
    student,
    dw_kernel,
    dw_bias,
    norm_gain,
    norm_bias,
    w_in,
    b_in,
    w_out,
    b_out,
    layer_scale,
):
    core = lax.axis_index("col")
    row = lax.axis_index("row")
    tile_v, tile_u, channels = student.shape
    hidden = w_in.shape[1]
    tiles = channels // LANES
    wide = tile_v + 2 * EDGE
    scalar = core.astype(jnp.int32)[None]
    f32, bf16 = jnp.float32, jnp.bfloat16
    rows = tile_u * tile_v
    middle = student.transpose(1, 0, 2)
    first_block = facing(middle, row, True)
    first_side = lax.ppermute(first_block, "row", row_pairs(True))
    edge = lax.ppermute(edge_lines(middle, core), "col", SWAP)
    second_block = jnp.concatenate(
        [facing(middle, row, False), facing(edge, row, False)], axis=1
    )
    second_side = lax.ppermute(second_block, "row", row_pairs(False))
    held, *_ = lax.optimization_barrier((proj_weight, first_block, second_block))
    targets, places, block = find_target(teacher, held, core, row, tile_u, tile_v)
    later, _ = lax.optimization_barrier((dw_bias, block))
    matmul = 2 * rows * channels * hidden
    whole = (tile_u, tile_v, channels)
    summed = jax.ShapeDtypeStruct(whole, f32)
    taps = pltpu.VMEM((TAPS * TAPS, tiles, SUBLANES, LANES), f32)
    own_pad, side_pad, rim_pad = (
        pltpu.VMEM((tiles, count, tile_v + 2 * EDGE, LANES), f32)
        for count in (tile_u, REACH, 2 * REACH)
    )
    place = jnp.stack([core, row % 2]).astype(jnp.int32)
    (inner,) = call(
        functools.partial(inner_kernel, False),
        "inner_up", [summed], [own_pad, taps], [scalar],
        [middle, edge, dw_kernel, later[None]], 1, 8,
    )
    arrived, _ = lax.optimization_barrier((first_side, inner))
    first_edge = lax.ppermute(edge_lines(arrived, core), "col", SWAP)
    (inner,) = call(
        functools.partial(side_kernel, False),
        "side_up", [summed], [side_pad, taps], [place],
        [first_side, first_edge, dw_kernel, inner], 1, 8,
    )
    saved = call(
        up_kernel,
        "up",
        [
            jax.ShapeDtypeStruct((rows, channels), f32),
            jax.ShapeDtypeStruct((rows, LANES), f32),
            jax.ShapeDtypeStruct((rows, hidden), bf16),
            jax.ShapeDtypeStruct((rows, hidden), bf16),
        ],
        [side_pad, taps, pltpu.VMEM(whole, f32), pltpu.VMEM((rows, channels), bf16)]
        + [pltpu.VMEM(w_in.shape, bf16), pltpu.SemaphoreType.DMA],
        [place],
        [second_side, dw_kernel, inner, norm_gain[None], norm_bias[None], w_in, b_in[None]],
        4 * matmul,
        16,
        (5,),
    )
    side, rim = (REACH, tile_v, channels), (REACH, EDGE, channels)
    sent = [side, side, (tile_u, EDGE, channels), rim, rim]
    mismatch, d_conv, even, odd, edge, even_edge, odd_edge = call(
        functools.partial(back_kernel, len(targets)),
        "back",
        [summed] + [jax.ShapeDtypeStruct(shape, bf16) for shape in (whole, *sent)],
        [
            pltpu.VMEM(whole, f32),
            pltpu.SemaphoreType.DMA,
            pltpu.VMEM(whole, bf16),
            pltpu.VMEM((rows, channels), bf16),
            pltpu.VMEM((rows, hidden), bf16),
            pltpu.VMEM((rows, channels), f32),
        ],
        [place, places],
        [middle, *saved, norm_gain[None], w_in, w_out, b_out[None], layer_scale[None], *targets],
        4 * matmul,
        16,
        out_anywhere=(0,),
    )
    even = lax.ppermute(even, "row", row_pairs(False))
    odd = lax.ppermute(odd, "row", row_pairs(True))
    edge = lax.ppermute(edge, "col", SWAP)
    even_edge = lax.ppermute(even_edge, ("row", "col"), across(row_pairs(False)))
    odd_edge = lax.ppermute(odd_edge, ("row", "col"), across(row_pairs(True)))
    (inner,) = call(
        functools.partial(inner_kernel, True),
        "inner_last", [summed],
        [own_pad, taps, pltpu.VMEM(whole, f32), pltpu.SemaphoreType.DMA], [scalar],
        [d_conv, edge, dw_kernel, mismatch], matmul, 8, anywhere=(3,),
    )
    (grad,) = call(
        last_kernel,
        "last",
        [jax.ShapeDtypeStruct((tile_v, tile_u, channels), f32)],
        [rim_pad, taps, pltpu.VMEM(whole, f32), pltpu.VMEM((tile_v, tile_u, channels), f32)]
        + [pltpu.SemaphoreType.DMA((tile_v // (GROUP * SUBLANES),))],
        [place],
        [even, odd, even_edge, odd_edge, dw_kernel, inner],
        1,
        10,
        out_anywhere=(0,),
    )
    return grad


def solution(mesh):
    placed = (
        P(("groups", "row"), "col"),
        P("col", None),
        P(("groups", "col"), "row", None),
        P(),
        P(),
        P(),
        P(),
        P(),
        P(),
        P(),
        P(),
        P(),
    )
    return jax.shard_map(
        on_device,
        mesh=mesh,
        in_specs=placed,
        out_specs=P(("groups", "col"), "row", None),
        check_vma=False,
    )
```

```python
import functools

import jax
import jax.numpy as jnp
from jax import lax
from jax.experimental import pallas as pl
from jax.experimental.pallas import tpu as pltpu
from jax.sharding import PartitionSpec as P

NORM_EPSILON = 1e-06
REACH = 3
TAPS = 2 * REACH + 1
LANES = 128
SUBLANES = 8
EDGE = 8
CHUNK = 16
UNROLL = 32
GROUP = 4
COPIES = 8
MLP_TILE = 512
CONTRACT_LAST = (((1,), (1,)), ((), ()))
SWAP = [(0, 1), (1, 0)]


def aligned(start, size):
    return pl.ds(pl.multiple_of(start, size), size)


def lane_tile(tile):
    return slice(tile * LANES, (tile + 1) * LANES)


def project_kernel(other, core_ref, teacher_hbm, weight, *rest):
    *outs, rows, sems = rest
    half = 1 - core_ref[0] if other else core_ref[0]
    lines, wide, depth = rows.shape
    count = next(n for n in (COPIES, 4, 2) if lines % n == 0)
    copies = []
    for index in range(count):
        here = pl.ds(index * (lines // count), lines // count)
        copy = pltpu.make_async_copy(teacher_hbm.at[here, half], rows.at[here], sems.at[index])
        copy.start()
        copies.append(copy)
    done = 0
    for out in outs:
        taken = out.shape[0] // wide
        parts = 2 if len(outs) == 1 else 1
        for part in range(parts):
            here = pl.ds(done + part * (taken // parts), taken // parts)
            last = pl.cdiv((done + (part + 1) * (taken // parts)) * count, lines)
            while copies and len(copies) > count - last:
                copies.pop(0).wait()
            size = taken // parts * wide
            product = jnp.dot(
                rows[here].reshape(size, depth), weight[...], preferred_element_type=jnp.float32
            )
            out[part * size : (part + 1) * size] = product.astype(out.dtype)
        done += taken


def combine_kernel(wide, turns_ref, home, first, second, third, *rest):
    *blocks, summed = rest
    for tile in range(summed.shape[0]):
        lanes = lane_tile(tile)
        start = 0
        for received in (first, second, third):
            here = slice(start, start + received.shape[0])
            start += received.shape[0]
            summed[tile, here] = home[here, lanes] + received[:, lanes].astype(jnp.float32)
    for index, block in enumerate(blocks):
        tile_u, lines, _ = block.shape
        for u in range(tile_u):
            rows = pl.ds(turns_ref[index] + u, lines, stride=wide)
            for tile in range(summed.shape[0]):
                block[u, :, lane_tile(tile)] = summed[tile, rows, :].astype(jnp.bfloat16)


def spread_taps(taps, kernel):
    for row_tap in range(TAPS):
        for col_tap in range(TAPS):
            for tile in range(taps.shape[1]):
                line = kernel[row_tap, col_tap : col_tap + 1, lane_tile(tile)]
                taps[row_tap * TAPS + col_tap, tile] = jnp.broadcast_to(line, (SUBLANES, LANES))


def spread(padded, place, part, source, start, row, count):
    for tile in range(padded.shape[0]):
        padded[tile, place, pl.ds(row, count), :] = part[
            source, pl.ds(start, count), lane_tile(tile)
        ].astype(jnp.float32)


def depthwise(padded, taps, begin, store, tile_u, count, offset, sources, flip):
    tiles = padded.shape[0]
    blocks = count // (GROUP * SUBLANES)

    def step(index, carry):
        tile = index // blocks
        base = pl.multiple_of((index % blocks) * (GROUP * SUBLANES), GROUP * SUBLANES)
        sums = [
            [begin(tile, u, base + half * SUBLANES) for u in range(tile_u)] for half in range(GROUP)
        ]
        for row_tap in range(TAPS):
            weights = []
            for col_tap in range(TAPS):
                tap = row_tap * TAPS + col_tap
                weights.append(taps[TAPS * TAPS - 1 - tap if flip else tap, tile])
            for place, source in enumerate(sources):
                for half in range(GROUP):
                    row = base + (half * SUBLANES + row_tap) + offset
                    values = padded[tile, place, pl.ds(row, SUBLANES), :]
                    for u in range(max(0, source - TAPS + 1), min(tile_u, source + 1)):
                        term = weights[source - u] * values
                        sums[half][u] = term if sums[half][u] is None else sums[half][u] + term
        for half in range(GROUP):
            for u in range(tile_u):
                store(tile, u, base + half * SUBLANES, sums[half][u])
        return carry

    lax.fori_loop(0, tiles * blocks, step, 0)


def row_parts(rows):
    half = rows // 2 // 16 * 16
    return slice(0, half), slice(half, rows)


def repeat(count, step):
    unroll = max(n for n in range(1, UNROLL + 1) if count % n == 0)

    def body(index, carry):
        step(index)
        return carry

    lax.fori_loop(0, count, body, 0, unroll=unroll)


def fill(padded, parts, core, tile_v):
    place = 0
    for part, edge, start in parts:
        for u in range(part.shape[0]):
            spread(padded, place, part, u, 0, EDGE, tile_v)
            for tile in range(padded.shape[0]):
                rim = edge[u, start : start + EDGE, lane_tile(tile)].astype(jnp.float32)
                nothing = jnp.zeros_like(rim)
                padded[tile, place, 0:EDGE, :] = jnp.where(core == 1, rim, nothing)
                padded[tile, place, EDGE + tile_v : 2 * EDGE + tile_v, :] = jnp.where(
                    core == 0, rim, nothing
                )
            place += 1


def inner_kernel(flip, core_ref, middle, edge, kernel, base_value, out, padded, taps, *fetch):
    tile_u, tile_v, channels = middle.shape
    copies = []
    if fetch:
        copies.append(pltpu.make_async_copy(base_value, *fetch))
        copies[0].start()
        base_value = fetch[0]
    spread_taps(taps, kernel)
    fill(padded, [(middle, edge, 0)], core_ref[0], tile_v)

    def place(tile, u, base):
        return u, aligned(base, SUBLANES), aligned(tile * LANES, LANES)

    def begin(tile, u, base):
        here = place(tile, u, base)
        if len(base_value.shape) == 2:
            return jnp.broadcast_to(base_value[:, here[2]], (SUBLANES, LANES))
        return base_value[here]

    def store(tile, u, base, value):
        out[place(tile, u, base)] = value

    for copy in copies:
        copy.wait()
    own = range(REACH, REACH + tile_u)
    depthwise(padded, taps, begin, store, tile_u, tile_v, EDGE - REACH, own, flip)


def side_conv(flip, core, on_left, side, edge, kernel, inner, store, padded, taps):
    tile_u, tile_v, _ = inner.shape
    spread_taps(taps, kernel)
    fill(padded, [(side, *edge)], core, tile_v)

    def begin(tile, u, base):
        return inner[u, aligned(base, SUBLANES), aligned(tile * LANES, LANES)]

    for is_left, first in ((True, 0), (False, REACH + tile_u)):
        sources = range(first, first + REACH)

        @pl.when(on_left == is_left)
        def _(sources=sources):
            depthwise(padded, taps, begin, store, tile_u, tile_v, EDGE - REACH, sources, flip)


def side_kernel(flip, place_ref, side, edge, kernel, inner, out, padded, taps):
    tile_v = inner.shape[1]

    def store(tile, u, base, value):
        out[u, aligned(base, SUBLANES), aligned(tile * LANES, LANES)] = value

    start = edge.shape[1] - EDGE
    side_conv(
        flip, place_ref[0], place_ref[1] == 0, side, (edge, start), kernel, inner, store, padded, taps
    )


def up_kernel(
    place_ref, side, kernel, inner, gain, shift, w_in_hbm, b_in,
    normal_form, inv_scale, activated, slope, padded, taps, summed, normed, w_in, sem,
):
    copy = pltpu.make_async_copy(w_in_hbm, w_in, sem)
    copy.start()
    rows, hidden = activated.shape
    _, tile_v, _ = inner.shape
    chunks = tile_v // CHUNK

    def store(tile, u, base, value):
        summed[u, aligned(base, SUBLANES), aligned(tile * LANES, LANES)] = value

    side_conv(
        False, place_ref[0], place_ref[1] == 1, side, (side, tile_v), kernel, inner, store, padded, taps
    )

    def norm_step(index):
        here = aligned(index * CHUNK, CHUNK)
        conv = summed[index // chunks, aligned((index % chunks) * CHUNK, CHUNK), :]
        centred = conv - jnp.mean(conv, axis=-1, keepdims=True)
        variance = jnp.mean(centred * centred, axis=-1, keepdims=True)
        inverse = lax.rsqrt(variance + NORM_EPSILON)
        form = centred * inverse
        normal_form[here, :] = form
        inv_scale[here, :] = jnp.broadcast_to(inverse, (CHUNK, LANES))
        normed[here, :] = (form * gain[...] + shift[...]).astype(jnp.bfloat16)

    repeat(rows // CHUNK, norm_step)

    copy.wait()
    for start in range(0, hidden, MLP_TILE):
        tile = slice(start, start + MLP_TILE)
        for here in row_parts(rows):
            pre = (
                jnp.dot(normed[here, :], w_in[:, tile], preferred_element_type=jnp.float32)
                + b_in[:, tile]
            )
            phi = 0.5 * (1.0 + lax.erf(pre * 0.7071067811865476))
            activated[here, tile] = (pre * phi).astype(jnp.bfloat16)
            rise = phi + pre * jnp.exp(-0.5 * pre * pre) * 0.3989422804014327
            slope[here, tile] = rise.astype(jnp.bfloat16)


def back_kernel(
    pieces, place_ref, places_ref, middle, normal_form, inv_scale, activated, slope,
    gain, w_in, w_out, b_out, scale, *rest,
):
    targets = rest[:pieces]
    mismatch_hbm, d_out, even, odd, edge, even_edge, odd_edge, *scratch = rest[pieces:]
    mismatch_out, sem, target, d_branch, d_hidden, d_normed = scratch
    tile_u, tile_v, channels = middle.shape
    rows, hidden = activated.shape
    chunks = tile_v // CHUNK
    for index, piece in enumerate(targets):
        target[:, aligned(places_ref[index], piece.shape[1]), :] = piece[...]

    for here in row_parts(rows):
        d_normed[here, :] = jnp.dot(
            activated[here, :], w_out[...], preferred_element_type=jnp.float32
        )

    def mismatch_step(index):
        u = index // chunks
        inside = aligned((index % chunks) * CHUNK, CHUNK)
        here = aligned(index * CHUNK, CHUNK)
        mismatch = (
            middle[u, inside, :].astype(jnp.float32)
            + scale[...] * (d_normed[here, :] + b_out[...])
            - target[u, inside, :].astype(jnp.float32)
        )
        mismatch_out[u, inside, :] = mismatch
        d_branch[here, :] = (scale[...] * mismatch).astype(jnp.bfloat16)

    repeat(tile_u * chunks, mismatch_step)
    copy = pltpu.make_async_copy(mismatch_out, mismatch_hbm, sem)
    copy.start()

    for start in range(0, hidden, MLP_TILE):
        tile = slice(start, start + MLP_TILE)
        for here in row_parts(rows):
            d_activated = lax.dot_general(
                d_branch[here, :], w_out[tile, :], CONTRACT_LAST, preferred_element_type=jnp.float32
            )
            d_hidden[here, tile] = (
                d_activated * slope[here, tile].astype(jnp.float32)
            ).astype(jnp.bfloat16)
    for here in row_parts(rows):
        d_normed[here, :] = lax.dot_general(
            d_hidden[here, :], w_in[...], CONTRACT_LAST, preferred_element_type=jnp.float32
        )

    def d_norm_step(index):
        u = index // chunks
        inside = aligned((index % chunks) * CHUNK, CHUNK)
        here = aligned(index * CHUNK, CHUNK)
        scaled = d_normed[here, :] * gain[...]
        form = normal_form[here, :]
        d_conv = inv_scale[here, :1] * (
            scaled
            - jnp.mean(scaled, axis=-1, keepdims=True)
            - form * jnp.mean(scaled * form, axis=-1, keepdims=True)
        )
        d_out[u, inside, :] = d_conv.astype(jnp.bfloat16)

    repeat(tile_u * chunks, d_norm_step)
    edge[...] = d_out[:, pl.ds(pl.multiple_of((1 - place_ref[0]) * (tile_v - EDGE), EDGE), EDGE), :]
    for block, block_edge, from_left in ((even, even_edge, place_ref[1]), (odd, odd_edge, 1 - place_ref[1])):
        columns = pl.ds((1 - from_left) * (tile_u - REACH), REACH)
        block[...] = d_out[columns]
        block_edge[...] = edge[columns]
    copy.wait()


def last_kernel(
    place_ref, even, odd, even_edge, odd_edge, kernel, inner, out,
    padded, taps, turned, staged, sems,
):
    tile_v, tile_u, channels = out.shape
    spread_taps(taps, kernel)
    sides = (even, even_edge, 0), (odd, odd_edge, 0)
    for parity in range(2):

        @pl.when(place_ref[1] == parity)
        def _(left=sides[1 - parity], right=sides[parity]):
            fill(padded, [left, right], place_ref[0], tile_v)

    sources = [*range(REACH), *range(REACH + tile_u, 2 * REACH + tile_u)]
    lines = GROUP * SUBLANES
    copies = []
    for first in range(0, tile_v, lines):

        def place(tile, u, base, first=first):
            return u, aligned(first + base, SUBLANES), aligned(tile * LANES, LANES)

        def begin(tile, u, base, place=place):
            return inner[place(tile, u, base)]

        def store(tile, u, base, value, place=place):
            turned[place(tile, u, base)] = value

        offset = first + EDGE - REACH
        depthwise(padded, taps, begin, store, tile_u, lines, offset, sources, True)
        here = pl.ds(first, lines)
        for u in range(tile_u):
            staged[here, u, :] = turned[u, here, :]
        copies.append(
            pltpu.make_async_copy(staged.at[here], out.at[here], sems.at[first // lines])
        )
        copies[-1].start()
    for copy in copies:
        copy.wait()


def call(
    kernel, name, outs, scratch, scalars, arrays, flops, limit, left_in_hbm=(), anywhere=(), out_anywhere=()
):
    vmem = pl.BlockSpec(memory_space=pltpu.VMEM)
    smem = pl.BlockSpec(memory_space=pltpu.SMEM)
    hbm = pl.BlockSpec(memory_space=pltpu.HBM)
    moved = 1 if flops == 1 else sum(a.size * a.dtype.itemsize for a in [*arrays, *outs])
    arrays = [
        pltpu.with_memory_space_constraint(a, pltpu.HBM) if index in left_in_hbm else a
        for index, a in enumerate(arrays)
    ]
    free = pl.BlockSpec(memory_space=pl.ANY)
    specs = [
        hbm if index in left_in_hbm else free if index in anywhere else vmem
        for index in range(len(arrays))
    ]
    return pl.pallas_call(
        kernel,
        out_shape=tuple(outs),
        in_specs=[smem] * len(scalars) + specs,
        out_specs=tuple(free if index in out_anywhere else vmem for index in range(len(outs))),
        scratch_shapes=scratch,
        compiler_params=pltpu.CompilerParams(vmem_limit_bytes=limit << 20),
        cost_estimate=pl.CostEstimate(flops=flops, bytes_accessed=moved, transcendentals=0),
        name=name,
    )(*scalars, *arrays)


def row_pairs(odd):
    row_count = lax.axis_size("row")
    lower = range(1 if odd else 0, row_count - 1, 2)
    return [pair for r in lower for pair in ((r, r + 1), (r + 1, r))]


def facing(tile, row, odd):
    to_right = (row % 2 == 1) if odd else (row % 2 == 0)
    return lax.dynamic_slice_in_dim(
        tile, jnp.where(to_right, tile.shape[0] - REACH, 0), REACH
    )


def edge_lines(tile, core):
    return lax.dynamic_slice_in_dim(
        tile, jnp.where(core == 0, tile.shape[1] - EDGE, 0), EDGE, axis=1
    )


def across(pairs):
    return [(a * 2 + c, b * 2 + 1 - c) for a, b in pairs for c in range(2)]


def find_target(teacher, proj_weight, core, row, tile_u, tile_v):
    row_count = lax.axis_size("row")
    halves = row_count // 2
    channels = proj_weight.shape[1]
    grid_u = tile_u * row_count
    lines = teacher.shape[0] // grid_u
    scalar = core.astype(jnp.int32)[None]
    half_line = grid_u // 2
    by_half = teacher.reshape(lines, 2, half_line, teacher.shape[1])
    size = (lines * half_line, channels)
    third = lines // 3
    pieces = [
        jax.ShapeDtypeStruct((part * half_line, channels), jnp.bfloat16)
        for part in (lines - 2 * third, third, third)
    ]
    scratch = [
        pltpu.VMEM((lines, half_line, teacher.shape[1]), jnp.bfloat16),
        pltpu.SemaphoreType.DMA((COPIES,)),
    ]
    aways = call(
        functools.partial(project_kernel, True),
        "project_away", pieces, scratch, [scalar], [by_half, proj_weight], 1, 12, (0,),
    )
    (home,) = call(
        functools.partial(project_kernel, False),
        "project_home", [jax.ShapeDtypeStruct(size, jnp.float32)],
        scratch, [scalar], [by_half, proj_weight], 1, 12, (0,),
    )
    received = [lax.ppermute(away, "col", SWAP) for away in aways]
    turns = [lax.rem(turn + row, halves) * tile_u for turn in range(halves)]
    if lines % 16:
        received = jnp.concatenate(received).astype(jnp.float32)
        summed = (home + received).astype(jnp.bfloat16)
        by_u = summed.reshape(lines, half_line, channels).transpose(1, 0, 2)
        blocks = [lax.dynamic_slice_in_dim(by_u, turn, tile_u) for turn in turns]
    else:
        blocks = call(
            functools.partial(combine_kernel, half_line),
            "combine",
            [jax.ShapeDtypeStruct((tile_u, lines, channels), jnp.bfloat16)] * halves,
            [pltpu.VMEM((channels // LANES, *size[:1], LANES), jnp.float32)],
            [jnp.stack(turns).astype(jnp.int32)],
            [home, *received],
            1,
            8,
        )
    pieces, places = [], []
    for turn in range(halves):
        pairs = []
        for r in range(row_count):
            for c in range(2):
                goal = (halves * c + (turn + r) % halves) * 2 + r // halves
                pairs.append((r * 2 + c, goal))
        pieces.append(lax.ppermute(blocks[turn], ("row", "col"), pairs))
        places.append(lax.rem(row + (halves - turn), halves) * lines)
    places = jnp.stack(places).astype(jnp.int32)
    if lines % 16:
        whole = jnp.zeros((tile_u, tile_v, channels), jnp.bfloat16)
        for index, piece in enumerate(pieces):
            whole = lax.dynamic_update_slice_in_dim(whole, piece, places[index], axis=1)
        return [whole], jnp.zeros((1,), jnp.int32), blocks[0]
    return pieces, places, blocks[0]


def on_device(
    teacher,
    proj_weight,
    student,
    dw_kernel,
    dw_bias,
    norm_gain,
    norm_bias,
    w_in,
    b_in,
    w_out,
    b_out,
    layer_scale,
):
    core = lax.axis_index("col")
    row = lax.axis_index("row")
    tile_v, tile_u, channels = student.shape
    hidden = w_in.shape[1]
    tiles = channels // LANES
    wide = tile_v + 2 * EDGE
    scalar = core.astype(jnp.int32)[None]
    f32, bf16 = jnp.float32, jnp.bfloat16
    rows = tile_u * tile_v
    middle = student.transpose(1, 0, 2)
    first_block = facing(middle, row, True)
    first_side = lax.ppermute(first_block, "row", row_pairs(True))
    edge = lax.ppermute(edge_lines(middle, core), "col", SWAP)
    second_block = jnp.concatenate(
        [facing(middle, row, False), facing(edge, row, False)], axis=1
    )
    second_side = lax.ppermute(second_block, "row", row_pairs(False))
    held, *_ = lax.optimization_barrier((proj_weight, first_block, second_block))
    targets, places, block = find_target(teacher, held, core, row, tile_u, tile_v)
    later, _ = lax.optimization_barrier((dw_bias, block))
    matmul = 2 * rows * channels * hidden
    whole = (tile_u, tile_v, channels)
    summed = jax.ShapeDtypeStruct(whole, f32)
    taps = pltpu.VMEM((TAPS * TAPS, tiles, SUBLANES, LANES), f32)
    own_pad, side_pad, rim_pad = (
        pltpu.VMEM((tiles, count, tile_v + 2 * EDGE, LANES), f32)
        for count in (tile_u, REACH, 2 * REACH)
    )
    place = jnp.stack([core, row % 2]).astype(jnp.int32)
    (inner,) = call(
        functools.partial(inner_kernel, False),
        "inner_up", [summed], [own_pad, taps], [scalar],
        [middle, edge, dw_kernel, later[None]], 1, 8,
    )
    arrived, _ = lax.optimization_barrier((first_side, inner))
    first_edge = lax.ppermute(edge_lines(arrived, core), "col", SWAP)
    (inner,) = call(
        functools.partial(side_kernel, False),
        "side_up", [summed], [side_pad, taps], [place],
        [first_side, first_edge, dw_kernel, inner], 1, 8,
    )
    saved = call(
        up_kernel,
        "up",
        [
            jax.ShapeDtypeStruct((rows, channels), f32),
            jax.ShapeDtypeStruct((rows, LANES), f32),
            jax.ShapeDtypeStruct((rows, hidden), bf16),
            jax.ShapeDtypeStruct((rows, hidden), bf16),
        ],
        [side_pad, taps, pltpu.VMEM(whole, f32), pltpu.VMEM((rows, channels), bf16)]
        + [pltpu.VMEM(w_in.shape, bf16), pltpu.SemaphoreType.DMA],
        [place],
        [second_side, dw_kernel, inner, norm_gain[None], norm_bias[None], w_in, b_in[None]],
        4 * matmul,
        16,
        (5,),
    )
    side, rim = (REACH, tile_v, channels), (REACH, EDGE, channels)
    sent = [side, side, (tile_u, EDGE, channels), rim, rim]
    mismatch, d_conv, even, odd, edge, even_edge, odd_edge = call(
        functools.partial(back_kernel, len(targets)),
        "back",
        [summed] + [jax.ShapeDtypeStruct(shape, bf16) for shape in (whole, *sent)],
        [
            pltpu.VMEM(whole, f32),
            pltpu.SemaphoreType.DMA,
            pltpu.VMEM(whole, bf16),
            pltpu.VMEM((rows, channels), bf16),
            pltpu.VMEM((rows, hidden), bf16),
            pltpu.VMEM((rows, channels), f32),
        ],
        [place, places],
        [middle, *saved, norm_gain[None], w_in, w_out, b_out[None], layer_scale[None], *targets],
        4 * matmul,
        16,
        out_anywhere=(0,),
    )
    even = lax.ppermute(even, "row", row_pairs(False))
    odd = lax.ppermute(odd, "row", row_pairs(True))
    edge = lax.ppermute(edge, "col", SWAP)
    even_edge = lax.ppermute(even_edge, ("row", "col"), across(row_pairs(False)))
    odd_edge = lax.ppermute(odd_edge, ("row", "col"), across(row_pairs(True)))
    (inner,) = call(
        functools.partial(inner_kernel, True),
        "inner_last", [summed],
        [own_pad, taps, pltpu.VMEM(whole, f32), pltpu.SemaphoreType.DMA], [scalar],
        [d_conv, edge, dw_kernel, mismatch], matmul, 8, anywhere=(3,),
    )
    (grad,) = call(
        last_kernel,
        "last",
        [jax.ShapeDtypeStruct((tile_v, tile_u, channels), f32)],
        [rim_pad, taps, pltpu.VMEM(whole, f32), pltpu.VMEM((tile_v, tile_u, channels), f32)]
        + [pltpu.SemaphoreType.DMA((tile_v // (GROUP * SUBLANES),))],
        [place],
        [even, odd, even_edge, odd_edge, dw_kernel, inner],
        1,
        10,
        out_anywhere=(0,),
    )
    return grad


def solution(mesh):
    placed = (
        P(("groups", "row"), "col"),
        P("col", None),
        P(("groups", "col"), "row", None),
        P(),
        P(),
        P(),
        P(),
        P(),
        P(),
        P(),
        P(),
        P(),
    )
    return jax.shard_map(
        on_device,
        mesh=mesh,
        in_specs=placed,
        out_specs=P(("groups", "col"), "row", None),
        check_vma=False,
    )
```
